256 devices in a mesh: wide: 128 (over z, x, y), narrow: 2 (over core).
Axes of the slice: x: 4, y: 4, z: 8, core: 2. Of those that a mesh axis runs over, the one named last changes fastest.
Arguments:
- point_feats: bfloat16 [65536, 512], P(('wide', 'narrow')), may hold values from -24 to 24
- region_ids: int32 [16384], P(('wide', 'narrow')), may hold values from 0 to 63, as said below
- w_qkv: bfloat16 [512, 1536], replicated, may hold values from -0.25 to 0.25
- w_out: bfloat16 [512, 512], replicated, may hold values from -0.25 to 0.25
- w_expert_in: bfloat16 [512, 131072], P(None, 'wide'), may hold values from -0.25 to 0.25
- b_expert_in: float32 [131072], P('wide'), may hold values from -4 to 4
- w_expert_out: bfloat16 [131072, 512], P('wide'), may hold values from -0.125 to 0.125
- out_cotangent: bfloat16 [65536, 512], P(('wide', 'narrow')), may hold values from -18 to 18
Outputs:
- layer_out: bfloat16 [65536, 512], P(('wide', 'narrow'))
- grad_feats: bfloat16 [65536, 512], P(('wide', 'narrow'))
- grad_attention: float32 [512, 2048], P(('wide', 'narrow'))
- grad_expert_in: float32 [512, 131072], P('narrow', 'wide')
- grad_expert_out: float32 [131072, 512], P('wide', 'narrow')
- grad_expert_bias: float32 [131072], P(('wide', 'narrow'))
The draws below stay inside these ranges and needn't reach their ends.
Inputs may be any that keep to these rules, and one draw needn't show every extreme that they name: `region_ids`: the 64 blocks of one device name any one region at most 2 times, and one region is named exactly 2 times by the blocks of every device.
All inputs are finite; a program needn't handle non-finite values.
Results may differ from the reference program's by a relative error of at most 0.0095.
Values may be sent and summed in bfloat16 or wider, within the bound.
No kernel may reach another device: no remote copies, remote signals or barrier semaphores. Data moves between devices by JAX's collectives and lax.ppermute only.
A program may use at most 128 MiB of HBM per device.

```python
import jax
import jax.numpy as jnp
from jax import lax

D = 512
HEADS = 8
HID = 2048
DOMAIN_SPECIALS = 64
P_DEV = 256
BLOCK = 4
DOMAIN_REPEAT_CAP = 2
BPD = 64
POINTS = 65536
BLOCKS = 16384
GROUP = 1024


def shaped_field(key, low_amp, high_amp):
    noise_key, dir_key = jax.random.split(key, 2)
    devices_count = POINTS // P_DEV
    noise = jnp.clip(jax.random.normal(noise_key, (POINTS, D), jnp.float32), -6.0, 6.0)
    directions = jnp.clip(jax.random.normal(dir_key, (devices_count, D), jnp.float32), -4.0, 4.0)
    place = jnp.arange(POINTS, dtype=jnp.float32) / (POINTS - 1)
    amplitude = low_amp + (high_amp - low_amp) * place
    return noise + amplitude[:, None] * jnp.repeat(directions, P_DEV, axis=0)


def draw_point_feats(key, part):
    return shaped_field(jax.random.fold_in(key, 11), 0.6, 3.0).astype(jnp.bfloat16)


def draw_out_cotangent(key, part):
    return shaped_field(jax.random.fold_in(key, 23), 0.5, 1.5).astype(jnp.bfloat16)


def draw_region_ids(key, part):
    devices_count = BLOCKS // BPD
    hot_key, rank_key, rest_key = jax.random.split(jax.random.fold_in(key, 37), 3)
    hot_region = jax.random.randint(hot_key, (), 0, DOMAIN_SPECIALS)
    domain_frequency = jax.random.permutation(rank_key, DOMAIN_SPECIALS - 1)
    eligible_domains = jnp.arange(DOMAIN_REPEAT_CAP * (DOMAIN_SPECIALS - 1), dtype=jnp.int32) // DOMAIN_REPEAT_CAP
    others = eligible_domains + (eligible_domains >= hot_region).astype(jnp.int32)
    rating_increment = (DOMAIN_SPECIALS - 1 - domain_frequency[eligible_domains]) * 64

    def one_device(device_key):
        rating_noise_seed, order_key = jax.random.split(device_key)
        domain_ratings = jax.random.randint(rating_noise_seed, (DOMAIN_REPEAT_CAP * (DOMAIN_SPECIALS - 1),), 0, 4096) + rating_increment
        distinct = domain_ratings * (DOMAIN_REPEAT_CAP * DOMAIN_SPECIALS) + jnp.arange(DOMAIN_REPEAT_CAP * (DOMAIN_SPECIALS - 1), dtype=jnp.int32)
        chosen = lax.top_k(distinct, BPD - DOMAIN_REPEAT_CAP)[1]
        labels = jnp.concatenate([jnp.full((DOMAIN_REPEAT_CAP,), hot_region, jnp.int32), others[chosen]])
        order = jax.random.permutation(order_key, BPD)
        return labels[order]
    device_keys = jax.random.split(rest_key, devices_count)
    return jax.vmap(one_device)(device_keys).reshape(BLOCKS).astype(jnp.int32)


def shard_levels(rng, extent, cuts, low, high):
    level = 1.0
    for position, blocks in cuts:
        steps = jax.random.uniform(jax.random.fold_in(jax.random.fold_in(rng, 6), position), (blocks,), jnp.float32, low / len(cuts), high / len(cuts))
        level = level * jnp.repeat(jnp.exp(steps), extent[position] // blocks).reshape((-1,) + (1,) * (len(extent) - 1 - position))
    return level


def gaussian(key, dims, deviation, most, shards=(), kind=jnp.bfloat16):
    result = deviation * jax.random.normal(key, dims, jnp.float32)
    if shards:
        result = result * shard_levels(key, dims, shards, -0.22, 0.18)
    return jnp.clip(result, -most, most).astype(kind)


def setup_inputs(seed: int = 0) -> dict:
    seeds = jax.random.split(jax.random.key(seed), 9)
    point_feats = draw_point_feats(jax.random.fold_in(seeds[8], 71), 0)
    region_ids = draw_region_ids(jax.random.fold_in(seeds[8], 71), 0)
    w_qkv = gaussian(seeds[2], (D, 3 * D), D ** -0.5, 0.25)
    w_out = gaussian(seeds[3], (D, D), D ** -0.5, 0.25)
    w_expert_in = gaussian(seeds[4], (D, DOMAIN_SPECIALS * HID), D ** -0.5, 0.25, ((1, 128),))
    b_expert_in = gaussian(seeds[5], (DOMAIN_SPECIALS * HID,), 1.0, 4.0, ((0, 128),), jnp.float32)
    w_expert_out = gaussian(seeds[6], (DOMAIN_SPECIALS * HID, D), HID ** -0.5, 0.125, ((0, 128),))
    out_cotangent = draw_out_cotangent(jax.random.fold_in(seeds[8], 71), 0)
    return dict(point_feats=point_feats, region_ids=region_ids, w_qkv=w_qkv, w_out=w_out, w_expert_in=w_expert_in, b_expert_in=b_expert_in, w_expert_out=w_expert_out, out_cotangent=out_cotangent)


gelu_scale = 0.7978845608
gelu_cubic = 0.044715

def gelu_value(values):
    inner = gelu_scale * (values + gelu_cubic * values * values * values)
    return 0.5 * values * (1.0 + jnp.tanh(inner))

def gelu_slope(values):
    tangent = jnp.tanh(gelu_scale * (values + gelu_cubic * values * values * values))
    return 0.5 * (1.0 + tangent) + 0.5 * values * (1.0 - tangent * tangent) * gelu_scale * (1.0 + 3.0 * gelu_cubic * values * values)

def normalize_heads(raw):
    floats = raw.astype(jnp.float32)
    centred = floats - lax.optimization_barrier(jnp.mean(floats, axis=-1, keepdims=True))
    scale_dev = jnp.sqrt(lax.optimization_barrier(jnp.mean(centred * centred, axis=-1, keepdims=True)) + 1e-05)
    normed = centred / scale_dev
    return (normed.astype(jnp.bfloat16), normed, scale_dev)

def normalize_back(grad_normed, normed, scale_dev):
    mean_grad = lax.optimization_barrier(jnp.mean(grad_normed, axis=-1, keepdims=True))
    mean_cross = lax.optimization_barrier(jnp.mean(grad_normed * normed, axis=-1, keepdims=True))
    return (grad_normed - mean_grad - normed * mean_cross) / scale_dev

def round_trip(values):
    return lax.optimization_barrier(values.astype(jnp.bfloat16)).astype(jnp.float32)

def reference(point_feats, region_ids, w_qkv, w_out, w_expert_in, b_expert_in, w_expert_out, out_cotangent):
    head_dim = D // HEADS
    qkv = jnp.dot(point_feats, w_qkv, preferred_element_type=jnp.float32).astype(jnp.bfloat16)
    queries = qkv[:, :D].reshape(POINTS, HEADS, head_dim)
    key_norm, key_unit, key_scale = normalize_heads(qkv[:, D:2 * D].reshape(POINTS, HEADS, head_dim))
    value_norm, value_unit, value_scale = normalize_heads(qkv[:, 2 * D:].reshape(POINTS, HEADS, head_dim))
    summary = jnp.einsum('phi,phj->hij', key_norm.astype(jnp.float32), value_norm.astype(jnp.float32)) / POINTS
    summary_b = summary.astype(jnp.bfloat16)
    mixed = jnp.einsum('phi,hij->phj', queries.astype(jnp.float32), summary_b.astype(jnp.float32)).astype(jnp.bfloat16).reshape(POINTS, D)
    attention = jnp.dot(mixed, w_out, preferred_element_type=jnp.float32)
    grad_mixed = jnp.dot(out_cotangent, w_out.T, preferred_element_type=jnp.float32).astype(jnp.bfloat16)
    grad_heads = grad_mixed.reshape(POINTS, HEADS, head_dim)
    grad_summary = jnp.einsum('phi,phj->hij', queries.astype(jnp.float32), grad_heads.astype(jnp.float32)) / POINTS
    grad_query = jnp.einsum('phj,hij->phi', grad_heads.astype(jnp.float32), summary_b.astype(jnp.float32)).astype(jnp.bfloat16)
    grad_keynorm = jnp.einsum('phj,hij->phi', value_norm.astype(jnp.float32), grad_summary)
    grad_valnorm = jnp.einsum('phi,hij->phj', key_norm.astype(jnp.float32), grad_summary)
    grad_key = normalize_back(grad_keynorm, key_unit, key_scale).astype(jnp.bfloat16)
    grad_value = normalize_back(grad_valnorm, value_unit, value_scale).astype(jnp.bfloat16)
    grad_qkv = jnp.concatenate([grad_query.reshape(POINTS, D), grad_key.reshape(POINTS, D), grad_value.reshape(POINTS, D)], axis=1)
    attention_back = jnp.dot(grad_qkv, w_qkv.T, preferred_element_type=jnp.float32)
    grad_attention = jnp.concatenate([jnp.dot(point_feats.T, grad_qkv, preferred_element_type=jnp.float32), jnp.dot(mixed.T, out_cotangent, preferred_element_type=jnp.float32)], axis=1) / POINTS
    capacity = DOMAIN_REPEAT_CAP * (BLOCKS // BPD)
    feat_blocks = jnp.concatenate([point_feats.reshape(BLOCKS, BLOCK * D), jnp.zeros((1, BLOCK * D), jnp.bfloat16)], axis=0)
    cot_blocks = jnp.concatenate([out_cotangent.reshape(BLOCKS, BLOCK * D), jnp.zeros((1, BLOCK * D), jnp.bfloat16)], axis=0)

    def expert_step(carry, expert):
        out_acc, back_acc = carry
        members = jnp.nonzero(region_ids == expert, size=capacity, fill_value=BLOCKS)[0].astype(jnp.int32)
        rows = feat_blocks[members].reshape(capacity * BLOCK, D)
        cots = cot_blocks[members].reshape(capacity * BLOCK, D)
        live = jnp.repeat(members < BLOCKS, BLOCK)[:, None]
        w_first = lax.dynamic_slice_in_dim(w_expert_in, expert * HID, HID, 1)
        bias = lax.dynamic_slice_in_dim(b_expert_in, expert * HID, HID, 0)
        w_second = lax.dynamic_slice_in_dim(w_expert_out, expert * HID, HID, 0)
        pre_act = jnp.dot(rows, w_first, preferred_element_type=jnp.float32) + bias
        hidden = jnp.where(live, gelu_value(pre_act), 0.0).astype(jnp.bfloat16)
        grad_hidden = jnp.dot(cots, w_second.T, preferred_element_type=jnp.float32)
        grad_pre = jnp.where(live, grad_hidden * gelu_slope(pre_act), 0.0).astype(jnp.bfloat16)
        out_sum = jnp.zeros((capacity * BLOCK, D), jnp.float32)
        back_sum = jnp.zeros((capacity * BLOCK, D), jnp.float32)
        for part_index in range(HID // GROUP):
            lower = part_index * GROUP
            upper = lower + GROUP
            out_sum = out_sum + round_trip(jnp.dot(hidden[:, lower:upper], w_second[lower:upper], preferred_element_type=jnp.float32))
            back_sum = back_sum + round_trip(jnp.dot(grad_pre[:, lower:upper], w_first[:, lower:upper].T, preferred_element_type=jnp.float32))
        out_acc = out_acc.at[members].add(out_sum.reshape(capacity, BLOCK * D))
        back_acc = back_acc.at[members].add(back_sum.reshape(capacity, BLOCK * D))
        grad_second = jnp.dot(hidden.T, cots, preferred_element_type=jnp.float32)
        grad_first = jnp.dot(rows.T, grad_pre, preferred_element_type=jnp.float32)
        grad_bias = lax.optimization_barrier(jnp.sum(grad_pre.astype(jnp.float32), axis=0))
        return ((out_acc, back_acc), (grad_first, grad_second, grad_bias))
    start = (jnp.zeros((BLOCKS + 1, BLOCK * D), jnp.float32), jnp.zeros((BLOCKS + 1, BLOCK * D), jnp.float32))
    (out_acc, back_acc), (firsts, seconds, biases) = lax.scan(expert_step, start, jnp.arange(DOMAIN_SPECIALS, dtype=jnp.int32))
    expert_out = out_acc[:BLOCKS].reshape(POINTS, D)
    expert_back = back_acc[:BLOCKS].reshape(POINTS, D)
    layer_out = (point_feats.astype(jnp.float32) + attention + expert_out).astype(jnp.bfloat16)
    grad_feats = (out_cotangent.astype(jnp.float32) + attention_back + expert_back).astype(jnp.bfloat16)
    share = DOMAIN_SPECIALS / POINTS
    grad_expert_in = jnp.transpose(firsts, (1, 0, 2)).reshape(D, DOMAIN_SPECIALS * HID) * share
    grad_expert_out = seconds.reshape(DOMAIN_SPECIALS * HID, D) * share
    grad_expert_bias = biases.reshape(DOMAIN_SPECIALS * HID) * share
    return (layer_out, grad_feats, grad_attention, grad_expert_in, grad_expert_out, grad_expert_bias)
```

```python
import jax
import jax.numpy as jnp
from jax import lax
from jax.experimental import pallas as pl
from jax.experimental.pallas import tpu as pltpu
from jax.sharding import PartitionSpec as P

F32 = jnp.float32
BF = jnp.bfloat16
EPS = 1e-05
GS = 0.7978845608
GC = 0.044715
W = 512
PTS = 256
NB = 64
CHIPS = 128
TOTAL = 65536.0
SHARE = 64.0 / 65536.0
HALF = 1024
VM = pl.BlockSpec(memory_space=pltpu.VMEM)
SM = pl.BlockSpec(memory_space=pltpu.SMEM)


def mm(a, b):
    return jnp.dot(a, b, preferred_element_type=F32)


def mm_t(a, b):
    return lax.dot_general(a, b, (((1,), (1,)), ((), ())), preferred_element_type=F32)


def t_mm(a, b):
    return lax.dot_general(a, b, (((0,), (0,)), ((), ())), preferred_element_type=F32)


def head_ones():
    r = lax.broadcasted_iota(jnp.int32, (W, W), 0) // 64
    c = lax.broadcasted_iota(jnp.int32, (W, W), 1) // 64
    return jnp.where(r == c, 1.0 / 64.0, 0.0).astype(BF)


def head_mean(v, ones):
    hi = v.astype(BF)
    lo = (v - hi.astype(F32)).astype(BF)
    return mm(hi, ones) + mm(lo, ones)


def normalize(raw, ones):
    cen = raw.astype(F32) - mm(raw, ones)
    scale = jnp.sqrt(head_mean(cen * cen, ones) + EPS)
    return cen / scale, scale


def low_rows(shape):
    return lax.broadcasted_iota(jnp.int32, shape, 0) < 4


def call(body, outs, scratch=(), smem_in=(), n_in=0, smem_out=(), cost=None, name=None):
    return pl.pallas_call(
        body,
        out_shape=outs,
        in_specs=[SM if i in smem_in else VM for i in range(n_in)],
        out_specs=[SM if i in smem_out else VM for i in range(len(outs))],
        scratch_shapes=list(scratch),
        cost_estimate=cost,
        name=name,
        compiler_params=pltpu.CompilerParams(vmem_limit_bytes=56 * 1024 * 1024),
    )


def cost(us):
    return pl.CostEstimate(flops=int(us * 1e9), bytes_accessed=int(us * 1e6), transcendentals=0)


def sds(shape, dtype):
    return jax.ShapeDtypeStruct(shape, dtype)


def front_kernel(ids, x_ref, c_ref, wq_ref, wo_ref, send, slots, qkv_ref, g_ref, cnt, ss):
    @pl.loop(0, NB)
    def _(i):
        cnt[i] = 0

    @pl.loop(0, NB)
    def _(b):
        r = ids[b]
        k = cnt[r]
        cnt[r] = k + 1
        slots[b] = 2 * r + k

    send[:, :, 0:W] = jnp.zeros((CHIPS, 8, W), BF)
    low = low_rows((8, W))

    @pl.loop(0, 16)
    def _(i):
        x = x_ref[pl.ds(pl.multiple_of(i * 16, 16), 16), :].astype(F32)
        c = c_ref[pl.ds(pl.multiple_of(i * 16, 16), 16), :].astype(F32)
        for h in range(2):
            xa, ca = x[8 * h : 8 * h + 8], c[8 * h : 8 * h + 8]
            xr, cr = pltpu.roll(xa, 4, 0), pltpu.roll(ca, 4, 0)
            send[slots[4 * i + 2 * h], :, 0:W] = jnp.where(low, xa, cr).astype(BF)
            send[slots[4 * i + 2 * h + 1], :, 0:W] = jnp.where(low, xr, ca).astype(BF)

    ones = head_ones()
    qkv = mm(x_ref[...], wq_ref[...]).astype(BF)
    qkv_ref[...] = qkv
    g = mm_t(c_ref[...], wo_ref[...]).astype(BF)
    g_ref[...] = g
    kn = normalize(qkv[:, W : 2 * W], ones)[0].astype(BF)
    vn = normalize(qkv[:, 2 * W :], ones)[0].astype(BF)
    left = lax.broadcasted_iota(jnp.int32, (64, 128), 1) < 64
    for j in range(4):
        s = slice(128 * j, 128 * j + 128)
        a = t_mm(kn[:, s], vn[:, s])
        ss[64 * j : 64 * j + 64, :] = jnp.where(left, a[:64], a[64:])
        a = t_mm(qkv[:, s], g[:, s])
        ss[256 + 64 * j : 320 + 64 * j, :] = jnp.where(left, a[:64], a[64:])
    low2 = low_rows((8, 128))

    @pl.loop(0, 64)
    def _(i):
        v = ss[pl.ds(pl.multiple_of(i * 8, 8), 8), :]
        hi = v.astype(BF).astype(F32)
        lo = v - hi
        send[2 * i, :, W:] = jnp.where(low2, hi, pltpu.roll(lo, 4, 0)).astype(BF)
        send[2 * i + 1, :, W:] = jnp.where(low2, pltpu.roll(hi, 4, 0), lo).astype(BF)


def chunk_kernel(recv, out):
    v = jnp.sum(recv[:, :, W:].astype(F32), axis=0)
    out[...] = v + pltpu.roll(v, 4, 0)


def spread_kernel(a_ref, b_ref, out):
    v = ((a_ref[...] + b_ref[...]) * (1.0 / TOTAL)).astype(BF)
    out[...] = jnp.broadcast_to(v[None], (CHIPS, 8, 128))


def expert_kernel(
    n_ref, recv, wi, wiy, win, wo, woy, won, b_ref, bp_ref, send, x_s, c_s, hid, gpre, o_s, k_s
):
    n = n_ref[0]
    mine = pl.ds(pl.multiple_of(n * 256, 256), 256)
    other = pl.ds(pl.multiple_of(256 - n * 256, 256), 256)
    low = low_rows((8, W))

    @pl.loop(0, 32)
    def _(i):
        xs, cs = [], []
        for h in range(2):
            a = recv[4 * i + 2 * h, :, 0:W].astype(F32)
            b = recv[4 * i + 2 * h + 1, :, 0:W].astype(F32)
            xs.append(jnp.where(low, a, pltpu.roll(b, 4, 0)))
            cs.append(jnp.where(low, pltpu.roll(a, 4, 0), b))
        rows = pl.ds(pl.multiple_of(i * 16, 16), 16)
        x_s[rows, :] = jnp.concatenate(xs, axis=0).astype(BF)
        c_s[rows, :] = jnp.concatenate(cs, axis=0).astype(BF)

    def act(pre, gh, cols):
        sq = pre * pre
        t = jnp.tanh(GS * (pre + GC * pre * sq))
        up = 0.5 * (1.0 + t)
        hid[:, cols] = (pre * up).astype(BF)
        slope = up + 0.5 * pre * (1.0 - t * t) * GS * (1.0 + 3.0 * GC * sq)
        gpre[:, cols] = (gh * slope).astype(BF)

    @pl.loop(0, 4)
    def _(i):
        cols = pl.ds(pl.multiple_of(i * 256, 256), 256)
        pre = mm(x_s[...], wi[:, cols]) + b_ref[:, cols]
        gh = mm_t(c_s[...], wo[cols, :])
        act(pre, gh, cols)

    @pl.loop(0, 4)
    def _(i):
        cols = pl.ds(pl.multiple_of(i * 256, 256), 256)
        pre = mm(x_s[:, mine], wiy[:, cols]) + mm(x_s[:, other], win[:, cols]) + bp_ref[:, cols]
        gh = mm_t(c_s[:, mine], woy[cols, :]) + mm_t(c_s[:, other], won[cols, :])
        act(pre, gh, pl.ds(pl.multiple_of(HALF + i * 256, 256), 256))

    for yr, kr, part in ((woy, wiy, mine), (won, win, other)):
        o_s[:, part] = mm(hid[:, :HALF], wo[:, part]) + mm(hid[:, HALF:], yr[...])
        k_s[:, part] = mm_t(gpre[:, :HALF], wi[part, :]) + mm_t(gpre[:, HALF:], kr[...])

    @pl.loop(0, 64)
    def _(i):
        rows = pl.ds(pl.multiple_of(i * 8, 8), 8)
        o, k = o_s[rows, :], k_s[rows, :]
        send[2 * i, :, :] = jnp.where(low, o, pltpu.roll(k, 4, 0)).astype(BF)
        send[2 * i + 1, :, :] = jnp.where(low, pltpu.roll(o, 4, 0), k).astype(BF)


def weight_kernel(n_ref, x_s, c_s, hid, gpre, keep_i, send_i, keep_o, send_o):
    n = n_ref[0]
    mine = pl.ds(pl.multiple_of(n * 256, 256), 256)
    other = pl.ds(pl.multiple_of(256 - n * 256, 256), 256)

    @pl.loop(0, 4)
    def _(i):
        cols = pl.ds(pl.multiple_of(i * 512, 512), 512)
        g = gpre[:, cols]
        keep_i[0:256, cols] = t_mm(x_s[:, mine], g) * SHARE
        send_i[0:256, cols] = (t_mm(x_s[:, other], g) * SHARE).astype(BF)
        bias = jnp.sum(g.astype(F32), axis=0, keepdims=True) * SHARE
        keep_i[256:272, cols] = jnp.broadcast_to(bias, (16, 512))
        send_i[256:272, cols] = jnp.broadcast_to(bias, (16, 512)).astype(BF)
        h = hid[:, cols]
        keep_o[cols, :] = t_mm(h, c_s[:, mine]) * SHARE
        send_o[cols, :] = (t_mm(h, c_s[:, other]) * SHARE).astype(BF)


def attn_kernel(
    n_ref, rs, qkv_ref, g_ref, x_ref, c_ref, wq_ref, wo_ref, base_o, base_k, keep, send, ss, gq
):
    n = n_ref[0]
    low = low_rows((8, 128))

    @pl.loop(0, 32)
    def _(i):
        t = [
            jnp.where(low, rs[4 * i + 2 * h].astype(F32), rs[4 * i + 2 * h + 1].astype(F32))
            for h in range(2)
        ]
        ss[pl.ds(pl.multiple_of(i * 16, 16), 16), :] = jnp.concatenate(t, axis=0).astype(BF)

    ones = head_ones()
    qkv, g = qkv_ref[...], g_ref[...]
    ku, ks = normalize(qkv[:, W : 2 * W], ones)
    vu, vs = normalize(qkv[:, 2 * W :], ones)
    kn, vn = ku.astype(BF), vu.astype(BF)
    left = lax.broadcasted_iota(jnp.int32, (64, 128), 1) < 64

    def diag(p):
        z = jnp.zeros_like(p)
        return jnp.concatenate([jnp.where(left, p, z), jnp.where(left, z, p)], axis=0)

    mixed, gk, gv = [], [], []
    for j in range(4):
        s = slice(128 * j, 128 * j + 128)
        sm = diag(ss[64 * j : 64 * j + 64, :].astype(F32)).astype(BF)
        gs = diag(ss[256 + 64 * j : 320 + 64 * j, :].astype(F32)).astype(BF)
        mixed.append(mm(qkv[:, s], sm).astype(BF))
        gq[:, s] = mm_t(g[:, s], sm).astype(BF)
        gk.append(mm_t(vn[:, s], gs))
        gv.append(mm(kn[:, s], gs))
    mixed = jnp.concatenate(mixed, axis=1)

    def back(gr, u, sc):
        return ((gr - head_mean(gr, ones) - u * head_mean(gr * u, ones)) / sc).astype(BF)

    gq[:, W : 2 * W] = back(jnp.concatenate(gk, axis=1), ku, ks)
    gq[:, 2 * W :] = back(jnp.concatenate(gv, axis=1), vu, vs)
    x, c = x_ref[...], c_ref[...]
    base_o[...] = x.astype(F32) + mm(mixed, wo_ref[...])
    base_k[...] = c.astype(F32) + mm_t(gq[...], wq_ref[...])

    def pick(core):
        r = lax.broadcasted_iota(jnp.int32, (W, PTS), 0)
        k = lax.broadcasted_iota(jnp.int32, (W, PTS), 1)
        return jnp.where(r == 4 * (k // 2) + 2 * core + k % 2, 1.0, 0.0).astype(BF)

    for core, dst in ((n, keep), (1 - n, send)):
        sel = pick(core)
        xk, mk = mm(x, sel).astype(BF), mm(mixed, sel).astype(BF)
        for q in range(3):
            cols = slice(W * q, W * q + W)
            dst[:, cols] = (t_mm(xk, gq[:, cols]) * (1.0 / TOTAL)).astype(dst.dtype)
        dst[:, 3 * W :] = (t_mm(mk, c) * (1.0 / TOTAL)).astype(dst.dtype)


def deal_kernel(keep, recv, out):
    r = lax.broadcasted_iota(jnp.int32, (2 * W, PTS), 0)
    k = lax.broadcasted_iota(jnp.int32, (2 * W, PTS), 1)
    acc = None
    for q in range(4):
        cols = slice(W * q, W * q + W)
        v = (keep[:, cols] + recv[:, cols].astype(F32)).astype(BF)
        part = mm(jnp.where(r == 4 * k + q, 1.0, 0.0).astype(BF), v)
        acc = part if acc is None else acc + part
    out[...] = acc.astype(BF)


def total_kernel(recv, out):
    out[...] = jnp.sum(recv[...].astype(F32), axis=0)


def final_kernel(slots, ret, base_o, base_k, lo, gf):
    low = low_rows((8, W))

    @pl.loop(0, 16)
    def _(i):
        os, ks = [], []
        for h in range(2):
            a = ret[slots[4 * i + 2 * h]].astype(F32)
            b = ret[slots[4 * i + 2 * h + 1]].astype(F32)
            os.append(jnp.where(low, a, pltpu.roll(b, 4, 0)))
            ks.append(jnp.where(low, pltpu.roll(a, 4, 0), b))
        rows = pl.ds(pl.multiple_of(i * 16, 16), 16)
        lo[rows, :] = (base_o[rows, :] + jnp.concatenate(os, axis=0)).astype(BF)
        gf[rows, :] = (base_k[rows, :] + jnp.concatenate(ks, axis=0)).astype(BF)


def on_device(x, ids, wq, wo_att, wi, bi, wo, c):
    n = lax.axis_index("narrow")
    nv = n.reshape(1).astype(jnp.int32)
    pair = [(i, i ^ 1) for i in range(CHIPS)]
    swap = [(0, 1), (1, 0)]

    def across(v):
        return lax.ppermute(v, "wide", pair)

    def beside(v):
        return lax.ppermute(v, "narrow", swap)

    def deal(v):
        return lax.all_to_all(v, "wide", split_axis=0, concat_axis=0, tiled=True)

    wiy = across(lax.dynamic_slice_in_dim(wi, n * 256, 256, 0))
    woy = across(lax.dynamic_slice_in_dim(wo, n * 256, 256, 1))
    bp = across(bi)
    win, won = beside(wiy), beside(woy)

    send, slots, qkv, g = call(
        front_kernel,
        [sds((CHIPS, 8, 640), BF), sds((NB,), jnp.int32), sds((PTS, 3 * W), BF), sds((PTS, W), BF)],
        [pltpu.SMEM((NB,), jnp.int32), pltpu.VMEM((W, 128), F32)],
        smem_in=(0,), n_in=5, smem_out=(1,), cost=cost(5), name="front",
    )(ids, x, c, wq, wo_att)
    recv = deal(send)
    (chunk,) = call(chunk_kernel, [sds((8, 128), F32)], n_in=1, cost=cost(1), name="chunk")(recv)
    (spread,) = call(spread_kernel, [sds((CHIPS, 8, 128), BF)], n_in=2, cost=cost(1), name="spread")(
        chunk, beside(chunk)
    )
    rs = deal(spread)
    ret, x_s, c_s, hid, gpre = call(
        expert_kernel,
        [sds((CHIPS, 8, W), BF), sds((W, W), BF), sds((W, W), BF), sds((W, 2 * HALF), BF), sds((W, 2 * HALF), BF)],
        [pltpu.VMEM((W, W), F32), pltpu.VMEM((W, W), F32)],
        smem_in=(0,), n_in=10, cost=cost(12), name="expert",
    )(nv, recv, wi, wiy, win, wo, woy, won, bi.reshape(1, HALF), bp.reshape(1, HALF))
    back = deal(ret)
    base_o, base_k, keep, away = call(
        attn_kernel,
        [sds((PTS, W), F32), sds((PTS, W), F32), sds((PTS, 4 * W), F32), sds((PTS, 4 * W), BF)],
        [pltpu.VMEM((W, 128), BF), pltpu.VMEM((PTS, 3 * W), BF)],
        smem_in=(0,), n_in=8, cost=cost(7), name="attn",
    )(nv, rs, qkv, g, x, c, wq, wo_att)
    (att_send,) = call(deal_kernel, [sds((2 * W, W), BF)], n_in=2, cost=cost(2), name="deal")(
        keep, beside(away)
    )
    att_recv = deal(att_send.reshape(CHIPS, 8, W))
    keep_i, send_i, keep_o, send_o = call(
        weight_kernel,
        [sds((272, 2 * HALF), F32), sds((272, 2 * HALF), BF), sds((2 * HALF, 256), F32), sds((2 * HALF, 256), BF)],
        smem_in=(0,), n_in=5, cost=cost(7), name="weight",
    )(nv, x_s, c_s, hid, gpre)
    sum_i = keep_i + beside(send_i).astype(F32)
    sum_o = keep_o + beside(send_o).astype(F32)
    tot_i = sum_i[:, :HALF] + across(sum_i[:, HALF:].astype(BF)).astype(F32)
    tot_o = sum_o[:HALF] + across(sum_o[HALF:].astype(BF)).astype(F32)
    grad_in = tot_i[:256]
    grad_b = lax.dynamic_slice_in_dim(tot_i[256], n * 512, 512, 0)
    layer_out, grad_feats = call(
        final_kernel, [sds((PTS, W), BF), sds((PTS, W), BF)], smem_in=(0,), n_in=4, cost=cost(2), name="final"
    )(slots, back, base_o, base_k)
    (att,) = call(total_kernel, [sds((8, W), F32)], n_in=1, cost=cost(1), name="total")(att_recv)
    return (layer_out, grad_feats, att.reshape(2, 4 * W), grad_in, tot_o, grad_b)


def solution(mesh):
    placed = (
        P(("wide", "narrow"), None),
        P(("wide", "narrow")),
        P(),
        P(),
        P(None, "wide"),
        P("wide"),
        P("wide", None),
        P(("wide", "narrow"), None),
    )
    return jax.shard_map(
        on_device,
        mesh=mesh,
        in_specs=placed,
        out_specs=(
            P(("wide", "narrow"), None),
            P(("wide", "narrow"), None),
            P(("wide", "narrow"), None),
            P("narrow", "wide"),
            P("wide", "narrow"),
            P(("wide", "narrow")),
        ),
        check_vma=False,
    )
```

```python
import jax
import jax.numpy as jnp
from jax import lax
from jax.experimental import pallas as pl
from jax.experimental.pallas import tpu as pltpu
from jax.sharding import PartitionSpec as P

F32 = jnp.float32
BF = jnp.bfloat16
EPS = 1e-05
GS = 0.7978845608
GC = 0.044715
W = 512
PTS = 256
NB = 64
CHIPS = 128
TOTAL = 65536.0
SHARE = 64.0 / 65536.0
HALF = 1024
VM = pl.BlockSpec(memory_space=pltpu.VMEM)
SM = pl.BlockSpec(memory_space=pltpu.SMEM)


def mm(a, b):
    return jnp.dot(a, b, preferred_element_type=F32)


def mm_t(a, b):
    return lax.dot_general(a, b, (((1,), (1,)), ((), ())), preferred_element_type=F32)


def t_mm(a, b):
    return lax.dot_general(a, b, (((0,), (0,)), ((), ())), preferred_element_type=F32)


def head_ones():
    r = lax.broadcasted_iota(jnp.int32, (W, W), 0) // 64
    c = lax.broadcasted_iota(jnp.int32, (W, W), 1) // 64
    return jnp.where(r == c, 1.0 / 64.0, 0.0).astype(BF)


def head_mean(v, ones):
    hi = v.astype(BF)
    lo = (v - hi.astype(F32)).astype(BF)
    return mm(hi, ones) + mm(lo, ones)


def normalize(raw, ones):
    cen = raw.astype(F32) - mm(raw, ones)
    scale = jnp.sqrt(head_mean(cen * cen, ones) + EPS)
    return cen / scale, scale


def low_rows(shape):
    return lax.broadcasted_iota(jnp.int32, shape, 0) < 4


def call(body, outs, scratch=(), smem_in=(), n_in=0, smem_out=(), cost=None):
    return pl.pallas_call(
        body,
        out_shape=outs,
        in_specs=[SM if i in smem_in else VM for i in range(n_in)],
        out_specs=[SM if i in smem_out else VM for i in range(len(outs))],
        scratch_shapes=list(scratch),
        cost_estimate=cost,
        compiler_params=pltpu.CompilerParams(vmem_limit_bytes=56 * 1024 * 1024),
    )


def cost(us):
    return pl.CostEstimate(flops=int(us * 1e9), bytes_accessed=int(us * 1e6), transcendentals=0)


def sds(shape, dtype):
    return jax.ShapeDtypeStruct(shape, dtype)


def front_kernel(ids, x_ref, c_ref, wq_ref, wo_ref, send, slots, qkv_ref, g_ref, ss, cnt):
    @pl.loop(0, NB)
    def _(i):
        cnt[i] = 0

    @pl.loop(0, NB)
    def _(b):
        r = ids[b]
        k = cnt[r]
        cnt[r] = k + 1
        slots[b] = 2 * r + k

    send[...] = jnp.zeros((CHIPS, 8, W), BF)
    low = low_rows((8, W))

    @pl.loop(0, 16)
    def _(i):
        x = x_ref[pl.ds(pl.multiple_of(i * 16, 16), 16), :].astype(F32)
        c = c_ref[pl.ds(pl.multiple_of(i * 16, 16), 16), :].astype(F32)
        for h in range(2):
            xa, ca = x[8 * h : 8 * h + 8], c[8 * h : 8 * h + 8]
            xr, cr = pltpu.roll(xa, 4, 0), pltpu.roll(ca, 4, 0)
            send[slots[4 * i + 2 * h]] = jnp.where(low, xa, cr).astype(BF)
            send[slots[4 * i + 2 * h + 1]] = jnp.where(low, xr, ca).astype(BF)

    ones = head_ones()
    qkv = mm(x_ref[...], wq_ref[...]).astype(BF)
    qkv_ref[...] = qkv
    g = mm_t(c_ref[...], wo_ref[...]).astype(BF)
    g_ref[...] = g
    kn = normalize(qkv[:, W : 2 * W], ones)[0].astype(BF)
    vn = normalize(qkv[:, 2 * W :], ones)[0].astype(BF)
    left = lax.broadcasted_iota(jnp.int32, (64, 128), 1) < 64
    for j in range(4):
        s = slice(128 * j, 128 * j + 128)
        a = t_mm(kn[:, s], vn[:, s])
        ss[64 * j : 64 * j + 64, :] = jnp.where(left, a[:64], a[64:])
        a = t_mm(qkv[:, s], g[:, s])
        ss[256 + 64 * j : 320 + 64 * j, :] = jnp.where(left, a[:64], a[64:])


def axis_rows(me, shift, ways, size):
    return pl.ds(pl.multiple_of(lax.rem(me + shift, ways) * size, size), size)


def sum_a(pos, own, other, keep, s1, s2, s3, tot):
    tot[...] = own[...] + other[...]
    keep[...] = tot[axis_rows(pos[1], 0, 4, 128), :]
    for k, dst in enumerate((s1, s2, s3)):
        dst[...] = tot[axis_rows(pos[1], k + 1, 4, 128), :].astype(BF)


def sum_b(pos, own, r1, r2, r3, keep, s1, s2, s3, tot):
    tot[...] = own[...] + r1[...].astype(F32) + r2[...].astype(F32) + r3[...].astype(F32)
    keep[...] = tot[axis_rows(pos[2], 0, 4, 32), :]
    for k, dst in enumerate((s1, s2, s3)):
        dst[...] = tot[axis_rows(pos[2], k + 1, 4, 32), :].astype(BF)


def sum_c(own, r1, r2, r3, out):
    v = own[...] + r1[...].astype(F32) + r2[...].astype(F32) + r3[...].astype(F32)
    out[...] = v.astype(BF)


def sum_d(own, r1, r2, r3, r4, r5, r6, r7, out):
    v = own[...].astype(F32)
    for r in (r1, r2, r3, r4, r5, r6, r7):
        v = v + r[...].astype(F32)
    out[...] = (v * (1.0 / TOTAL)).astype(BF)


def sum_e(pos, own, r1, r2, r3, out):
    for k, src in enumerate((own, r1, r2, r3)):
        out[axis_rows(pos[2], (4 - k) % 4, 4, 32), :] = src[...]


def expert_kernel(
    pos, recv, wi, wiy, win, wo, woy, won, b_ref, bp_ref, send, x_s, c_s, hid, gpre, o_s, k_s
):
    n = pos[3]
    mine = pl.ds(pl.multiple_of(n * 256, 256), 256)
    other = pl.ds(pl.multiple_of(256 - n * 256, 256), 256)
    low = low_rows((8, W))

    @pl.loop(0, 32)
    def _(i):
        xs, cs = [], []
        for h in range(2):
            a = recv[4 * i + 2 * h].astype(F32)
            b = recv[4 * i + 2 * h + 1].astype(F32)
            xs.append(jnp.where(low, a, pltpu.roll(b, 4, 0)))
            cs.append(jnp.where(low, pltpu.roll(a, 4, 0), b))
        rows = pl.ds(pl.multiple_of(i * 16, 16), 16)
        x_s[rows, :] = jnp.concatenate(xs, axis=0).astype(BF)
        c_s[rows, :] = jnp.concatenate(cs, axis=0).astype(BF)

    def act(pre, gh, cols):
        sq = pre * pre
        t = jnp.tanh(GS * (pre + GC * pre * sq))
        up = 0.5 * (1.0 + t)
        hid[:, cols] = (pre * up).astype(BF)
        slope = up + 0.5 * pre * (1.0 - t * t) * GS * (1.0 + 3.0 * GC * sq)
        gpre[:, cols] = (gh * slope).astype(BF)

    @pl.loop(0, 4)
    def _(i):
        cols = pl.ds(pl.multiple_of(i * 256, 256), 256)
        pre = mm(x_s[...], wi[:, cols]) + b_ref[:, cols]
        gh = mm_t(c_s[...], wo[cols, :])
        act(pre, gh, cols)

    @pl.loop(0, 4)
    def _(i):
        cols = pl.ds(pl.multiple_of(i * 256, 256), 256)
        pre = mm(x_s[:, mine], wiy[:, cols]) + mm(x_s[:, other], win[:, cols]) + bp_ref[:, cols]
        gh = mm_t(c_s[:, mine], woy[cols, :]) + mm_t(c_s[:, other], won[cols, :])
        act(pre, gh, pl.ds(pl.multiple_of(HALF + i * 256, 256), 256))

    for yr, kr, part in ((woy, wiy, mine), (won, win, other)):
        o_s[:, part] = mm(hid[:, :HALF], wo[:, part]) + mm(hid[:, HALF:], yr[...])
        k_s[:, part] = mm_t(gpre[:, :HALF], wi[part, :]) + mm_t(gpre[:, HALF:], kr[...])

    @pl.loop(0, 64)
    def _(i):
        rows = pl.ds(pl.multiple_of(i * 8, 8), 8)
        o, k = o_s[rows, :], k_s[rows, :]
        send[2 * i, :, :] = jnp.where(low, o, pltpu.roll(k, 4, 0)).astype(BF)
        send[2 * i + 1, :, :] = jnp.where(low, pltpu.roll(o, 4, 0), k).astype(BF)


def weight_in_kernel(pos, x_s, gpre, keep, send):
    n = pos[3]
    mine = pl.ds(pl.multiple_of(n * 256, 256), 256)
    other = pl.ds(pl.multiple_of(256 - n * 256, 256), 256)

    @pl.loop(0, 4)
    def _(i):
        cols = pl.ds(pl.multiple_of(i * 512, 512), 512)
        g = gpre[:, cols]
        keep[0:256, cols] = t_mm(x_s[:, mine], g) * SHARE
        send[0:256, cols] = (t_mm(x_s[:, other], g) * SHARE).astype(BF)
        bias = jnp.sum(g.astype(F32), axis=0, keepdims=True) * SHARE
        keep[256:272, cols] = jnp.broadcast_to(bias, (16, 512))
        send[256:272, cols] = jnp.broadcast_to(bias, (16, 512)).astype(BF)


def weight_out_kernel(pos, c_s, hid, keep, send):
    n = pos[3]
    mine = pl.ds(pl.multiple_of(n * 256, 256), 256)
    other = pl.ds(pl.multiple_of(256 - n * 256, 256), 256)

    @pl.loop(0, 4)
    def _(i):
        cols = pl.ds(pl.multiple_of(i * 512, 512), 512)
        h = hid[:, cols]
        keep[cols, :] = t_mm(h, c_s[:, mine]) * SHARE
        send[cols, :] = (t_mm(h, c_s[:, other]) * SHARE).astype(BF)


def merge_in_kernel(keep, recv, here, away):
    here[...] = keep[:, :HALF] + recv[:, :HALF].astype(F32)
    away[...] = (keep[:, HALF:] + recv[:, HALF:].astype(F32)).astype(BF)


def merge_out_kernel(keep, recv, here, away):
    here[...] = keep[:HALF, :] + recv[:HALF, :].astype(F32)
    away[...] = (keep[HALF:, :] + recv[HALF:, :].astype(F32)).astype(BF)


def end_in_kernel(pos, here, recv, out, bias, row):
    out[...] = here[:256, :] + recv[:256, :].astype(F32)
    row[...] = (here[256:272, :] + recv[256:272, :].astype(F32))[0:8, :]
    bias[...] = row[0:1, pl.ds(pl.multiple_of(pos[3] * 512, 512), 512)]


def end_out_kernel(here, recv, out):
    out[...] = here[...] + recv[...].astype(F32)


def attn_kernel(
    pos, s0, s1, s2, s3, qkv_ref, g_ref, x_ref, c_ref, wq_ref, wo_ref, base_o, base_k, keep, send, ss, gq
):
    n = pos[3]
    for k, src in enumerate((s0, s1, s2, s3)):
        ss[axis_rows(pos[1], (4 - k) % 4, 4, 128), :] = src[...]
    ones = head_ones()
    qkv, g = qkv_ref[...], g_ref[...]
    ku, ks = normalize(qkv[:, W : 2 * W], ones)
    vu, vs = normalize(qkv[:, 2 * W :], ones)
    kn, vn = ku.astype(BF), vu.astype(BF)
    left = lax.broadcasted_iota(jnp.int32, (64, 128), 1) < 64

    def diag(p):
        z = jnp.zeros_like(p)
        return jnp.concatenate([jnp.where(left, p, z), jnp.where(left, z, p)], axis=0)

    mixed, gk, gv = [], [], []
    for j in range(4):
        s = slice(128 * j, 128 * j + 128)
        sm = diag(ss[64 * j : 64 * j + 64, :].astype(F32)).astype(BF)
        gs = diag(ss[256 + 64 * j : 320 + 64 * j, :].astype(F32)).astype(BF)
        mixed.append(mm(qkv[:, s], sm).astype(BF))
        gq[:, s] = mm_t(g[:, s], sm).astype(BF)
        gk.append(mm_t(vn[:, s], gs))
        gv.append(mm(kn[:, s], gs))
    mixed = jnp.concatenate(mixed, axis=1)

    def back(gr, u, sc):
        return ((gr - head_mean(gr, ones) - u * head_mean(gr * u, ones)) / sc).astype(BF)

    gq[:, W : 2 * W] = back(jnp.concatenate(gk, axis=1), ku, ks)
    gq[:, 2 * W :] = back(jnp.concatenate(gv, axis=1), vu, vs)
    x, c = x_ref[...], c_ref[...]
    base_o[...] = x.astype(F32) + mm(mixed, wo_ref[...])
    base_k[...] = c.astype(F32) + mm_t(gq[...], wq_ref[...])

    def pick(core):
        r = lax.broadcasted_iota(jnp.int32, (W, PTS), 0)
        k = lax.broadcasted_iota(jnp.int32, (W, PTS), 1)
        chip = (k // 2 % 8) * 16 + (k // 64) * 4 + k // 16 % 4
        return jnp.where(r == 4 * chip + 2 * core + k % 2, 1.0, 0.0).astype(BF)

    for core, dst in ((n, keep), (1 - n, send)):
        sel = pick(core)
        xk, mk = mm(x, sel).astype(BF), mm(mixed, sel).astype(BF)
        for q in range(3):
            cols = slice(W * q, W * q + W)
            dst[:, cols] = (t_mm(xk, gq[:, cols]) * (1.0 / TOTAL)).astype(dst.dtype)
        dst[:, 3 * W :] = (t_mm(mk, c) * (1.0 / TOTAL)).astype(dst.dtype)


def att_a(pos, own, near, keep, s1, s2, s3, tot):
    tot[...] = own[...] + near[...].astype(F32)
    keep[...] = tot[axis_rows(pos[1], 0, 4, 64), :]
    for k, dst in enumerate((s1, s2, s3)):
        dst[...] = tot[axis_rows(pos[1], k + 1, 4, 64), :].astype(BF)


def att_b(pos, own, r1, r2, r3, keep, s1, s2, s3, tot):
    tot[...] = own[...] + r1[...].astype(F32) + r2[...].astype(F32) + r3[...].astype(F32)
    keep[...] = tot[axis_rows(pos[2], 0, 4, 16), :]
    for k, dst in enumerate((s1, s2, s3)):
        dst[...] = tot[axis_rows(pos[2], k + 1, 4, 16), :].astype(BF)


def att_c(pos, own, r1, r2, r3, keep, s1, s2, s3, s4, s5, s6, s7, tot, deal):
    tot[...] = own[...] + r1[...].astype(F32) + r2[...].astype(F32) + r3[...].astype(F32)
    for r in range(16):
        for q in range(4):
            k = (r // 2) * 8 + (r % 2) * 4 + q
            deal[k : k + 1, :] = tot[r : r + 1, W * q : W * q + W]
    keep[...] = deal[axis_rows(pos[0], 0, 8, 8), :]
    for k, dst in enumerate((s1, s2, s3, s4, s5, s6, s7)):
        dst[...] = deal[axis_rows(pos[0], k + 1, 8, 8), :].astype(BF)


def att_d(own, r1, r2, r3, r4, r5, r6, r7, out):
    v = own[...]
    for r in (r1, r2, r3, r4, r5, r6, r7):
        v = v + r[...].astype(F32)
    out[...] = v


def final_kernel(slots, ret, base_o, base_k, lo, gf):
    low = low_rows((8, W))

    @pl.loop(0, 16)
    def _(i):
        os, ks = [], []
        for h in range(2):
            a = ret[slots[4 * i + 2 * h]].astype(F32)
            b = ret[slots[4 * i + 2 * h + 1]].astype(F32)
            os.append(jnp.where(low, a, pltpu.roll(b, 4, 0)))
            ks.append(jnp.where(low, pltpu.roll(a, 4, 0), b))
        rows = pl.ds(pl.multiple_of(i * 16, 16), 16)
        lo[rows, :] = (base_o[rows, :] + jnp.concatenate(os, axis=0)).astype(BF)
        gf[rows, :] = (base_k[rows, :] + jnp.concatenate(ks, axis=0)).astype(BF)


def layer(x, ids, wq, wo_att, wi, bi, wo, c):
    n = lax.axis_index("narrow")
    w = lax.axis_index("wide")
    pos = jnp.stack([w // 16, w // 4 % 4, w % 4, n]).astype(jnp.int32)
    pair = [(i, i ^ 1) for i in range(CHIPS)]
    swap = [(0, 1), (1, 0)]
    stride = {"x": (4, 4), "y": (1, 4), "z": (16, 8)}

    def across(v):
        return lax.ppermute(v, "wide", pair)

    def beside(v):
        return lax.ppermute(v, "narrow", swap)

    def shift(v, axis, k):
        step, ways = stride[axis]
        moves = []
        for i in range(CHIPS):
            at = i // step % ways
            moves.append((i, i + ((at + k) % ways - at) * step))
        return lax.ppermute(v, "wide", moves)

    def shifts(vs, axis):
        return [shift(v, axis, k + 1) for k, v in enumerate(vs)]

    def deal(v):
        return lax.all_to_all(v, "wide", split_axis=0, concat_axis=0, tiled=True)

    def run(body, us, outs, args, scratch=(), smem_in=(), smem_out=()):
        return call(body, outs, scratch, smem_in=smem_in, n_in=len(args), smem_out=smem_out, cost=cost(us))(*args)

    wiy = across(lax.dynamic_slice_in_dim(wi, n * 256, 256, 0))
    woy = across(lax.dynamic_slice_in_dim(wo, n * 256, 256, 1))
    bp = across(bi)
    win, won = beside(wiy), beside(woy)

    send, slots, qkv, g, ss = run(
        front_kernel, 5,
        [sds((CHIPS, 8, W), BF), sds((NB,), jnp.int32), sds((PTS, 3 * W), BF), sds((PTS, W), BF), sds((W, 128), F32)],
        (ids, x, c, wq, wo_att), [pltpu.SMEM((NB,), jnp.int32)], (0,), (1,),
    )
    recv = deal(send)

    keep, *out = run(
        sum_a, 1, [sds((128, 128), F32)] + [sds((128, 128), BF)] * 3,
        (pos, ss, beside(ss)), [pltpu.VMEM((W, 128), F32)], (0,),
    )
    keep, *out = run(
        sum_b, 1, [sds((32, 128), F32)] + [sds((32, 128), BF)] * 3,
        (pos, keep, *shifts(out, "x")), [pltpu.VMEM((128, 128), F32)], (0,),
    )
    (part,) = run(sum_c, 1, [sds((32, 128), BF)], (keep, *shifts(out, "y")))
    (part,) = run(sum_d, 1, [sds((32, 128), BF)], (part, *shifts([part] * 7, "z")))
    (part,) = run(sum_e, 1, [sds((128, 128), BF)], (pos, part, *shifts([part] * 3, "y")), smem_in=(0,))
    parts = [part, *shifts([part] * 3, "x")]

    ret, x_s, c_s, hid, gpre = run(
        expert_kernel, 12,
        [sds((CHIPS, 8, W), BF), sds((W, W), BF), sds((W, W), BF), sds((W, 2 * HALF), BF), sds((W, 2 * HALF), BF)],
        (pos, recv, wi, wiy, win, wo, woy, won, bi.reshape(1, HALF), bp.reshape(1, HALF)),
        [pltpu.VMEM((W, W), F32), pltpu.VMEM((W, W), F32)], (0,),
    )
    back = deal(ret)
    base_o, base_k, keep, away = run(
        attn_kernel, 7,
        [sds((PTS, W), F32), sds((PTS, W), F32), sds((PTS, 4 * W), F32), sds((PTS, 4 * W), BF)],
        (pos, *parts, qkv, g, x, c, wq, wo_att),
        [pltpu.VMEM((W, 128), BF), pltpu.VMEM((PTS, 3 * W), BF)], (0,),
    )
    near = beside(away)
    keep_i, send_i = run(
        weight_in_kernel, 4, [sds((272, 2 * HALF), F32), sds((272, 2 * HALF), BF)], (pos, x_s, gpre), (), (0,)
    )
    got_i = beside(send_i)
    keep, *out = run(
        att_a, 2, [sds((64, 4 * W), F32)] + [sds((64, 4 * W), BF)] * 3,
        (pos, keep, near), [pltpu.VMEM((PTS, 4 * W), F32)], (0,),
    )
    got_x = shifts(out, "x")
    keep_o, send_o = run(
        weight_out_kernel, 4, [sds((2 * HALF, 256), F32), sds((2 * HALF, 256), BF)], (pos, c_s, hid), (), (0,)
    )
    got_o = beside(send_o)
    here_i, away_i = run(merge_in_kernel, 1, [sds((272, HALF), F32), sds((272, HALF), BF)], (keep_i, got_i))
    far_i = across(away_i)
    here_o, away_o = run(merge_out_kernel, 1, [sds((HALF, 256), F32), sds((HALF, 256), BF)], (keep_o, got_o))
    far_o = across(away_o)
    keep, *out = run(
        att_b, 1, [sds((16, 4 * W), F32)] + [sds((16, 4 * W), BF)] * 3,
        (pos, keep, *got_x), [pltpu.VMEM((64, 4 * W), F32)], (0,),
    )
    keep, *out = run(
        att_c, 1, [sds((8, W), F32)] + [sds((8, W), BF)] * 7,
        (pos, keep, *shifts(out, "y")), [pltpu.VMEM((16, 4 * W), F32), pltpu.VMEM((64, W), F32)], (0,),
    )
    got_z = shifts(out, "z")
    layer_out, grad_feats = run(
        final_kernel, 2, [sds((PTS, W), BF), sds((PTS, W), BF)], (slots, back, base_o, base_k), (), (0,)
    )
    (att,) = run(att_d, 1, [sds((8, W), F32)], (keep, *got_z))
    grad_in, grad_b = run(
        end_in_kernel, 1, [sds((256, HALF), F32), sds((1, 512), F32)],
        (pos, here_i, far_i), [pltpu.VMEM((8, HALF), F32)], (0,),
    )
    (grad_out,) = run(end_out_kernel, 1, [sds((HALF, 256), F32)], (here_o, far_o))
    return (layer_out, grad_feats, att.reshape(2, 4 * W), grad_in, grad_out, grad_b.reshape(512))


def solution(mesh):
    placed = (
        P(("wide", "narrow"), None),
        P(("wide", "narrow")),
        P(),
        P(),
        P(None, "wide"),
        P("wide"),
        P("wide", None),
        P(("wide", "narrow"), None),
    )
    return jax.shard_map(
        layer,
        mesh=mesh,
        in_specs=placed,
        out_specs=(
            P(("wide", "narrow"), None),
            P(("wide", "narrow"), None),
            P(("wide", "narrow"), None),
            P("narrow", "wide"),
            P("wide", "narrow"),
            P(("wide", "narrow")),
        ),
        check_vma=False,
    )
```

```python
import jax
import jax.numpy as jnp
from jax import lax
from jax.experimental import pallas as pl
from jax.experimental.pallas import tpu as pltpu
from jax.sharding import PartitionSpec as P

F32 = jnp.float32
BF = jnp.bfloat16
EPS = 1e-05
GS = 0.7978845608
GC = 0.044715
W = 512
PTS = 256
NB = 64
CHIPS = 128
TOTAL = 65536.0
SHARE = 64.0 / 65536.0
HALF = 1024
VM = pl.BlockSpec(memory_space=pltpu.VMEM)
SM = pl.BlockSpec(memory_space=pltpu.SMEM)


def mm(a, b):
    return jnp.dot(a, b, preferred_element_type=F32)


def mm_t(a, b):
    return lax.dot_general(a, b, (((1,), (1,)), ((), ())), preferred_element_type=F32)


def t_mm(a, b):
    return lax.dot_general(a, b, (((0,), (0,)), ((), ())), preferred_element_type=F32)


def head_ones():
    r = lax.broadcasted_iota(jnp.int32, (W, W), 0) // 64
    c = lax.broadcasted_iota(jnp.int32, (W, W), 1) // 64
    return jnp.where(r == c, 1.0 / 64.0, 0.0).astype(BF)


def head_mean(v, ones):
    hi = v.astype(BF)
    lo = (v - hi.astype(F32)).astype(BF)
    return mm(hi, ones) + mm(lo, ones)


def normalize(raw, ones):
    cen = raw.astype(F32) - mm(raw, ones)
    scale = jnp.sqrt(head_mean(cen * cen, ones) + EPS)
    return cen / scale, scale


def low_rows(shape):
    return lax.broadcasted_iota(jnp.int32, shape, 0) < 4


def call(body, outs, scratch=(), smem_in=(), n_in=0, smem_out=(), cost=None, specs=None):
    return pl.pallas_call(
        body,
        out_shape=outs,
        grid=(1,) if specs else (),
        in_specs=[(specs or {}).get(i, SM if i in smem_in else VM) for i in range(n_in)],
        out_specs=[SM if i in smem_out else VM for i in range(len(outs))],
        scratch_shapes=list(scratch),
        cost_estimate=cost,
        compiler_params=pltpu.CompilerParams(vmem_limit_bytes=56 * 1024 * 1024),
    )


def cost(us):
    return pl.CostEstimate(flops=int(us * 1e9), bytes_accessed=int(us * 1e6), transcendentals=0)


def sds(shape, dtype):
    return jax.ShapeDtypeStruct(shape, dtype)


def front_kernel(ids, x_ref, c_ref, wq_ref, wo_ref, send, slots, qkv_ref, g_ref, cnt, ss):
    @pl.loop(0, NB)
    def _(i):
        cnt[i] = 0

    @pl.loop(0, NB)
    def _(b):
        r = ids[b]
        k = cnt[r]
        cnt[r] = k + 1
        slots[b] = 2 * r + k

    send[:, :, 0:W] = jnp.zeros((CHIPS, 8, W), BF)
    low = low_rows((8, W))

    @pl.loop(0, 16)
    def _(i):
        x = x_ref[pl.ds(pl.multiple_of(i * 16, 16), 16), :].astype(F32)
        c = c_ref[pl.ds(pl.multiple_of(i * 16, 16), 16), :].astype(F32)
        for h in range(2):
            xa, ca = x[8 * h : 8 * h + 8], c[8 * h : 8 * h + 8]
            xr, cr = pltpu.roll(xa, 4, 0), pltpu.roll(ca, 4, 0)
            send[slots[4 * i + 2 * h], :, 0:W] = jnp.where(low, xa, cr).astype(BF)
            send[slots[4 * i + 2 * h + 1], :, 0:W] = jnp.where(low, xr, ca).astype(BF)

    ones = head_ones()
    qkv = mm(x_ref[...], wq_ref[...]).astype(BF)
    qkv_ref[...] = qkv
    g = mm_t(c_ref[...], wo_ref[...]).astype(BF)
    g_ref[...] = g
    kn = normalize(qkv[:, W : 2 * W], ones)[0].astype(BF)
    vn = normalize(qkv[:, 2 * W :], ones)[0].astype(BF)
    left = lax.broadcasted_iota(jnp.int32, (64, 128), 1) < 64
    for j in range(4):
        s = slice(128 * j, 128 * j + 128)
        a = t_mm(kn[:, s], vn[:, s])
        ss[64 * j : 64 * j + 64, :] = jnp.where(left, a[:64], a[64:])
        a = t_mm(qkv[:, s], g[:, s])
        ss[256 + 64 * j : 320 + 64 * j, :] = jnp.where(left, a[:64], a[64:])
    low2 = low_rows((8, 128))

    @pl.loop(0, 64)
    def _(i):
        v = ss[pl.ds(pl.multiple_of(i * 8, 8), 8), :]
        hi = v.astype(BF).astype(F32)
        lo = v - hi
        send[2 * i, :, W:] = jnp.where(low2, hi, pltpu.roll(lo, 4, 0)).astype(BF)
        send[2 * i + 1, :, W:] = jnp.where(low2, pltpu.roll(hi, 4, 0), lo).astype(BF)


def query_kernel(pos, x_ref, g_ref, keep, send):
    x, g = x_ref[...], g_ref[...]
    for core, dst in ((pos[3], keep), (1 - pos[3], send)):
        xk = mm(x, pick(core)).astype(BF)
        dst[...] = (t_mm(xk, g) * (1.0 / TOTAL)).astype(dst.dtype)


def pick(core):
    r = lax.broadcasted_iota(jnp.int32, (W, PTS), 0)
    k = lax.broadcasted_iota(jnp.int32, (W, PTS), 1)
    return jnp.where(r == 4 * (k % CHIPS) + 2 * core + k // CHIPS, 1.0, 0.0).astype(BF)


def chunk_kernel(recv, out):
    v = jnp.sum(recv[...].astype(F32), axis=0)
    out[...] = v + pltpu.roll(v, 4, 0)


def spread_kernel(a_ref, b_ref, keep, near, out, rows):
    v = ((a_ref[...] + b_ref[...]) * (1.0 / TOTAL)).astype(BF)
    out[:, :, 0:128] = jnp.broadcast_to(v[None], (CHIPS, 8, 128))
    tot = keep[...] + near[...].astype(F32)
    for j in range(2):
        for q in range(4):
            rows[pl.ds(4 * j + q, CHIPS, stride=8), :] = tot[CHIPS * j : CHIPS * j + CHIPS, 128 * q : 128 * q + 128]
    out[:, :, 128:256] = rows[...].reshape(CHIPS, 8, 128).astype(BF)


def expert_kernel(
    pos, recv, wi, wiy, win, wo, woy, won, b_ref, bp_ref, send, x_s, c_s, hid, gpre, o_s, k_s
):
    n = pos[3]
    mine = pl.ds(pl.multiple_of(n * 256, 256), 256)
    other = pl.ds(pl.multiple_of(256 - n * 256, 256), 256)
    low = low_rows((8, W))

    @pl.loop(0, 32)
    def _(i):
        xs, cs = [], []
        for h in range(2):
            a = recv[4 * i + 2 * h].astype(F32)
            b = recv[4 * i + 2 * h + 1].astype(F32)
            xs.append(jnp.where(low, a, pltpu.roll(b, 4, 0)))
            cs.append(jnp.where(low, pltpu.roll(a, 4, 0), b))
        rows = pl.ds(pl.multiple_of(i * 16, 16), 16)
        x_s[rows, :] = jnp.concatenate(xs, axis=0).astype(BF)
        c_s[rows, :] = jnp.concatenate(cs, axis=0).astype(BF)

    def act(pre, gh, cols):
        sq = pre * pre
        t = jnp.tanh(GS * (pre + GC * pre * sq))
        up = 0.5 * (1.0 + t)
        hid[:, cols] = (pre * up).astype(BF)
        slope = up + 0.5 * pre * (1.0 - t * t) * GS * (1.0 + 3.0 * GC * sq)
        gpre[:, cols] = (gh * slope).astype(BF)

    @pl.loop(0, 4)
    def _(i):
        cols = pl.ds(pl.multiple_of(i * 256, 256), 256)
        pre = mm(x_s[...], wi[:, cols]) + b_ref[:, cols]
        gh = mm_t(c_s[...], wo[cols, :])
        act(pre, gh, cols)

    @pl.loop(0, 4)
    def _(i):
        cols = pl.ds(pl.multiple_of(i * 256, 256), 256)
        pre = mm(x_s[:, mine], wiy[:, cols]) + mm(x_s[:, other], win[:, cols]) + bp_ref[:, cols]
        gh = mm_t(c_s[:, mine], woy[cols, :]) + mm_t(c_s[:, other], won[cols, :])
        act(pre, gh, pl.ds(pl.multiple_of(HALF + i * 256, 256), 256))

    for yr, kr, part in ((woy, wiy, mine), (won, win, other)):
        o_s[:, part] = mm(hid[:, :HALF], wo[:, part]) + mm(hid[:, HALF:], yr[...])
        k_s[:, part] = mm_t(gpre[:, :HALF], wi[part, :]) + mm_t(gpre[:, HALF:], kr[...])

    @pl.loop(0, 64)
    def _(i):
        rows = pl.ds(pl.multiple_of(i * 8, 8), 8)
        o, k = o_s[rows, :], k_s[rows, :]
        send[2 * i, :, :] = jnp.where(low, o, pltpu.roll(k, 4, 0)).astype(BF)
        send[2 * i + 1, :, :] = jnp.where(low, pltpu.roll(o, 4, 0), k).astype(BF)


def weight_in_kernel(pos, x_s, gpre, keep, send):
    n = pos[3]
    mine = pl.ds(pl.multiple_of(n * 256, 256), 256)
    other = pl.ds(pl.multiple_of(256 - n * 256, 256), 256)

    @pl.loop(0, 4)
    def _(i):
        cols = pl.ds(pl.multiple_of(i * 512, 512), 512)
        g = gpre[:, cols]
        keep[0:256, cols] = t_mm(x_s[:, mine], g) * SHARE
        send[0:256, cols] = (t_mm(x_s[:, other], g) * SHARE).astype(BF)
        bias = jnp.sum(g.astype(F32), axis=0, keepdims=True) * SHARE
        keep[256:272, cols] = jnp.broadcast_to(bias, (16, 512))
        send[256:272, cols] = jnp.broadcast_to(bias, (16, 512)).astype(BF)


def weight_out_kernel(pos, c_s, hid, keep, send):
    n = pos[3]
    mine = pl.ds(pl.multiple_of(n * 256, 256), 256)
    other = pl.ds(pl.multiple_of(256 - n * 256, 256), 256)

    @pl.loop(0, 4)
    def _(i):
        cols = pl.ds(pl.multiple_of(i * 512, 512), 512)
        h = hid[:, cols]
        keep[cols, :] = t_mm(h, c_s[:, mine]) * SHARE
        send[cols, :] = (t_mm(h, c_s[:, other]) * SHARE).astype(BF)


def merge_in_kernel(keep, recv, here, away):
    here[...] = keep[:, :HALF] + recv[:, :HALF].astype(F32)
    away[...] = (keep[:, HALF:] + recv[:, HALF:].astype(F32)).astype(BF)


def merge_out_kernel(keep, recv, here, away):
    here[...] = keep[:HALF, :] + recv[:HALF, :].astype(F32)
    away[...] = (keep[HALF:, :] + recv[HALF:, :].astype(F32)).astype(BF)


def end_in_kernel(pos, here, recv, out, bias, row):
    out[...] = here[:256, :] + recv[:256, :].astype(F32)
    row[...] = (here[256:272, :] + recv[256:272, :].astype(F32))[0:8, :]
    bias[...] = row[0:1, pl.ds(pl.multiple_of(pos[3] * 512, 512), 512)]


def end_out_kernel(here, recv, out):
    out[...] = here[...] + recv[...].astype(F32)


def attn_kernel(pos, rs, qkv_ref, g_ref, x_ref, c_ref, mix_ref, gq, keep, send, query, ss):
    low = low_rows((8, 128))

    @pl.loop(0, 32)
    def _(i):
        t = [
            jnp.where(low, rs[4 * i + 2 * h, :, 0:128].astype(F32), rs[4 * i + 2 * h + 1, :, 0:128].astype(F32))
            for h in range(2)
        ]
        ss[pl.ds(pl.multiple_of(i * 16, 16), 16), :] = jnp.concatenate(t, axis=0).astype(BF)

    ones = head_ones()
    qkv, g = qkv_ref[...], g_ref[...]
    ku, ks = normalize(qkv[:, W : 2 * W], ones)
    vu, vs = normalize(qkv[:, 2 * W :], ones)
    kn, vn = ku.astype(BF), vu.astype(BF)
    left = lax.broadcasted_iota(jnp.int32, (64, 128), 1) < 64
    total = jnp.sum(rs[:, :, 128:256].astype(F32), axis=0)
    total_hi = total.astype(BF)
    total_lo = (total - total_hi.astype(F32)).astype(BF)
    block = lax.broadcasted_iota(jnp.int32, (8, 128), 0) % 4

    def diag(p):
        z = jnp.zeros_like(p)
        return jnp.concatenate([jnp.where(left, p, z), jnp.where(left, z, p)], axis=0)

    gk, gv = [], []
    rows = jnp.zeros((8, 128), F32)
    for j in range(4):
        s = slice(128 * j, 128 * j + 128)
        sm = diag(ss[64 * j : 64 * j + 64, :].astype(F32)).astype(BF)
        gs = diag(ss[256 + 64 * j : 320 + 64 * j, :].astype(F32)).astype(BF)
        mix_ref[:, s] = mm(qkv[:, s], sm).astype(BF)
        gq[:, s] = mm_t(g[:, s], sm).astype(BF)
        rows = jnp.where(block == j, mm_t(total_hi, sm) + mm_t(total_lo, sm), rows)
        gk.append(mm_t(vn[:, s], gs))
        gv.append(mm(kn[:, s], gs))
    query[...] = rows

    def back(gr, u, sc):
        return ((gr - head_mean(gr, ones) - u * head_mean(gr * u, ones)) / sc).astype(BF)

    gq[:, W : 2 * W] = back(jnp.concatenate(gk, axis=1), ku, ks)
    gq[:, 2 * W :] = back(jnp.concatenate(gv, axis=1), vu, vs)
    x, c, mixed = x_ref[...], c_ref[...], mix_ref[...]
    for core, dst in ((pos[3], keep), (1 - pos[3], send)):
        sel = pick(core)
        xk, mk = mm(x, sel).astype(BF), mm(mixed, sel).astype(BF)
        for q in range(2):
            dst[:, W * q : W * q + W] = (t_mm(xk, gq[:, W * q + W : W * q + 2 * W]) * (1.0 / TOTAL)).astype(dst.dtype)
        dst[:, 2 * W :] = (t_mm(mk, c) * (1.0 / TOTAL)).astype(dst.dtype)


def base_kernel(x, c, mixed, gq, wq, wo, base_o, base_k):
    base_o[...] = x[...].astype(F32) + mm(mixed[...], wo[...])
    base_k[...] = c[...].astype(F32) + mm_t(gq[...], wq[...])


def join_kernel(ret, keep, near, out, rows):
    out[:, :, 0:W] = ret[...]
    size = 8 * CHIPS
    for t in range(3):
        for j in range(2):
            part = slice(CHIPS * j, CHIPS * j + CHIPS)
            for q in range(4):
                cols = slice(384 * q + 128 * t, 384 * q + 128 * t + 128)
                v = keep[part, cols] + near[part, cols].astype(F32)
                rows[pl.ds(size * t + 4 * j + q, CHIPS, stride=8), :] = v
        v = rows[size * t : size * t + size, :].reshape(CHIPS, 8, 128)
        out[:, :, W + 128 * t : W + 128 * t + 128] = v.astype(BF)


def final_kernel(slots, ret, base_o, base_k, query, lo, gf, att):
    low = low_rows((8, W))

    @pl.loop(0, 16)
    def _(i):
        os, ks = [], []
        for h in range(2):
            a = ret[slots[4 * i + 2 * h], :, 0:W].astype(F32)
            b = ret[slots[4 * i + 2 * h + 1], :, 0:W].astype(F32)
            os.append(jnp.where(low, a, pltpu.roll(b, 4, 0)))
            ks.append(jnp.where(low, pltpu.roll(a, 4, 0), b))
        rows = pl.ds(pl.multiple_of(i * 16, 16), 16)
        lo[rows, :] = (base_o[rows, :] + jnp.concatenate(os, axis=0)).astype(BF)
        gf[rows, :] = (base_k[rows, :] + jnp.concatenate(ks, axis=0)).astype(BF)

    v = jnp.sum(ret[:, :, W:].astype(F32), axis=0)
    q = query[...]
    for j in range(2):
        for b in range(4):
            r = slice(4 * j + b, 4 * j + b + 1)
            att[j : j + 1, 128 * b : 128 * b + 128] = q[r]
            att[j : j + 1, W + 384 * b : W + 384 * b + 384] = v[r]


def layer(x, ids, wq, wo_att, wi, bi, wo, c):
    n = lax.axis_index("narrow")
    w = lax.axis_index("wide")
    pos = jnp.stack([w // 16, w // 4 % 4, w % 4, n]).astype(jnp.int32)
    pair = [(i, i ^ 1) for i in range(CHIPS)]
    swap = [(0, 1), (1, 0)]

    def across(v):
        return lax.ppermute(v, "wide", pair)

    def beside(v):
        return lax.ppermute(v, "narrow", swap)

    def deal(v):
        return lax.all_to_all(v, "wide", split_axis=0, concat_axis=0, tiled=True)

    def run(body, us, outs, args, scratch=(), smem_in=(), smem_out=(), specs=None):
        return call(
            body, outs, scratch, smem_in=smem_in, n_in=len(args), smem_out=smem_out, cost=cost(us),
            specs=specs,
        )(*args)

    wiy = across(lax.dynamic_slice_in_dim(wi, n * 256, 256, 0))
    woy = across(lax.dynamic_slice_in_dim(wo, n * 256, 256, 1))
    bp = across(bi)
    win, won = beside(wiy), beside(woy)

    send, slots, qkv, g = run(
        front_kernel, 5,
        [sds((CHIPS, 8, 640), BF), sds((NB,), jnp.int32), sds((PTS, 3 * W), BF), sds((PTS, W), BF)],
        (ids, x, c, wq, wo_att), [pltpu.SMEM((NB,), jnp.int32), pltpu.VMEM((W, 128), F32)], (0,), (1,),
    )
    recv = deal(send)
    keep_q, away_q = run(query_kernel, 2, [sds((PTS, W), F32), sds((PTS, W), BF)], (pos, x, g), (), (0,))
    near_q = beside(away_q)
    (chunk,) = run(
        chunk_kernel, 1, [sds((8, 128), F32)], (recv,),
        specs={0: pl.BlockSpec((CHIPS, 8, 128), lambda i: (0, 0, 4))},
    )
    (spread,) = run(
        spread_kernel, 1, [sds((CHIPS, 8, 256), BF)], (chunk, beside(chunk), keep_q, near_q),
        [pltpu.VMEM((8 * CHIPS, 128), F32)],
    )
    rs = deal(spread)
    ret, x_s, c_s, hid, gpre = run(
        expert_kernel, 12,
        [sds((CHIPS, 8, W), BF), sds((W, W), BF), sds((W, W), BF), sds((W, 2 * HALF), BF), sds((W, 2 * HALF), BF)],
        (pos, recv, wi, wiy, win, wo, woy, won, bi.reshape(1, HALF), bp.reshape(1, HALF)),
        [pltpu.VMEM((W, W), F32), pltpu.VMEM((W, W), F32)], (0,),
        specs={1: pl.BlockSpec((CHIPS, 8, W), lambda i: (0, 0, 0))},
    )
    mixed, gq, keep, away, query = run(
        attn_kernel, 7,
        [sds((PTS, W), BF), sds((PTS, 3 * W), BF), sds((PTS, 3 * W), F32), sds((PTS, 3 * W), BF), sds((8, 128), F32)],
        (pos, rs, qkv, g, x, c), [pltpu.VMEM((W, 128), BF)], (0,),
    )
    near = beside(away)
    base_o, base_k = run(base_kernel, 2, [sds((PTS, W), F32), sds((PTS, W), F32)], (x, c, mixed, gq, wq, wo_att))
    (joined,) = run(join_kernel, 2, [sds((CHIPS, 8, 896), BF)], (ret, keep, near), [pltpu.VMEM((24 * CHIPS, 128), F32)])
    back = deal(joined)
    keep_i, send_i = run(
        weight_in_kernel, 4, [sds((272, 2 * HALF), F32), sds((272, 2 * HALF), BF)], (pos, x_s, gpre), (), (0,)
    )
    got_i = beside(send_i)
    keep_o, send_o = run(
        weight_out_kernel, 4, [sds((2 * HALF, 256), F32), sds((2 * HALF, 256), BF)], (pos, c_s, hid), (), (0,)
    )
    got_o = beside(send_o)
    here_i, away_i = run(merge_in_kernel, 1, [sds((272, HALF), F32), sds((272, HALF), BF)], (keep_i, got_i))
    far_i = across(away_i)
    here_o, away_o = run(merge_out_kernel, 1, [sds((HALF, 256), F32), sds((HALF, 256), BF)], (keep_o, got_o))
    far_o = across(away_o)
    grad_in, grad_b = run(
        end_in_kernel, 1, [sds((256, HALF), F32), sds((1, 512), F32)],
        (pos, here_i, far_i), [pltpu.VMEM((8, HALF), F32)], (0,),
    )
    (grad_out,) = run(end_out_kernel, 1, [sds((HALF, 256), F32)], (here_o, far_o))
    layer_out, grad_feats, att = run(
        final_kernel, 3, [sds((PTS, W), BF), sds((PTS, W), BF), sds((2, 4 * W), F32)],
        (slots, back, base_o, base_k, query), (), (0,),
    )
    return (layer_out, grad_feats, att, grad_in, grad_out, grad_b.reshape(512))


def solution(mesh):
    placed = (
        P(("wide", "narrow"), None),
        P(("wide", "narrow")),
        P(),
        P(),
        P(None, "wide"),
        P("wide"),
        P("wide", None),
        P(("wide", "narrow"), None),
    )
    return jax.shard_map(
        layer,
        mesh=mesh,
        in_specs=placed,
        out_specs=(
            P(("wide", "narrow"), None),
            P(("wide", "narrow"), None),
            P(("wide", "narrow"), None),
            P("narrow", "wide"),
            P("wide", "narrow"),
            P(("wide", "narrow")),
        ),
        check_vma=False,
    )
```

```python
import jax
import jax.numpy as jnp
from jax import lax
from jax.experimental import pallas as pl
from jax.experimental.pallas import tpu as pltpu
from jax.sharding import PartitionSpec as P

F32 = jnp.float32
BF = jnp.bfloat16
EPS = 1e-05
GS = 0.7978845608
GC = 0.044715
W = 512
PTS = 256
NB = 64
CHIPS = 128
TOTAL = 65536.0
SHARE = 64.0 / 65536.0
HALF = 1024
VM = pl.BlockSpec(memory_space=pltpu.VMEM)
SM = pl.BlockSpec(memory_space=pltpu.SMEM)


def mm(a, b):
    return jnp.dot(a, b, preferred_element_type=F32)


def mm_t(a, b):
    return lax.dot_general(a, b, (((1,), (1,)), ((), ())), preferred_element_type=F32)


def t_mm(a, b):
    return lax.dot_general(a, b, (((0,), (0,)), ((), ())), preferred_element_type=F32)


def head_ones():
    r = lax.broadcasted_iota(jnp.int32, (W, W), 0) // 64
    c = lax.broadcasted_iota(jnp.int32, (W, W), 1) // 64
    return jnp.where(r == c, 1.0 / 64.0, 0.0).astype(BF)


def head_mean(v, ones):
    hi = v.astype(BF)
    lo = (v - hi.astype(F32)).astype(BF)
    return mm(hi, ones) + mm(lo, ones)


def normalize(raw, ones):
    cen = raw.astype(F32) - mm(raw, ones)
    scale = jnp.sqrt(head_mean(cen * cen, ones) + EPS)
    return cen / scale, scale


def low_rows(shape):
    return lax.broadcasted_iota(jnp.int32, shape, 0) < 4


def call(body, outs, scratch=(), smem_in=(), n_in=0, smem_out=(), cost=None, specs=None, mib=24):
    return pl.pallas_call(
        body,
        out_shape=outs,
        grid=(1,) if specs else (),
        in_specs=[(specs or {}).get(i, SM if i in smem_in else VM) for i in range(n_in)],
        out_specs=[SM if i in smem_out else VM for i in range(len(outs))],
        scratch_shapes=list(scratch),
        cost_estimate=cost,
        compiler_params=pltpu.CompilerParams(vmem_limit_bytes=mib * 1024 * 1024),
    )


def cost(us):
    return pl.CostEstimate(flops=int(us * 1e9), bytes_accessed=int(us * 1e6), transcendentals=0)


def sds(shape, dtype):
    return jax.ShapeDtypeStruct(shape, dtype)


def front_kernel(ids, x_ref, c_ref, wq_ref, wo_ref, send, slots, qkv_ref, g_ref, cnt, ss):
    @pl.loop(0, NB)
    def _(i):
        cnt[i] = 0

    @pl.loop(0, NB)
    def _(b):
        r = ids[b]
        k = cnt[r]
        cnt[r] = k + 1
        slots[b] = 2 * r + k

    send[:, :, 0:W] = jnp.zeros((CHIPS, 8, W), BF)
    low = low_rows((8, W))

    @pl.loop(0, 16)
    def _(i):
        x = x_ref[pl.ds(pl.multiple_of(i * 16, 16), 16), :].astype(F32)
        c = c_ref[pl.ds(pl.multiple_of(i * 16, 16), 16), :].astype(F32)
        for h in range(2):
            xa, ca = x[8 * h : 8 * h + 8], c[8 * h : 8 * h + 8]
            xr, cr = pltpu.roll(xa, 4, 0), pltpu.roll(ca, 4, 0)
            send[slots[4 * i + 2 * h], :, 0:W] = jnp.where(low, xa, cr).astype(BF)
            send[slots[4 * i + 2 * h + 1], :, 0:W] = jnp.where(low, xr, ca).astype(BF)

    ones = head_ones()
    qkv = mm(x_ref[...], wq_ref[...]).astype(BF)
    qkv_ref[...] = qkv
    g = mm_t(c_ref[...], wo_ref[...]).astype(BF)
    g_ref[...] = g
    kn = normalize(qkv[:, W : 2 * W], ones)[0].astype(BF)
    vn = normalize(qkv[:, 2 * W :], ones)[0].astype(BF)
    left = lax.broadcasted_iota(jnp.int32, (64, 128), 1) < 64
    for j in range(4):
        s = slice(128 * j, 128 * j + 128)
        a = t_mm(kn[:, s], vn[:, s])
        ss[64 * j : 64 * j + 64, :] = jnp.where(left, a[:64], a[64:])
        a = t_mm(qkv[:, s], g[:, s])
        ss[256 + 64 * j : 320 + 64 * j, :] = jnp.where(left, a[:64], a[64:])
    low2 = low_rows((8, 128))

    @pl.loop(0, 64)
    def _(i):
        v = ss[pl.ds(pl.multiple_of(i * 8, 8), 8), :]
        hi = v.astype(BF).astype(F32)
        lo = v - hi
        send[2 * i, :, W:] = jnp.where(low2, hi, pltpu.roll(lo, 4, 0)).astype(BF)
        send[2 * i + 1, :, W:] = jnp.where(low2, pltpu.roll(hi, 4, 0), lo).astype(BF)


def query_kernel(pos, x_ref, g_ref, keep, send):
    x, g = x_ref[...], g_ref[...]
    for core, dst in ((pos[3], keep), (1 - pos[3], send)):
        xk = mm(x, pick(core)).astype(BF)
        dst[...] = (t_mm(xk, g) * (1.0 / TOTAL)).astype(dst.dtype)


def pick(core):
    r = lax.broadcasted_iota(jnp.int32, (W, PTS), 0)
    k = lax.broadcasted_iota(jnp.int32, (W, PTS), 1)
    return jnp.where(r == 4 * (k % CHIPS) + 2 * core + k // CHIPS, 1.0, 0.0).astype(BF)


def deal_query_kernel(keep, near, out, rows):
    tot = keep[...] + near[...].astype(F32)
    for j in range(2):
        for q in range(4):
            rows[pl.ds(4 * j + q, CHIPS, stride=8), :] = tot[CHIPS * j : CHIPS * j + CHIPS, 128 * q : 128 * q + 128]
    out[...] = rows[...].reshape(CHIPS, 8, 128).astype(BF)


def spread_kernel(recv, query, out):
    v = jnp.sum(recv[...].astype(F32), axis=0)
    v = (v + pltpu.roll(v, 4, 0)) * (1.0 / TOTAL)
    hi = v.astype(BF).astype(F32)
    v = jnp.where(low_rows((8, 128)), hi, v - hi).astype(BF)
    out[:, :, 0:128] = jnp.broadcast_to(v[None], (CHIPS, 8, 128))
    out[:, :, 128:256] = query[...]


def expert_kernel(
    pos, recv, wi, wiy, win, wo, woy, won, b_ref, bp_ref, send, x_s, c_s, hid, gpre, o_s, k_s
):
    n = pos[3]
    mine = pl.ds(pl.multiple_of(n * 256, 256), 256)
    other = pl.ds(pl.multiple_of(256 - n * 256, 256), 256)
    low = low_rows((8, W))

    @pl.loop(0, 32)
    def _(i):
        xs, cs = [], []
        for h in range(2):
            a = recv[4 * i + 2 * h].astype(F32)
            b = recv[4 * i + 2 * h + 1].astype(F32)
            xs.append(jnp.where(low, a, pltpu.roll(b, 4, 0)))
            cs.append(jnp.where(low, pltpu.roll(a, 4, 0), b))
        rows = pl.ds(pl.multiple_of(i * 16, 16), 16)
        x_s[rows, :] = jnp.concatenate(xs, axis=0).astype(BF)
        c_s[rows, :] = jnp.concatenate(cs, axis=0).astype(BF)

    def act(pre, gh, cols):
        sq = pre * pre
        t = jnp.tanh(GS * (pre + GC * pre * sq))
        up = 0.5 * (1.0 + t)
        hid[:, cols] = (pre * up).astype(BF)
        slope = up + 0.5 * pre * (1.0 - t * t) * GS * (1.0 + 3.0 * GC * sq)
        gpre[:, cols] = (gh * slope).astype(BF)

    @pl.loop(0, 4)
    def _(i):
        cols = pl.ds(pl.multiple_of(i * 256, 256), 256)
        pre = mm(x_s[...], wi[:, cols]) + b_ref[:, cols]
        gh = mm_t(c_s[...], wo[cols, :])
        act(pre, gh, cols)

    @pl.loop(0, 4)
    def _(i):
        cols = pl.ds(pl.multiple_of(i * 256, 256), 256)
        pre = mm(x_s[:, mine], wiy[:, cols]) + mm(x_s[:, other], win[:, cols]) + bp_ref[:, cols]
        gh = mm_t(c_s[:, mine], woy[cols, :]) + mm_t(c_s[:, other], won[cols, :])
        act(pre, gh, pl.ds(pl.multiple_of(HALF + i * 256, 256), 256))

    for yr, kr, part in ((woy, wiy, mine), (won, win, other)):
        o_s[:, part] = mm(hid[:, :HALF], wo[:, part]) + mm(hid[:, HALF:], yr[...])
        k_s[:, part] = mm_t(gpre[:, :HALF], wi[part, :]) + mm_t(gpre[:, HALF:], kr[...])

    @pl.loop(0, 64)
    def _(i):
        rows = pl.ds(pl.multiple_of(i * 8, 8), 8)
        o, k = o_s[rows, :], k_s[rows, :]
        send[2 * i, :, :] = jnp.where(low, o, pltpu.roll(k, 4, 0)).astype(BF)
        send[2 * i + 1, :, :] = jnp.where(low, pltpu.roll(o, 4, 0), k).astype(BF)


def weight_kernel(pos, x_s, c_s, hid, gpre, keep_i, send_i, keep_o, send_o):
    n = pos[3]
    mine = pl.ds(pl.multiple_of(n * 256, 256), 256)
    other = pl.ds(pl.multiple_of(256 - n * 256, 256), 256)

    @pl.loop(0, 2)
    def _(i):
        cols = pl.ds(pl.multiple_of(i * 512, 512), 512)
        g = gpre[:, cols]
        keep_i[0:256, cols] = t_mm(x_s[:, mine], g) * SHARE
        send_i[0:256, cols] = (t_mm(x_s[:, other], g) * SHARE).astype(BF)
        bias = jnp.sum(g.astype(F32), axis=0, keepdims=True) * SHARE
        keep_i[256:272, cols] = jnp.broadcast_to(bias, (16, 512))
        send_i[256:272, cols] = jnp.broadcast_to(bias, (16, 512)).astype(BF)
        h = hid[:, cols]
        keep_o[cols, :] = t_mm(h, c_s[:, mine]) * SHARE
        send_o[cols, :] = (t_mm(h, c_s[:, other]) * SHARE).astype(BF)


def merge_kernel(keep_i, got_i, keep_o, got_o, away_i, away_o):
    away_i[...] = (keep_i[...] + got_i[...].astype(F32)).astype(BF)
    away_o[...] = (keep_o[...] + got_o[...].astype(F32)).astype(BF)


def end_kernel(pos, keep_i, got_i, far_i, keep_o, got_o, far_o, grad_i, bias, grad_o, row):
    def total(a, b, c, rows):
        return a[rows, :] + b[rows, :].astype(F32) + c[rows, :].astype(F32)

    grad_i[...] = total(keep_i, got_i, far_i, slice(0, 256))
    row[...] = total(keep_i, got_i, far_i, slice(256, 272))[0:8, :]
    bias[...] = row[0:1, pl.ds(pl.multiple_of(pos[3] * 512, 512), 512)]
    grad_o[...] = total(keep_o, got_o, far_o, slice(0, HALF))


def attn_kernel(pos, rs, rs2, qkv_ref, g_ref, x_ref, c_ref, mix_ref, gq, keep, send, query, ss):
    low = low_rows((8, 128))

    @pl.loop(0, 32)
    def _(i):
        tiles = []
        for h in range(2):
            pair = []
            for k in range(2):
                d = 4 * i + 2 * h + k
                v = rs[d, :, 0:128].astype(F32) + rs2[d].astype(F32)
                pair.append(v + pltpu.roll(v, 4, 0))
            tiles.append(jnp.where(low, pair[0], pair[1]))
        ss[pl.ds(pl.multiple_of(i * 16, 16), 16), :] = jnp.concatenate(tiles, axis=0).astype(BF)

    ones = head_ones()
    qkv, g = qkv_ref[...], g_ref[...]
    ku, ks = normalize(qkv[:, W : 2 * W], ones)
    vu, vs = normalize(qkv[:, 2 * W :], ones)
    kn, vn = ku.astype(BF), vu.astype(BF)
    left = lax.broadcasted_iota(jnp.int32, (64, 128), 1) < 64
    total = jnp.sum(rs[:, :, 128:256].astype(F32), axis=0)
    total_hi = total.astype(BF)
    total_lo = (total - total_hi.astype(F32)).astype(BF)
    block = lax.broadcasted_iota(jnp.int32, (8, 128), 0) % 4

    def diag(p):
        z = jnp.zeros_like(p)
        return jnp.concatenate([jnp.where(left, p, z), jnp.where(left, z, p)], axis=0)

    gk, gv = [], []
    rows = jnp.zeros((8, 128), F32)
    for j in range(4):
        s = slice(128 * j, 128 * j + 128)
        sm = diag(ss[64 * j : 64 * j + 64, :].astype(F32)).astype(BF)
        gs = diag(ss[256 + 64 * j : 320 + 64 * j, :].astype(F32)).astype(BF)
        mix_ref[:, s] = mm(qkv[:, s], sm).astype(BF)
        gq[:, s] = mm_t(g[:, s], sm).astype(BF)
        rows = jnp.where(block == j, mm_t(total_hi, sm) + mm_t(total_lo, sm), rows)
        gk.append(mm_t(vn[:, s], gs))
        gv.append(mm(kn[:, s], gs))
    query[...] = rows

    def back(gr, u, sc):
        return ((gr - head_mean(gr, ones) - u * head_mean(gr * u, ones)) / sc).astype(BF)

    gq[:, W : 2 * W] = back(jnp.concatenate(gk, axis=1), ku, ks)
    gq[:, 2 * W :] = back(jnp.concatenate(gv, axis=1), vu, vs)
    x, c, mixed = x_ref[...], c_ref[...], mix_ref[...]
    for core, dst in ((pos[3], keep), (1 - pos[3], send)):
        sel = pick(core)
        xk, mk = mm(x, sel).astype(BF), mm(mixed, sel).astype(BF)
        for q in range(2):
            dst[:, W * q : W * q + W] = (t_mm(xk, gq[:, W * q + W : W * q + 2 * W]) * (1.0 / TOTAL)).astype(dst.dtype)
        dst[:, 2 * W :] = (t_mm(mk, c) * (1.0 / TOTAL)).astype(dst.dtype)


def base_kernel(x, c, mixed, gq, wq, wo, base_o, base_k):
    base_o[...] = x[...].astype(F32) + mm(mixed[...], wo[...])
    base_k[...] = c[...].astype(F32) + mm_t(gq[...], wq[...])


def join_kernel(ret, keep, near, out, rows):
    out[:, :, 0:W] = ret[...]
    size = 8 * CHIPS
    for t in range(3):
        for j in range(2):
            part = slice(CHIPS * j, CHIPS * j + CHIPS)
            for q in range(4):
                cols = slice(384 * q + 128 * t, 384 * q + 128 * t + 128)
                v = keep[part, cols] + near[part, cols].astype(F32)
                rows[pl.ds(size * t + 4 * j + q, CHIPS, stride=8), :] = v
        v = rows[size * t : size * t + size, :].reshape(CHIPS, 8, 128)
        out[:, :, W + 128 * t : W + 128 * t + 128] = v.astype(BF)


def final_kernel(slots, ret, base_o, base_k, query, lo, gf, att):
    low = low_rows((8, W))

    @pl.loop(0, 16)
    def _(i):
        os, ks = [], []
        for h in range(2):
            a = ret[slots[4 * i + 2 * h], :, 0:W].astype(F32)
            b = ret[slots[4 * i + 2 * h + 1], :, 0:W].astype(F32)
            os.append(jnp.where(low, a, pltpu.roll(b, 4, 0)))
            ks.append(jnp.where(low, pltpu.roll(a, 4, 0), b))
        rows = pl.ds(pl.multiple_of(i * 16, 16), 16)
        lo[rows, :] = (base_o[rows, :] + jnp.concatenate(os, axis=0)).astype(BF)
        gf[rows, :] = (base_k[rows, :] + jnp.concatenate(ks, axis=0)).astype(BF)

    v = jnp.sum(ret[:, :, W:].astype(F32), axis=0)
    q = query[...]
    for j in range(2):
        for b in range(4):
            r = slice(4 * j + b, 4 * j + b + 1)
            att[j : j + 1, 128 * b : 128 * b + 128] = q[r]
            att[j : j + 1, W + 384 * b : W + 384 * b + 384] = v[r]


def layer(x, ids, wq, wo_att, wi, bi, wo, c):
    n = lax.axis_index("narrow")
    w = lax.axis_index("wide")
    pos = jnp.stack([w // 16, w // 4 % 4, w % 4, n]).astype(jnp.int32)
    pair = [(i, i ^ 1) for i in range(CHIPS)]
    swap = [(0, 1), (1, 0)]

    def across(v):
        return lax.ppermute(v, "wide", pair)

    def beside(v):
        return lax.ppermute(v, "narrow", swap)

    def deal(v):
        return lax.all_to_all(v, "wide", split_axis=0, concat_axis=0, tiled=True)

    def run(body, us, outs, args, scratch=(), smem_in=(), smem_out=(), specs=None, mib=24):
        return call(
            body, outs, scratch, smem_in=smem_in, n_in=len(args), smem_out=smem_out, cost=cost(us),
            specs=specs, mib=mib,
        )(*args)

    wiy = across(lax.dynamic_slice_in_dim(wi, n * 256, 256, 0))
    woy = across(lax.dynamic_slice_in_dim(wo, n * 256, 256, 1))
    bp = across(bi)
    win, won = beside(wiy), beside(woy)

    send, slots, qkv, g = run(
        front_kernel, 5,
        [sds((CHIPS, 8, 640), BF), sds((NB,), jnp.int32), sds((PTS, 3 * W), BF), sds((PTS, W), BF)],
        (ids, x, c, wq, wo_att), [pltpu.SMEM((NB,), jnp.int32), pltpu.VMEM((W, 128), F32)], (0,), (1,),
    )
    recv = deal(send)
    keep_q, away_q = run(query_kernel, 2, [sds((PTS, W), F32), sds((PTS, W), BF)], (pos, x, g), (), (0,))
    (dealt_q,) = run(
        deal_query_kernel, 1, [sds((CHIPS, 8, 128), BF)], (keep_q, beside(away_q)),
        [pltpu.VMEM((8 * CHIPS, 128), F32)],
    )
    (spread,) = run(
        spread_kernel, 1, [sds((CHIPS, 8, 256), BF)], (recv, dealt_q),
        specs={0: pl.BlockSpec((CHIPS, 8, 128), lambda i: (0, 0, 4))},
    )
    rs = deal(spread)
    ret, x_s, c_s, hid, gpre = run(
        expert_kernel, 12,
        [sds((CHIPS, 8, W), BF), sds((W, W), BF), sds((W, W), BF), sds((W, 2 * HALF), BF), sds((W, 2 * HALF), BF)],
        (pos, recv, wi, wiy, win, wo, woy, won, bi.reshape(1, HALF), bp.reshape(1, HALF)),
        [pltpu.VMEM((W, W), F32), pltpu.VMEM((W, W), F32)], (0,),
        specs={1: pl.BlockSpec((CHIPS, 8, W), lambda i: (0, 0, 0))}, mib=32,
    )
    rs2 = beside(rs)

    def weights(half):
        part = pl.BlockSpec((W, HALF), lambda i: (0, half))
        return run(
            weight_kernel, 5,
            [sds((272, HALF), F32), sds((272, HALF), BF), sds((HALF, 256), F32), sds((HALF, 256), BF)],
            (pos, x_s, c_s, hid, gpre), (), (0,), specs={3: part, 4: part},
        )

    keep_i, send_i, keep_o, send_o = weights(1)
    got_i, got_o = beside(send_i), beside(send_o)
    mixed, gq, keep, away, query = run(
        attn_kernel, 7,
        [sds((PTS, W), BF), sds((PTS, 3 * W), BF), sds((PTS, 3 * W), F32), sds((PTS, 3 * W), BF), sds((8, 128), F32)],
        (pos, rs, rs2, qkv, g, x, c), [pltpu.VMEM((W, 128), BF)], (0,),
        specs={2: pl.BlockSpec((CHIPS, 8, 128), lambda i: (0, 0, 0))},
    )
    near = beside(away)
    away_i, away_o = run(merge_kernel, 2, [sds((272, HALF), BF), sds((HALF, 256), BF)], (keep_i, got_i, keep_o, got_o))
    far_i, far_o = across(away_i), across(away_o)
    (joined,) = run(join_kernel, 2, [sds((CHIPS, 8, 896), BF)], (ret, keep, near), [pltpu.VMEM((24 * CHIPS, 128), F32)])
    back = deal(joined)
    base_o, base_k = run(base_kernel, 2, [sds((PTS, W), F32), sds((PTS, W), F32)], (x, c, mixed, gq, wq, wo_att))
    keep_i, send_i, keep_o, send_o = weights(0)
    got_i, got_o = beside(send_i), beside(send_o)
    grad_in, grad_b, grad_out = run(
        end_kernel, 3, [sds((256, HALF), F32), sds((1, 512), F32), sds((HALF, 256), F32)],
        (pos, keep_i, got_i, far_i, keep_o, got_o, far_o), [pltpu.VMEM((8, HALF), F32)], (0,),
    )
    layer_out, grad_feats, att = run(
        final_kernel, 3, [sds((PTS, W), BF), sds((PTS, W), BF), sds((2, 4 * W), F32)],
        (slots, back, base_o, base_k, query), (), (0,),
    )
    return (layer_out, grad_feats, att, grad_in, grad_out, grad_b.reshape(512))


def solution(mesh):
    placed = (
        P(("wide", "narrow"), None),
        P(("wide", "narrow")),
        P(),
        P(),
        P(None, "wide"),
        P("wide"),
        P("wide", None),
        P(("wide", "narrow"), None),
    )
    return jax.shard_map(
        layer,
        mesh=mesh,
        in_specs=placed,
        out_specs=(
            P(("wide", "narrow"), None),
            P(("wide", "narrow"), None),
            P(("wide", "narrow"), None),
            P("narrow", "wide"),
            P("wide", "narrow"),
            P(("wide", "narrow")),
        ),
        check_vma=False,
    )
```

```python
import jax
import jax.numpy as jnp
from jax import lax
from jax.experimental import pallas as pl
from jax.experimental.pallas import tpu as pltpu
from jax.sharding import PartitionSpec as P

F32 = jnp.float32
BF = jnp.bfloat16
EPS = 1e-05
GS = 0.7978845608
GC = 0.044715
W = 512
PTS = 256
NB = 64
CHIPS = 128
TOTAL = 65536.0
SHARE = 64.0 / 65536.0
HALF = 1024
VM = pl.BlockSpec(memory_space=pltpu.VMEM)
SM = pl.BlockSpec(memory_space=pltpu.SMEM)


def mm(a, b):
    return jnp.dot(a, b, preferred_element_type=F32)


def mm_t(a, b):
    return lax.dot_general(a, b, (((1,), (1,)), ((), ())), preferred_element_type=F32)


def t_mm(a, b):
    return lax.dot_general(a, b, (((0,), (0,)), ((), ())), preferred_element_type=F32)


def head_ones():
    r = lax.broadcasted_iota(jnp.int32, (W, W), 0) // 64
    c = lax.broadcasted_iota(jnp.int32, (W, W), 1) // 64
    return jnp.where(r == c, 1.0 / 64.0, 0.0).astype(BF)


def head_mean(v, ones):
    hi = v.astype(BF)
    lo = (v - hi.astype(F32)).astype(BF)
    return mm(hi, ones) + mm(lo, ones)


def normalize(raw, ones):
    cen = raw.astype(F32) - mm(raw, ones)
    scale = jnp.sqrt(head_mean(cen * cen, ones) + EPS)
    return cen / scale, scale


def low_rows(shape):
    return lax.broadcasted_iota(jnp.int32, shape, 0) < 4


def call(body, outs, scratch=(), smem_in=(), n_in=0, smem_out=(), cost=None, specs=None, mib=24):
    return pl.pallas_call(
        body,
        out_shape=outs,
        grid=(1,) if specs else (),
        in_specs=[(specs or {}).get(i, SM if i in smem_in else VM) for i in range(n_in)],
        out_specs=[SM if i in smem_out else VM for i in range(len(outs))],
        scratch_shapes=list(scratch),
        cost_estimate=cost,
        compiler_params=pltpu.CompilerParams(vmem_limit_bytes=mib * 1024 * 1024),
    )


def cost(us):
    return pl.CostEstimate(flops=int(us * 1e9), bytes_accessed=int(us * 1e6), transcendentals=0)


def sds(shape, dtype):
    return jax.ShapeDtypeStruct(shape, dtype)


def far(shape, dtype):
    return pltpu.HBM(shape, dtype)


def in_hbm(v):
    return pltpu.with_memory_space_constraint(v, pltpu.HBM)


def front_kernel(ids, x_ref, c_ref, wq_hbm, wo_hbm, send, slots, qkv_ref, g_ref, cnt, ss, wq_ref, wo_ref, sems):
    loads = [
        pltpu.make_async_copy(wq_hbm, wq_ref, sems.at[0]),
        pltpu.make_async_copy(wo_hbm, wo_ref, sems.at[1]),
    ]
    for load in loads:
        load.start()

    @pl.loop(0, NB)
    def _(i):
        cnt[i] = 0

    @pl.loop(0, NB)
    def _(b):
        r = ids[b]
        k = cnt[r]
        cnt[r] = k + 1
        slots[b] = 2 * r + k

    send[:, :, 0:W] = jnp.zeros((CHIPS, 8, W), BF)
    low = low_rows((8, W))

    @pl.loop(0, 16)
    def _(i):
        x = x_ref[pl.ds(pl.multiple_of(i * 16, 16), 16), :].astype(F32)
        c = c_ref[pl.ds(pl.multiple_of(i * 16, 16), 16), :].astype(F32)
        for h in range(2):
            xa, ca = x[8 * h : 8 * h + 8], c[8 * h : 8 * h + 8]
            xr, cr = pltpu.roll(xa, 4, 0), pltpu.roll(ca, 4, 0)
            send[slots[4 * i + 2 * h], :, 0:W] = jnp.where(low, xa, cr).astype(BF)
            send[slots[4 * i + 2 * h + 1], :, 0:W] = jnp.where(low, xr, ca).astype(BF)

    for load in loads:
        load.wait()
    ones = head_ones()
    qkv = mm(x_ref[...], wq_ref[...]).astype(BF)
    qkv_ref[...] = qkv
    g = mm_t(c_ref[...], wo_ref[...]).astype(BF)
    g_ref[...] = g
    kn = normalize(qkv[:, W : 2 * W], ones)[0].astype(BF)
    vn = normalize(qkv[:, 2 * W :], ones)[0].astype(BF)
    left = lax.broadcasted_iota(jnp.int32, (64, 128), 1) < 64
    for j in range(4):
        s = slice(128 * j, 128 * j + 128)
        a = t_mm(kn[:, s], vn[:, s])
        ss[64 * j : 64 * j + 64, :] = jnp.where(left, a[:64], a[64:])
        a = t_mm(qkv[:, s], g[:, s])
        ss[256 + 64 * j : 320 + 64 * j, :] = jnp.where(left, a[:64], a[64:])
    low2 = low_rows((8, 128))

    @pl.loop(0, 64)
    def _(i):
        v = ss[pl.ds(pl.multiple_of(i * 8, 8), 8), :]
        hi = v.astype(BF).astype(F32)
        lo = v - hi
        send[2 * i, :, W:] = jnp.where(low2, hi, pltpu.roll(lo, 4, 0)).astype(BF)
        send[2 * i + 1, :, W:] = jnp.where(low2, pltpu.roll(hi, 4, 0), lo).astype(BF)


def query_kernel(pos, x_ref, g_ref, keep, send):
    x, g = x_ref[...], g_ref[...]
    for core, dst in ((pos[3], keep), (1 - pos[3], send)):
        xk = mm(x, pick(core)).astype(BF)
        dst[...] = (t_mm(xk, g) * (1.0 / TOTAL)).astype(dst.dtype)


def pick(core):
    r = lax.broadcasted_iota(jnp.int32, (W, PTS), 0)
    k = lax.broadcasted_iota(jnp.int32, (W, PTS), 1)
    return jnp.where(r == 4 * (k % CHIPS) + 2 * core + k // CHIPS, 1.0, 0.0).astype(BF)


def deal_query_kernel(keep, near, out, rows):
    tot = keep[...] + near[...].astype(F32)
    for j in range(2):
        for q in range(4):
            rows[pl.ds(4 * j + q, CHIPS, stride=8), :] = tot[CHIPS * j : CHIPS * j + CHIPS, 128 * q : 128 * q + 128]
    out[...] = rows[...].reshape(CHIPS, 8, 128).astype(BF)


def spread_kernel(recv, query, out):
    v = jnp.sum(recv[...].astype(F32), axis=0)
    v = (v + pltpu.roll(v, 4, 0)) * (1.0 / TOTAL)
    hi = v.astype(BF).astype(F32)
    v = jnp.where(low_rows((8, 128)), hi, v - hi).astype(BF)
    out[:, :, 0:128] = jnp.broadcast_to(v[None], (CHIPS, 8, 128))
    out[:, :, 128:256] = query[...]


def expert_kernel(
    pos, recv, wi, wiy, win, wo, woy, won, b_ref, bp_ref,
    send, x_out, c_out, hid_out, gpre_out, keep_i, send_i, keep_o, send_o, x_s, c_s, hid, gpre, o_s, k_s
):
    n = pos[3]
    mine = pl.ds(pl.multiple_of(n * 256, 256), 256)
    other = pl.ds(pl.multiple_of(256 - n * 256, 256), 256)
    low = low_rows((8, W))

    @pl.loop(0, 32)
    def _(i):
        xs, cs = [], []
        for h in range(2):
            a = recv[4 * i + 2 * h].astype(F32)
            b = recv[4 * i + 2 * h + 1].astype(F32)
            xs.append(jnp.where(low, a, pltpu.roll(b, 4, 0)))
            cs.append(jnp.where(low, pltpu.roll(a, 4, 0), b))
        rows = pl.ds(pl.multiple_of(i * 16, 16), 16)
        x_s[rows, :] = jnp.concatenate(xs, axis=0).astype(BF)
        c_s[rows, :] = jnp.concatenate(cs, axis=0).astype(BF)

    def act(pre, gh, cols):
        sq = pre * pre
        t = jnp.tanh(GS * (pre + GC * pre * sq))
        up = 0.5 * (1.0 + t)
        hid[:, cols] = (pre * up).astype(BF)
        slope = up + 0.5 * pre * (1.0 - t * t) * GS * (1.0 + 3.0 * GC * sq)
        gpre[:, cols] = (gh * slope).astype(BF)

    @pl.loop(0, 4)
    def _(i):
        cols = pl.ds(pl.multiple_of(i * 256, 256), 256)
        pre = mm(x_s[...], wi[:, cols]) + b_ref[:, cols]
        gh = mm_t(c_s[...], wo[cols, :])
        act(pre, gh, cols)

    @pl.loop(0, 4)
    def _(i):
        cols = pl.ds(pl.multiple_of(i * 256, 256), 256)
        pre = mm(x_s[:, mine], wiy[:, cols]) + mm(x_s[:, other], win[:, cols]) + bp_ref[:, cols]
        gh = mm_t(c_s[:, mine], woy[cols, :]) + mm_t(c_s[:, other], won[cols, :])
        act(pre, gh, pl.ds(pl.multiple_of(HALF + i * 256, 256), 256))

    for yr, kr, part in ((woy, wiy, mine), (won, win, other)):
        o_s[:, part] = mm(hid[:, :HALF], wo[:, part]) + mm(hid[:, HALF:], yr[...])
        k_s[:, part] = mm_t(gpre[:, :HALF], wi[part, :]) + mm_t(gpre[:, HALF:], kr[...])

    @pl.loop(0, 64)
    def _(i):
        rows = pl.ds(pl.multiple_of(i * 8, 8), 8)
        o, k = o_s[rows, :], k_s[rows, :]
        send[2 * i, :, :] = jnp.where(low, o, pltpu.roll(k, 4, 0)).astype(BF)
        send[2 * i + 1, :, :] = jnp.where(low, pltpu.roll(o, 4, 0), k).astype(BF)

    x_out[...] = x_s[...]
    c_out[...] = c_s[...]
    hid_out[...] = hid[:, :HALF]
    gpre_out[...] = gpre[:, :HALF]
    grad_part(n, HALF, x_s, c_s, hid, gpre, keep_i, send_i, keep_o, send_o)


def grad_part(n, start, x_s, c_s, hid, gpre, keep_i, send_i, keep_o, send_o):
    mine = pl.ds(pl.multiple_of(n * 256, 256), 256)
    other = pl.ds(pl.multiple_of(256 - n * 256, 256), 256)

    @pl.loop(0, 2)
    def _(i):
        cols = pl.ds(pl.multiple_of(i * 512, 512), 512)
        src = pl.ds(pl.multiple_of(start + i * 512, 512), 512)
        g = gpre[:, src]
        keep_i[0:256, cols] = t_mm(x_s[:, mine], g) * SHARE
        send_i[0:256, cols] = (t_mm(x_s[:, other], g) * SHARE).astype(BF)
        bias = jnp.sum(g.astype(F32), axis=0, keepdims=True) * SHARE
        keep_i[256:272, cols] = jnp.broadcast_to(bias, (16, 512))
        send_i[256:272, cols] = jnp.broadcast_to(bias, (16, 512)).astype(BF)
        h = hid[:, src]
        keep_o[cols, :] = t_mm(h, c_s[:, mine]) * SHARE
        send_o[cols, :] = (t_mm(h, c_s[:, other]) * SHARE).astype(BF)


def weight_kernel(pos, x_s, c_s, hid, gpre, keep_i, send_i, keep_o, send_o):
    grad_part(pos[3], 0, x_s, c_s, hid, gpre, keep_i, send_i, keep_o, send_o)


def merge_kernel(keep_i, got_i, keep_o, got_o, away_i, away_o):
    away_i[...] = (keep_i[...] + got_i[...].astype(F32)).astype(BF)
    away_o[...] = (keep_o[...] + got_o[...].astype(F32)).astype(BF)


def end_kernel(pos, keep_i, got_i, far_i, keep_o, got_o, far_o, grad_i, bias, grad_o, row):
    def total(a, b, c, rows):
        return a[rows, :] + b[rows, :].astype(F32) + c[rows, :].astype(F32)

    grad_i[...] = total(keep_i, got_i, far_i, slice(0, 256))
    row[...] = total(keep_i, got_i, far_i, slice(256, 272))[0:8, :]
    bias[...] = row[0:1, pl.ds(pl.multiple_of(pos[3] * 512, 512), 512)]
    grad_o[...] = total(keep_o, got_o, far_o, slice(0, HALF))


def attn_kernel(pos, rs, rs2, qkv_ref, g_ref, x_ref, c_ref, mix_ref, gq, keep, send, query, ss):
    low = low_rows((8, 128))

    @pl.loop(0, 32)
    def _(i):
        tiles = []
        for h in range(2):
            pair = []
            for k in range(2):
                d = 4 * i + 2 * h + k
                v = rs[d, :, 0:128].astype(F32) + rs2[d].astype(F32)
                pair.append(v + pltpu.roll(v, 4, 0))
            tiles.append(jnp.where(low, pair[0], pair[1]))
        ss[pl.ds(pl.multiple_of(i * 16, 16), 16), :] = jnp.concatenate(tiles, axis=0).astype(BF)

    ones = head_ones()
    qkv, g = qkv_ref[...], g_ref[...]
    ku, ks = normalize(qkv[:, W : 2 * W], ones)
    vu, vs = normalize(qkv[:, 2 * W :], ones)
    kn, vn = ku.astype(BF), vu.astype(BF)
    left = lax.broadcasted_iota(jnp.int32, (64, 128), 1) < 64
    total = jnp.sum(rs[:, :, 128:256].astype(F32), axis=0)
    total_hi = total.astype(BF)
    total_lo = (total - total_hi.astype(F32)).astype(BF)
    block = lax.broadcasted_iota(jnp.int32, (8, 128), 0) % 4

    def diag(p):
        z = jnp.zeros_like(p)
        return jnp.concatenate([jnp.where(left, p, z), jnp.where(left, z, p)], axis=0)

    gk, gv = [], []
    rows = jnp.zeros((8, 128), F32)
    for j in range(4):
        s = slice(128 * j, 128 * j + 128)
        sm = diag(ss[64 * j : 64 * j + 64, :].astype(F32)).astype(BF)
        gs = diag(ss[256 + 64 * j : 320 + 64 * j, :].astype(F32)).astype(BF)
        mix_ref[:, s] = mm(qkv[:, s], sm).astype(BF)
        gq[:, s] = mm_t(g[:, s], sm).astype(BF)
        rows = jnp.where(block == j, mm_t(total_hi, sm) + mm_t(total_lo, sm), rows)
        gk.append(mm_t(vn[:, s], gs))
        gv.append(mm(kn[:, s], gs))
    query[...] = rows

    def back(gr, u, sc):
        return ((gr - head_mean(gr, ones) - u * head_mean(gr * u, ones)) / sc).astype(BF)

    gq[:, W : 2 * W] = back(jnp.concatenate(gk, axis=1), ku, ks)
    gq[:, 2 * W :] = back(jnp.concatenate(gv, axis=1), vu, vs)
    x, c, mixed = x_ref[...], c_ref[...], mix_ref[...]
    for core, dst in ((pos[3], keep), (1 - pos[3], send)):
        sel = pick(core)
        xk, mk = mm(x, sel).astype(BF), mm(mixed, sel).astype(BF)
        for q in range(2):
            dst[:, W * q : W * q + W] = (t_mm(xk, gq[:, W * q + W : W * q + 2 * W]) * (1.0 / TOTAL)).astype(dst.dtype)
        dst[:, 2 * W :] = (t_mm(mk, c) * (1.0 / TOTAL)).astype(dst.dtype)


def base_kernel(x, c, mixed, gq, wq, wo, base_o, base_k):
    base_o[...] = x[...].astype(F32) + mm(mixed[...], wo[...])
    base_k[...] = c[...].astype(F32) + mm_t(gq[...], wq[...])


def join_kernel(ret, keep, near, out, rows):
    out[:, :, 0:W] = ret[...]
    size = 8 * CHIPS
    for t in range(3):
        for j in range(2):
            part = slice(CHIPS * j, CHIPS * j + CHIPS)
            for q in range(4):
                cols = slice(384 * q + 128 * t, 384 * q + 128 * t + 128)
                v = keep[part, cols] + near[part, cols].astype(F32)
                rows[pl.ds(size * t + 4 * j + q, CHIPS, stride=8), :] = v
        v = rows[size * t : size * t + size, :].reshape(CHIPS, 8, 128)
        out[:, :, W + 128 * t : W + 128 * t + 128] = v.astype(BF)


def final_kernel(slots, ret, base_o, base_k, query, lo, gf, att):
    low = low_rows((8, W))

    @pl.loop(0, 16)
    def _(i):
        os, ks = [], []
        for h in range(2):
            a = ret[slots[4 * i + 2 * h], :, 0:W].astype(F32)
            b = ret[slots[4 * i + 2 * h + 1], :, 0:W].astype(F32)
            os.append(jnp.where(low, a, pltpu.roll(b, 4, 0)))
            ks.append(jnp.where(low, pltpu.roll(a, 4, 0), b))
        rows = pl.ds(pl.multiple_of(i * 16, 16), 16)
        lo[rows, :] = (base_o[rows, :] + jnp.concatenate(os, axis=0)).astype(BF)
        gf[rows, :] = (base_k[rows, :] + jnp.concatenate(ks, axis=0)).astype(BF)

    v = jnp.sum(ret[:, :, W:].astype(F32), axis=0)
    q = query[...]
    for j in range(2):
        for b in range(4):
            r = slice(4 * j + b, 4 * j + b + 1)
            att[j : j + 1, 128 * b : 128 * b + 128] = q[r]
            att[j : j + 1, W + 384 * b : W + 384 * b + 384] = v[r]


def layer(x, ids, wq, wo_att, wi, bi, wo, c):
    n = lax.axis_index("narrow")
    w = lax.axis_index("wide")
    pos = jnp.stack([w // 16, w // 4 % 4, w % 4, n]).astype(jnp.int32)
    pair = [(i, i ^ 1) for i in range(CHIPS)]
    swap = [(0, 1), (1, 0)]

    def across(v):
        return lax.ppermute(v, "wide", pair)

    def beside(v):
        return lax.ppermute(v, "narrow", swap)

    def deal(v):
        return lax.all_to_all(v, "wide", split_axis=0, concat_axis=0, tiled=True)

    def run(body, us, outs, args, scratch=(), smem_in=(), smem_out=(), specs=None, mib=24):
        return call(
            body, outs, scratch, smem_in=smem_in, n_in=len(args), smem_out=smem_out, cost=cost(us),
            specs=specs, mib=mib,
        )(*args)

    wiy = across(lax.dynamic_slice_in_dim(wi, n * 256, 256, 0))
    woy = across(lax.dynamic_slice_in_dim(wo, n * 256, 256, 1))
    bp = across(bi)
    win, won = beside(wiy), beside(woy)

    anywhere = pl.BlockSpec(memory_space=pltpu.HBM)
    send, slots, qkv, g = run(
        front_kernel, 5,
        [far((CHIPS, 8, 640), BF), sds((NB,), jnp.int32), far((PTS, 3 * W), BF), far((PTS, W), BF)],
        (ids, in_hbm(x), in_hbm(c), in_hbm(wq), in_hbm(wo_att)),
        [
            pltpu.SMEM((NB,), jnp.int32), pltpu.VMEM((W, 128), F32), pltpu.VMEM((W, 3 * W), BF),
            pltpu.VMEM((W, W), BF), pltpu.SemaphoreType.DMA((2,)),
        ],
        (0,), (1,), specs={3: anywhere, 4: anywhere}, mib=48,
    )
    recv = deal(send)
    keep_q, away_q = run(query_kernel, 2, [sds((PTS, W), F32), sds((PTS, W), BF)], (pos, x, g), (), (0,))
    (dealt_q,) = run(
        deal_query_kernel, 1, [sds((CHIPS, 8, 128), BF)], (keep_q, beside(away_q)),
        [pltpu.VMEM((8 * CHIPS, 128), F32)],
    )
    (spread,) = run(
        spread_kernel, 1, [far((CHIPS, 8, 256), BF)], (recv, dealt_q),
        specs={0: pl.BlockSpec((CHIPS, 8, 128), lambda i: (0, 0, 4))},
    )
    rs = deal(spread)
    grads = [((272, HALF), F32), ((272, HALF), BF), ((HALF, 256), F32), ((HALF, 256), BF)]
    ret, x_s, c_s, hid, gpre, keep_i, send_i, keep_o, send_o = run(
        expert_kernel, 12,
        [far((CHIPS, 8, W), BF), far((W, W), BF), far((W, W), BF), far((W, HALF), BF), far((W, HALF), BF)]
        + [far(*v) for v in grads],
        (pos, recv, *map(in_hbm, (wi, wiy, win, wo, woy, won)), bi.reshape(1, HALF), bp.reshape(1, HALF)),
        [pltpu.VMEM((W, W), BF)] * 2 + [pltpu.VMEM((W, 2 * HALF), BF)] * 2 + [pltpu.VMEM((W, W), F32)] * 2, (0,),
        specs={1: pl.BlockSpec((CHIPS, 8, W), lambda i: (0, 0, 0))}, mib=48,
    )
    got_i, got_o = beside(send_i), beside(send_o)
    rs2 = beside(rs)
    mixed, gq, keep, away, query = run(
        attn_kernel, 7,
        [sds((PTS, W), BF), sds((PTS, 3 * W), BF), sds((PTS, 3 * W), F32), sds((PTS, 3 * W), BF), sds((8, 128), F32)],
        (pos, rs, rs2, qkv, g, x, c), [pltpu.VMEM((W, 128), BF)], (0,),
        specs={2: pl.BlockSpec((CHIPS, 8, 128), lambda i: (0, 0, 0))},
    )
    near = beside(away)
    base_o, base_k = run(base_kernel, 1, [far((PTS, W), F32), far((PTS, W), F32)], (x, c, mixed, gq, wq, wo_att))
    away_i, away_o = run(merge_kernel, 1, [sds((272, HALF), BF), sds((HALF, 256), BF)], (keep_i, got_i, keep_o, got_o))
    far_i, far_o = across(away_i), across(away_o)
    (joined,) = run(join_kernel, 2, [far((CHIPS, 8, 896), BF)], (ret, keep, near), [pltpu.VMEM((24 * CHIPS, 128), F32)])
    back = deal(joined)
    keep_i, send_i, keep_o, send_o = run(
        weight_kernel, 5, [sds(*v) for v in grads], (pos, x_s, c_s, hid, gpre), (), (0,)
    )
    got_i, got_o = beside(send_i), beside(send_o)
    grad_in, grad_b, grad_out = run(
        end_kernel, 3, [sds((256, HALF), F32), sds((1, 512), F32), sds((HALF, 256), F32)],
        (pos, keep_i, got_i, far_i, keep_o, got_o, far_o), [pltpu.VMEM((8, HALF), F32)], (0,),
    )
    layer_out, grad_feats, att = run(
        final_kernel, 3, [sds((PTS, W), BF), sds((PTS, W), BF), sds((2, 4 * W), F32)],
        (slots, back, in_hbm(base_o), in_hbm(base_k), query), (), (0,),
    )
    return (layer_out, grad_feats, att, grad_in, grad_out, grad_b.reshape(512))


def solution(mesh):
    placed = (
        P(("wide", "narrow"), None),
        P(("wide", "narrow")),
        P(),
        P(),
        P(None, "wide"),
        P("wide"),
        P("wide", None),
        P(("wide", "narrow"), None),
    )
    return jax.shard_map(
        layer,
        mesh=mesh,
        in_specs=placed,
        out_specs=(
            P(("wide", "narrow"), None),
            P(("wide", "narrow"), None),
            P(("wide", "narrow"), None),
            P("narrow", "wide"),
            P("wide", "narrow"),
            P(("wide", "narrow")),
        ),
        check_vma=False,
    )
```

```python
import jax
import jax.numpy as jnp
from jax import lax
from jax.experimental import pallas as pl
from jax.experimental.pallas import tpu as pltpu
from jax.sharding import PartitionSpec as P

F32 = jnp.float32
BF = jnp.bfloat16
EPS = 1e-05
GS = 0.7978845608
GC = 0.044715
W = 512
PTS = 256
NB = 64
CHIPS = 128
TOTAL = 65536.0
SHARE = 64.0 / 65536.0
HALF = 1024
VM = pl.BlockSpec(memory_space=pltpu.VMEM)
SM = pl.BlockSpec(memory_space=pltpu.SMEM)


def mm(a, b):
    return jnp.dot(a, b, preferred_element_type=F32)


def mm_t(a, b):
    return lax.dot_general(a, b, (((1,), (1,)), ((), ())), preferred_element_type=F32)


def t_mm(a, b):
    return lax.dot_general(a, b, (((0,), (0,)), ((), ())), preferred_element_type=F32)


def head_ones():
    r = lax.broadcasted_iota(jnp.int32, (W, W), 0) // 64
    c = lax.broadcasted_iota(jnp.int32, (W, W), 1) // 64
    return jnp.where(r == c, 1.0 / 64.0, 0.0).astype(BF)


def head_mean(v, ones):
    hi = v.astype(BF)
    lo = (v - hi.astype(F32)).astype(BF)
    return mm(hi, ones) + mm(lo, ones)


def normalize(raw, ones):
    cen = raw.astype(F32) - mm(raw, ones)
    scale = jnp.sqrt(head_mean(cen * cen, ones) + EPS)
    return cen / scale, scale


def low_rows(shape):
    return lax.broadcasted_iota(jnp.int32, shape, 0) < 4


def call(body, outs, scratch=(), smem_in=(), n_in=0, smem_out=(), cost=None, specs=None, mib=24, out_hbm=False):
    return pl.pallas_call(
        body,
        out_shape=outs,
        grid=(1,) if specs else (),
        in_specs=[(specs or {}).get(i, SM if i in smem_in else VM) for i in range(n_in)],
        out_specs=[
            pl.BlockSpec(memory_space=pltpu.HBM) if out_hbm else SM if i in smem_out else VM for i in range(len(outs))
        ],
        scratch_shapes=list(scratch),
        cost_estimate=cost,
        compiler_params=pltpu.CompilerParams(vmem_limit_bytes=mib * 1024 * 1024),
    )


def cost(us):
    return pl.CostEstimate(flops=int(us * 1e9), bytes_accessed=int(us * 1e6), transcendentals=0)


def sds(shape, dtype):
    return jax.ShapeDtypeStruct(shape, dtype)


def far(shape, dtype):
    return pltpu.HBM(shape, dtype)


def in_hbm(v):
    return pltpu.with_memory_space_constraint(v, pltpu.HBM)


def front_kernel(ids, x_ref, c_ref, wq_hbm, wo_hbm, send, slots, qkv_ref, g_ref, cnt, ss, wq_ref, wo_ref, sems):
    loads = [
        pltpu.make_async_copy(wq_hbm, wq_ref, sems.at[0]),
        pltpu.make_async_copy(wo_hbm, wo_ref, sems.at[1]),
    ]
    for load in loads:
        load.start()

    @pl.loop(0, NB)
    def _(i):
        cnt[i] = 0

    @pl.loop(0, NB)
    def _(b):
        r = ids[b]
        k = cnt[r]
        cnt[r] = k + 1
        slots[b] = 2 * r + k

    send[:, :, 0:W] = jnp.zeros((CHIPS, 8, W), BF)
    low = low_rows((8, W))

    @pl.loop(0, 16)
    def _(i):
        x = x_ref[pl.ds(pl.multiple_of(i * 16, 16), 16), :].astype(F32)
        c = c_ref[pl.ds(pl.multiple_of(i * 16, 16), 16), :].astype(F32)
        for h in range(2):
            xa, ca = x[8 * h : 8 * h + 8], c[8 * h : 8 * h + 8]
            xr, cr = pltpu.roll(xa, 4, 0), pltpu.roll(ca, 4, 0)
            send[slots[4 * i + 2 * h], :, 0:W] = jnp.where(low, xa, cr).astype(BF)
            send[slots[4 * i + 2 * h + 1], :, 0:W] = jnp.where(low, xr, ca).astype(BF)

    for load in loads:
        load.wait()
    ones = head_ones()
    qkv = mm(x_ref[...], wq_ref[...]).astype(BF)
    qkv_ref[...] = qkv
    g = mm_t(c_ref[...], wo_ref[...]).astype(BF)
    g_ref[...] = g
    kn = normalize(qkv[:, W : 2 * W], ones)[0].astype(BF)
    vn = normalize(qkv[:, 2 * W :], ones)[0].astype(BF)
    left = lax.broadcasted_iota(jnp.int32, (64, 128), 1) < 64
    for j in range(4):
        s = slice(128 * j, 128 * j + 128)
        a = t_mm(kn[:, s], vn[:, s])
        ss[64 * j : 64 * j + 64, :] = jnp.where(left, a[:64], a[64:])
        a = t_mm(qkv[:, s], g[:, s])
        ss[256 + 64 * j : 320 + 64 * j, :] = jnp.where(left, a[:64], a[64:])
    low2 = low_rows((8, 128))

    @pl.loop(0, 64)
    def _(i):
        v = ss[pl.ds(pl.multiple_of(i * 8, 8), 8), :]
        hi = v.astype(BF).astype(F32)
        lo = v - hi
        send[2 * i, :, W:] = jnp.where(low2, hi, pltpu.roll(lo, 4, 0)).astype(BF)
        send[2 * i + 1, :, W:] = jnp.where(low2, pltpu.roll(hi, 4, 0), lo).astype(BF)


def query_kernel(pos, x_ref, g_ref, keep, send):
    x, g = x_ref[...], g_ref[...]
    for core, dst in ((pos[3], keep), (1 - pos[3], send)):
        xk = mm(x, pick(core)).astype(BF)
        dst[...] = (t_mm(xk, g) * (1.0 / TOTAL)).astype(dst.dtype)


def pick(core):
    r = lax.broadcasted_iota(jnp.int32, (W, PTS), 0)
    k = lax.broadcasted_iota(jnp.int32, (W, PTS), 1)
    return jnp.where(r == 4 * (k % CHIPS) + 2 * core + k // CHIPS, 1.0, 0.0).astype(BF)


def deal_query_kernel(keep, near, out, rows):
    tot = keep[...] + near[...].astype(F32)
    for j in range(2):
        for q in range(4):
            rows[pl.ds(4 * j + q, CHIPS, stride=8), :] = tot[CHIPS * j : CHIPS * j + CHIPS, 128 * q : 128 * q + 128]
    out[...] = rows[...].reshape(CHIPS, 8, 128).astype(BF)


def spread_kernel(recv, query, out):
    v = jnp.sum(recv[...].astype(F32), axis=0)
    v = (v + pltpu.roll(v, 4, 0)) * (1.0 / TOTAL)
    hi = v.astype(BF).astype(F32)
    v = jnp.where(low_rows((8, 128)), hi, v - hi).astype(BF)
    out[:, :, 0:128] = jnp.broadcast_to(v[None], (CHIPS, 8, 128))
    out[:, :, 128:256] = query[...]


def slice_kernel(axis, src, out, sem):
    part = pl.ds(pl.multiple_of(lax.axis_index("narrow") * 256, 256), 256)
    load = pltpu.make_async_copy(src.at[part, :] if axis == 0 else src.at[:, part], out, sem)
    load.start()
    load.wait()


def act(pre, gh, cols, hid, gpre):
    sq = pre * pre
    t = jnp.tanh(GS * (pre + GC * pre * sq))
    up = 0.5 * (1.0 + t)
    hid[:, cols] = (pre * up).astype(BF)
    slope = up + 0.5 * pre * (1.0 - t * t) * GS * (1.0 + 3.0 * GC * sq)
    gpre[:, cols] = (gh * slope).astype(BF)


def expert_kernel(
    pos, recv, wi_h, wiy_h, win_h, wo_h, woy_h, won_h, b_ref, bp_ref,
    send_h, x_h, c_h, hid_h, gpre_h, ki_h, si_h, ko_h, so_h,
    x_s, c_s, hid, gpre, hid_p, gpre_p, o_s, k_s, send, ki, si, ko, so, wi, wiy, win, wo, woy, won, in_sems, out_sems,
):
    n = pos[3]
    mine = pl.ds(pl.multiple_of(n * 256, 256), 256)
    other = pl.ds(pl.multiple_of(256 - n * 256, 256), 256)
    low = low_rows((8, W))
    loads = [
        pltpu.make_async_copy(a, b, in_sems.at[k])
        for k, (a, b) in enumerate(
            ((wi_h, wi), (wo_h, wo), (wiy_h, wiy), (woy_h, woy), (win_h, win), (won_h, won))
        )
    ]
    stores = [
        pltpu.make_async_copy(a, b, out_sems.at[k])
        for k, (a, b) in enumerate(
            (
                (x_s, x_h), (c_s, c_h), (hid, hid_h), (gpre, gpre_h),
                (ki, ki_h), (si, si_h), (ko, ko_h), (so, so_h), (send, send_h),
            )
        )
    ]
    for load in loads:
        load.start()

    @pl.loop(0, 32)
    def _(i):
        xs, cs = [], []
        for h in range(2):
            a = recv[4 * i + 2 * h].astype(F32)
            b = recv[4 * i + 2 * h + 1].astype(F32)
            xs.append(jnp.where(low, a, pltpu.roll(b, 4, 0)))
            cs.append(jnp.where(low, pltpu.roll(a, 4, 0), b))
        rows = pl.ds(pl.multiple_of(i * 16, 16), 16)
        x_s[rows, :] = jnp.concatenate(xs, axis=0).astype(BF)
        c_s[rows, :] = jnp.concatenate(cs, axis=0).astype(BF)

    stores[0].start()
    stores[1].start()
    loads[0].wait()
    loads[1].wait()

    @pl.loop(0, 4)
    def _(i):
        cols = pl.ds(pl.multiple_of(i * 256, 256), 256)
        pre = mm(x_s[...], wi[:, cols]) + b_ref[:, cols]
        gh = mm_t(c_s[...], wo[cols, :])
        act(pre, gh, cols, hid, gpre)

    stores[2].start()
    stores[3].start()
    for load in loads[2:]:
        load.wait()

    @pl.loop(0, 4)
    def _(i):
        cols = pl.ds(pl.multiple_of(i * 256, 256), 256)
        pre = mm(x_s[:, mine], wiy[:, cols]) + mm(x_s[:, other], win[:, cols]) + bp_ref[:, cols]
        gh = mm_t(c_s[:, mine], woy[cols, :]) + mm_t(c_s[:, other], won[cols, :])
        act(pre, gh, cols, hid_p, gpre_p)

    grad_part(n, x_s, c_s, hid_p, gpre_p, ki, si, ko, so)
    for store in stores[4:8]:
        store.start()

    for yr, kr, part in ((woy, wiy, mine), (won, win, other)):
        o_s[:, part] = mm(hid[...], wo[:, part]) + mm(hid_p[...], yr[...])
        k_s[:, part] = mm_t(gpre[...], wi[part, :]) + mm_t(gpre_p[...], kr[...])

    @pl.loop(0, 64)
    def _(i):
        rows = pl.ds(pl.multiple_of(i * 8, 8), 8)
        o, k = o_s[rows, :], k_s[rows, :]
        send[2 * i, :, :] = jnp.where(low, o, pltpu.roll(k, 4, 0)).astype(BF)
        send[2 * i + 1, :, :] = jnp.where(low, pltpu.roll(o, 4, 0), k).astype(BF)

    stores[8].start()
    for store in stores:
        store.wait()


def grad_part(n, x_s, c_s, hid, gpre, keep_i, send_i, keep_o, send_o):
    mine = pl.ds(pl.multiple_of(n * 256, 256), 256)
    other = pl.ds(pl.multiple_of(256 - n * 256, 256), 256)

    @pl.loop(0, 2)
    def _(i):
        cols = pl.ds(pl.multiple_of(i * 512, 512), 512)
        g = gpre[:, cols]
        keep_i[0:256, cols] = t_mm(x_s[:, mine], g) * SHARE
        send_i[0:256, cols] = (t_mm(x_s[:, other], g) * SHARE).astype(BF)
        bias = jnp.sum(g.astype(F32), axis=0, keepdims=True) * SHARE
        keep_i[256:272, cols] = jnp.broadcast_to(bias, (16, 512))
        send_i[256:272, cols] = jnp.broadcast_to(bias, (16, 512)).astype(BF)
        h = hid[:, cols]
        keep_o[cols, :] = t_mm(h, c_s[:, mine]) * SHARE
        send_o[cols, :] = (t_mm(h, c_s[:, other]) * SHARE).astype(BF)


def weight_kernel(pos, x_s, c_s, hid, gpre, keep_i, send_i, keep_o, send_o):
    grad_part(pos[3], x_s, c_s, hid, gpre, keep_i, send_i, keep_o, send_o)


def merge_kernel(keep_i, got_i, keep_o, got_o, away_i, away_o):
    away_i[...] = (keep_i[...] + got_i[...].astype(F32)).astype(BF)
    away_o[...] = (keep_o[...] + got_o[...].astype(F32)).astype(BF)


def end_kernel(pos, keep_i, got_i, far_i, keep_o, got_o, far_o, grad_i, bias, grad_o, row):
    def total(a, b, c, rows):
        return a[rows, :] + b[rows, :].astype(F32) + c[rows, :].astype(F32)

    grad_i[...] = total(keep_i, got_i, far_i, slice(0, 256))
    row[...] = total(keep_i, got_i, far_i, slice(256, 272))[0:8, :]
    bias[...] = row[0:1, pl.ds(pl.multiple_of(pos[3] * 512, 512), 512)]
    grad_o[...] = total(keep_o, got_o, far_o, slice(0, HALF))


def attn_kernel(pos, rs, rs2, qkv_ref, g_ref, x_ref, c_ref, mix_ref, gq, keep, send, query, ss):
    low = low_rows((8, 128))

    @pl.loop(0, 32)
    def _(i):
        tiles = []
        for h in range(2):
            pair = []
            for k in range(2):
                d = 4 * i + 2 * h + k
                v = rs[d, :, 0:128].astype(F32) + rs2[d].astype(F32)
                pair.append(v + pltpu.roll(v, 4, 0))
            tiles.append(jnp.where(low, pair[0], pair[1]))
        ss[pl.ds(pl.multiple_of(i * 16, 16), 16), :] = jnp.concatenate(tiles, axis=0).astype(BF)

    ones = head_ones()
    qkv, g = qkv_ref[...], g_ref[...]
    ku, ks = normalize(qkv[:, W : 2 * W], ones)
    vu, vs = normalize(qkv[:, 2 * W :], ones)
    kn, vn = ku.astype(BF), vu.astype(BF)
    left = lax.broadcasted_iota(jnp.int32, (64, 128), 1) < 64
    total = jnp.sum(rs[:, :, 128:256].astype(F32), axis=0)
    total_hi = total.astype(BF)
    total_lo = (total - total_hi.astype(F32)).astype(BF)
    block = lax.broadcasted_iota(jnp.int32, (8, 128), 0) % 4

    def diag(p):
        z = jnp.zeros_like(p)
        return jnp.concatenate([jnp.where(left, p, z), jnp.where(left, z, p)], axis=0)

    gk, gv = [], []
    rows = jnp.zeros((8, 128), F32)
    for j in range(4):
        s = slice(128 * j, 128 * j + 128)
        sm = diag(ss[64 * j : 64 * j + 64, :].astype(F32)).astype(BF)
        gs = diag(ss[256 + 64 * j : 320 + 64 * j, :].astype(F32)).astype(BF)
        mix_ref[:, s] = mm(qkv[:, s], sm).astype(BF)
        gq[:, s] = mm_t(g[:, s], sm).astype(BF)
        rows = jnp.where(block == j, mm_t(total_hi, sm) + mm_t(total_lo, sm), rows)
        gk.append(mm_t(vn[:, s], gs))
        gv.append(mm(kn[:, s], gs))
    query[...] = rows

    def back(gr, u, sc):
        return ((gr - head_mean(gr, ones) - u * head_mean(gr * u, ones)) / sc).astype(BF)

    gq[:, W : 2 * W] = back(jnp.concatenate(gk, axis=1), ku, ks)
    gq[:, 2 * W :] = back(jnp.concatenate(gv, axis=1), vu, vs)
    x, c, mixed = x_ref[...], c_ref[...], mix_ref[...]
    for core, dst in ((pos[3], keep), (1 - pos[3], send)):
        sel = pick(core)
        xk, mk = mm(x, sel).astype(BF), mm(mixed, sel).astype(BF)
        for q in range(2):
            dst[:, W * q : W * q + W] = (t_mm(xk, gq[:, W * q + W : W * q + 2 * W]) * (1.0 / TOTAL)).astype(dst.dtype)
        dst[:, 2 * W :] = (t_mm(mk, c) * (1.0 / TOTAL)).astype(dst.dtype)


def base_kernel(x, c, mixed, gq, wq, wo, base_o, base_k):
    base_o[...] = x[...].astype(F32) + mm(mixed[...], wo[...])
    base_k[...] = c[...].astype(F32) + mm_t(gq[...], wq[...])


def join_kernel(ret, keep, near, out, rows):
    out[:, :, 0:W] = ret[...]
    size = 8 * CHIPS
    for t in range(3):
        for j in range(2):
            part = slice(CHIPS * j, CHIPS * j + CHIPS)
            for q in range(4):
                cols = slice(384 * q + 128 * t, 384 * q + 128 * t + 128)
                v = keep[part, cols] + near[part, cols].astype(F32)
                rows[pl.ds(size * t + 4 * j + q, CHIPS, stride=8), :] = v
        v = rows[size * t : size * t + size, :].reshape(CHIPS, 8, 128)
        out[:, :, W + 128 * t : W + 128 * t + 128] = v.astype(BF)


def final_kernel(slots, ret, base_o, base_k, query, lo, gf, att):
    low = low_rows((8, W))

    @pl.loop(0, 16)
    def _(i):
        os, ks = [], []
        for h in range(2):
            a = ret[slots[4 * i + 2 * h], :, 0:W].astype(F32)
            b = ret[slots[4 * i + 2 * h + 1], :, 0:W].astype(F32)
            os.append(jnp.where(low, a, pltpu.roll(b, 4, 0)))
            ks.append(jnp.where(low, pltpu.roll(a, 4, 0), b))
        rows = pl.ds(pl.multiple_of(i * 16, 16), 16)
        lo[rows, :] = (base_o[rows, :] + jnp.concatenate(os, axis=0)).astype(BF)
        gf[rows, :] = (base_k[rows, :] + jnp.concatenate(ks, axis=0)).astype(BF)

    v = jnp.sum(ret[:, :, W:].astype(F32), axis=0)
    q = query[...]
    for j in range(2):
        for b in range(4):
            r = slice(4 * j + b, 4 * j + b + 1)
            att[j : j + 1, 128 * b : 128 * b + 128] = q[r]
            att[j : j + 1, W + 384 * b : W + 384 * b + 384] = v[r]


def layer(x, ids, wq, wo_att, wi, bi, wo, c):
    n = lax.axis_index("narrow")
    w = lax.axis_index("wide")
    pos = jnp.stack([w // 16, w // 4 % 4, w % 4, n]).astype(jnp.int32)
    pair = [(i, i ^ 1) for i in range(CHIPS)]
    swap = [(0, 1), (1, 0)]

    def across(v):
        return lax.ppermute(v, "wide", pair)

    def beside(v):
        return lax.ppermute(v, "narrow", swap)

    def deal(v):
        return lax.all_to_all(v, "wide", split_axis=0, concat_axis=0, tiled=True)

    def run(body, us, outs, args, scratch=(), smem_in=(), smem_out=(), specs=None, mib=24, out_hbm=False):
        return call(
            body, outs, scratch, smem_in=smem_in, n_in=len(args), smem_out=smem_out, cost=cost(us),
            specs=specs, mib=mib, out_hbm=out_hbm,
        )(*args)

    anywhere = pl.BlockSpec(memory_space=pltpu.HBM)

    def half(v, axis):
        shape = (256, HALF) if axis == 0 else (HALF, 256)
        (out,) = run(
            lambda *refs: slice_kernel(axis, *refs), 1, [sds(shape, BF)], (in_hbm(v),),
            [pltpu.SemaphoreType.DMA], specs={0: anywhere},
        )
        return out

    wiy = across(half(wi, 0))
    woy = across(half(wo, 1))
    bp = across(bi)
    win, won = beside(wiy), beside(woy)

    send, slots, qkv, g = run(
        front_kernel, 5,
        [far((CHIPS, 8, 640), BF), sds((NB,), jnp.int32), far((PTS, 3 * W), BF), far((PTS, W), BF)],
        (in_hbm(ids), in_hbm(x), in_hbm(c), in_hbm(wq), in_hbm(wo_att)),
        [
            pltpu.SMEM((NB,), jnp.int32), pltpu.VMEM((W, 128), F32), pltpu.VMEM((W, 3 * W), BF),
            pltpu.VMEM((W, W), BF), pltpu.SemaphoreType.DMA((2,)),
        ],
        (0,), (1,), specs={3: anywhere, 4: anywhere}, mib=48,
    )
    recv = deal(send)
    keep_q, away_q = run(query_kernel, 2, [sds((PTS, W), F32), sds((PTS, W), BF)], (pos, x, g), (), (0,))
    (dealt_q,) = run(
        deal_query_kernel, 1, [sds((CHIPS, 8, 128), BF)], (keep_q, beside(away_q)),
        [pltpu.VMEM((8 * CHIPS, 128), F32)],
    )
    (spread,) = run(
        spread_kernel, 1, [far((CHIPS, 8, 256), BF)], (recv, dealt_q),
        specs={0: pl.BlockSpec((CHIPS, 8, 128), lambda i: (0, 0, 4))},
    )
    rs = deal(spread)
    grads = [((272, HALF), F32), ((272, HALF), BF), ((HALF, 256), F32), ((HALF, 256), BF)]
    ret, x_s, c_s, hid, gpre, keep_i, send_i, keep_o, send_o = run(
        expert_kernel, 12,
        [far((CHIPS, 8, W), BF), far((W, W), BF), far((W, W), BF), far((W, HALF), BF), far((W, HALF), BF)]
        + [far(*v) for v in grads],
        (pos, recv, *map(in_hbm, (wi, wiy, win, wo, woy, won)), bi.reshape(1, HALF), bp.reshape(1, HALF)),
        [pltpu.VMEM((W, W), BF)] * 2 + [pltpu.VMEM((W, HALF), BF)] * 4 + [pltpu.VMEM((W, W), F32)] * 2
        + [pltpu.VMEM((CHIPS, 8, W), BF)] + [pltpu.VMEM(*v) for v in grads]
        + [
            pltpu.VMEM(v, BF)
            for v in ((W, HALF), (256, HALF), (256, HALF), (HALF, W), (HALF, 256), (HALF, 256))
        ]
        + [pltpu.SemaphoreType.DMA((6,)), pltpu.SemaphoreType.DMA((9,))],
        (0,),
        specs={1: pl.BlockSpec((CHIPS, 8, W), lambda i: (0, 0, 0)), **{k: anywhere for k in range(2, 8)}},
        out_hbm=True, mib=48,
    )
    got_i, got_o = beside(send_i), beside(send_o)
    rs2 = beside(rs)
    mixed, gq, keep, away, query = run(
        attn_kernel, 7,
        [sds((PTS, W), BF), sds((PTS, 3 * W), BF), sds((PTS, 3 * W), F32), sds((PTS, 3 * W), BF), sds((8, 128), F32)],
        (pos, rs, rs2, qkv, g, x, c), [pltpu.VMEM((W, 128), BF)], (0,),
        specs={2: pl.BlockSpec((CHIPS, 8, 128), lambda i: (0, 0, 0))},
    )
    near = beside(away)
    base_o, base_k = run(base_kernel, 1, [far((PTS, W), F32), far((PTS, W), F32)], (x, c, mixed, gq, wq, wo_att))
    away_i, away_o = run(merge_kernel, 1, [sds((272, HALF), BF), sds((HALF, 256), BF)], (keep_i, got_i, keep_o, got_o))
    far_i, far_o = across(away_i), across(away_o)
    (joined,) = run(join_kernel, 2, [far((CHIPS, 8, 896), BF)], (ret, keep, near), [pltpu.VMEM((24 * CHIPS, 128), F32)])
    back = deal(joined)
    keep_i, send_i, keep_o, send_o = run(
        weight_kernel, 5, [sds(*v) for v in grads], (pos, x_s, c_s, hid, gpre), (), (0,)
    )
    got_i, got_o = beside(send_i), beside(send_o)
    grad_in, grad_b, grad_out = run(
        end_kernel, 3, [sds((256, HALF), F32), sds((1, 512), F32), sds((HALF, 256), F32)],
        (pos, keep_i, got_i, far_i, keep_o, got_o, far_o), [pltpu.VMEM((8, HALF), F32)], (0,),
    )
    layer_out, grad_feats, att = run(
        final_kernel, 3, [sds((PTS, W), BF), sds((PTS, W), BF), sds((2, 4 * W), F32)],
        (slots, back, in_hbm(base_o), in_hbm(base_k), query), (), (0,),
    )
    return (layer_out, grad_feats, att, grad_in, grad_out, grad_b.reshape(512))


def solution(mesh):
    placed = (
        P(("wide", "narrow"), None),
        P(("wide", "narrow")),
        P(),
        P(),
        P(None, "wide"),
        P("wide"),
        P("wide", None),
        P(("wide", "narrow"), None),
    )
    return jax.shard_map(
        layer,
        mesh=mesh,
        in_specs=placed,
        out_specs=(
            P(("wide", "narrow"), None),
            P(("wide", "narrow"), None),
            P(("wide", "narrow"), None),
            P("narrow", "wide"),
            P("wide", "narrow"),
            P(("wide", "narrow")),
        ),
        check_vma=False,
    )
```

```python
import jax
import jax.numpy as jnp
from jax import lax
from jax.experimental import pallas as pl
from jax.experimental.pallas import tpu as pltpu
from jax.sharding import PartitionSpec as P

F32 = jnp.float32
BF = jnp.bfloat16
EPS = 1e-05
GS = 0.7978845608
GC = 0.044715
W = 512
PTS = 256
NB = 64
CHIPS = 128
TOTAL = 65536.0
SHARE = 64.0 / 65536.0
HALF = 1024
VM = pl.BlockSpec(memory_space=pltpu.VMEM)
SM = pl.BlockSpec(memory_space=pltpu.SMEM)


def mm(a, b):
    return jnp.dot(a, b, preferred_element_type=F32)


def mm_t(a, b):
    return lax.dot_general(a, b, (((1,), (1,)), ((), ())), preferred_element_type=F32)


def t_mm(a, b):
    return lax.dot_general(a, b, (((0,), (0,)), ((), ())), preferred_element_type=F32)


def head_ones():
    r = lax.broadcasted_iota(jnp.int32, (W, W), 0) // 64
    c = lax.broadcasted_iota(jnp.int32, (W, W), 1) // 64
    return jnp.where(r == c, 1.0 / 64.0, 0.0).astype(BF)


def head_mean(v, ones):
    hi = v.astype(BF)
    lo = (v - hi.astype(F32)).astype(BF)
    return mm(hi, ones) + mm(lo, ones)


def normalize(raw, ones):
    cen = raw.astype(F32) - mm(raw, ones)
    scale = jnp.sqrt(head_mean(cen * cen, ones) + EPS)
    return cen / scale, scale


def low_rows(shape):
    return lax.broadcasted_iota(jnp.int32, shape, 0) < 4


def call(body, outs, scratch=(), smem_in=(), n_in=0, smem_out=(), cost=None, specs=None, mib=24, out_hbm=False):
    return pl.pallas_call(
        body,
        out_shape=outs,
        grid=(1,) if specs else (),
        in_specs=[(specs or {}).get(i, SM if i in smem_in else VM) for i in range(n_in)],
        out_specs=[
            pl.BlockSpec(memory_space=pltpu.HBM) if out_hbm else SM if i in smem_out else VM for i in range(len(outs))
        ],
        scratch_shapes=list(scratch),
        cost_estimate=cost,
        compiler_params=pltpu.CompilerParams(vmem_limit_bytes=mib * 1024 * 1024),
    )


def cost(us):
    return pl.CostEstimate(flops=int(us * 1e9), bytes_accessed=int(us * 1e6), transcendentals=0)


def sds(shape, dtype):
    return jax.ShapeDtypeStruct(shape, dtype)


def far(shape, dtype):
    return pltpu.HBM(shape, dtype)


def in_hbm(v):
    return pltpu.with_memory_space_constraint(v, pltpu.HBM)


def front_kernel(ids, x_ref, c_ref, wq_hbm, wo_hbm, send, slots, qkv_ref, g_ref, cnt, ss, wq_ref, wo_ref, sems):
    loads = [
        pltpu.make_async_copy(wq_hbm, wq_ref, sems.at[0]),
        pltpu.make_async_copy(wo_hbm, wo_ref, sems.at[1]),
    ]
    for load in loads:
        load.start()

    for i in range(NB):
        cnt[i] = 0

    @pl.loop(0, NB // 8)
    def _(step):
      for b in [8 * step + u for u in range(8)]:
        r = ids[b]
        k = cnt[r]
        cnt[r] = k + 1
        slots[b] = 2 * r + k

    send[:, :, 0:W] = jnp.zeros((CHIPS, 8, W), BF)
    low = low_rows((8, W))

    @pl.loop(0, 4)
    def _(step):
      for i in [4 * step + u for u in range(4)]:
        x = x_ref[pl.ds(pl.multiple_of(i * 16, 16), 16), :].astype(F32)
        c = c_ref[pl.ds(pl.multiple_of(i * 16, 16), 16), :].astype(F32)
        for h in range(2):
            xa, ca = x[8 * h : 8 * h + 8], c[8 * h : 8 * h + 8]
            xr, cr = pltpu.roll(xa, 4, 0), pltpu.roll(ca, 4, 0)
            send[slots[4 * i + 2 * h], :, 0:W] = jnp.where(low, xa, cr).astype(BF)
            send[slots[4 * i + 2 * h + 1], :, 0:W] = jnp.where(low, xr, ca).astype(BF)

    for load in loads:
        load.wait()
    ones = head_ones()
    qkv = mm(x_ref[...], wq_ref[...]).astype(BF)
    qkv_ref[...] = qkv
    g = mm_t(c_ref[...], wo_ref[...]).astype(BF)
    g_ref[...] = g
    kn = normalize(qkv[:, W : 2 * W], ones)[0].astype(BF)
    vn = normalize(qkv[:, 2 * W :], ones)[0].astype(BF)
    left = lax.broadcasted_iota(jnp.int32, (64, 128), 1) < 64
    for j in range(4):
        s = slice(128 * j, 128 * j + 128)
        a = t_mm(kn[:, s], vn[:, s])
        ss[64 * j : 64 * j + 64, :] = jnp.where(left, a[:64], a[64:])
        a = t_mm(qkv[:, s], g[:, s])
        ss[256 + 64 * j : 320 + 64 * j, :] = jnp.where(left, a[:64], a[64:])
    low2 = low_rows((8, 128))

    @pl.loop(0, 16)
    def _(step):
      for i in [4 * step + u for u in range(4)]:
        v = ss[pl.ds(pl.multiple_of(i * 8, 8), 8), :]
        hi = v.astype(BF).astype(F32)
        lo = v - hi
        send[2 * i, :, W:] = jnp.where(low2, hi, pltpu.roll(lo, 4, 0)).astype(BF)
        send[2 * i + 1, :, W:] = jnp.where(low2, pltpu.roll(hi, 4, 0), lo).astype(BF)


def query_kernel(pos, x_ref, g_ref, keep, send):
    x, g = x_ref[...], g_ref[...]
    for core, dst in ((pos[3], keep), (1 - pos[3], send)):
        xk = mm(x, pick(core)).astype(BF)
        dst[...] = (t_mm(xk, g) * (1.0 / TOTAL)).astype(dst.dtype)


def pick(core):
    r = lax.broadcasted_iota(jnp.int32, (W, PTS), 0)
    k = lax.broadcasted_iota(jnp.int32, (W, PTS), 1)
    return jnp.where(r == 4 * (k % CHIPS) + 2 * core + k // CHIPS, 1.0, 0.0).astype(BF)


def deal_query_kernel(keep, near, out, rows):
    tot = keep[...] + near[...].astype(F32)
    for j in range(2):
        for q in range(4):
            rows[pl.ds(4 * j + q, CHIPS, stride=8), :] = tot[CHIPS * j : CHIPS * j + CHIPS, 128 * q : 128 * q + 128]
    out[...] = rows[...].reshape(CHIPS, 8, 128).astype(BF)


def spread_kernel(recv, query, out):
    v = jnp.sum(recv[...].astype(F32), axis=0)
    v = (v + pltpu.roll(v, 4, 0)) * (1.0 / TOTAL)
    hi = v.astype(BF).astype(F32)
    v = jnp.where(low_rows((8, 128)), hi, v - hi).astype(BF)
    out[:, :, 0:128] = jnp.broadcast_to(v[None], (CHIPS, 8, 128))
    out[:, :, 128:256] = query[...]


def slice_kernel(axis, src, out, sem):
    part = pl.ds(pl.multiple_of(lax.axis_index("narrow") * 256, 256), 256)
    load = pltpu.make_async_copy(src.at[part, :] if axis == 0 else src.at[:, part], out, sem)
    load.start()
    load.wait()


def act(pre, gh, cols, hid, gpre):
    sq = pre * pre
    t = jnp.tanh(GS * (pre + GC * pre * sq))
    up = 0.5 * (1.0 + t)
    hid[:, cols] = (pre * up).astype(BF)
    slope = up + 0.5 * pre * (1.0 - t * t) * GS * (1.0 + 3.0 * GC * sq)
    gpre[:, cols] = (gh * slope).astype(BF)


def expert_kernel(
    pos, recv, wi_h, wiy_h, win_h, wo_h, woy_h, won_h, b_ref, bp_ref,
    send_h, x_h, c_h, hid_h, gpre_h, ki_h, si_h, ko_h, so_h,
    x_s, c_s, hid, gpre, hid_p, gpre_p, o_s, k_s, send, ki, si, ko, so, wi, wiy, win, wo, woy, won, in_sems, out_sems,
):
    n = pos[3]
    mine = pl.ds(pl.multiple_of(n * 256, 256), 256)
    other = pl.ds(pl.multiple_of(256 - n * 256, 256), 256)
    low = low_rows((8, W))
    loads = [
        pltpu.make_async_copy(a, b, in_sems.at[k])
        for k, (a, b) in enumerate(
            ((wi_h, wi), (wo_h, wo), (wiy_h, wiy), (woy_h, woy), (win_h, win), (won_h, won))
        )
    ]
    stores = [
        pltpu.make_async_copy(a, b, out_sems.at[k])
        for k, (a, b) in enumerate(
            (
                (x_s, x_h), (c_s, c_h), (hid, hid_h), (gpre, gpre_h),
                (ki, ki_h), (si, si_h), (ko, ko_h), (so, so_h), (send, send_h),
            )
        )
    ]
    for load in loads:
        load.start()

    @pl.loop(0, 8)
    def _(step):
      for i in [4 * step + u for u in range(4)]:
        xs, cs = [], []
        for h in range(2):
            a = recv[4 * i + 2 * h].astype(F32)
            b = recv[4 * i + 2 * h + 1].astype(F32)
            xs.append(jnp.where(low, a, pltpu.roll(b, 4, 0)))
            cs.append(jnp.where(low, pltpu.roll(a, 4, 0), b))
        rows = pl.ds(pl.multiple_of(i * 16, 16), 16)
        x_s[rows, :] = jnp.concatenate(xs, axis=0).astype(BF)
        c_s[rows, :] = jnp.concatenate(cs, axis=0).astype(BF)

    stores[0].start()
    stores[1].start()
    loads[0].wait()
    loads[1].wait()

    for i in range(4):
        cols = slice(i * 256, i * 256 + 256)
        pre = mm(x_s[...], wi[:, cols]) + b_ref[:, cols]
        gh = mm_t(c_s[...], wo[cols, :])
        act(pre, gh, cols, hid, gpre)

    stores[2].start()
    stores[3].start()
    for load in loads[2:]:
        load.wait()

    for i in range(4):
        cols = slice(i * 256, i * 256 + 256)
        pre = mm(x_s[:, mine], wiy[:, cols]) + mm(x_s[:, other], win[:, cols]) + bp_ref[:, cols]
        gh = mm_t(c_s[:, mine], woy[cols, :]) + mm_t(c_s[:, other], won[cols, :])
        act(pre, gh, cols, hid_p, gpre_p)

    grad_part(n, x_s, c_s, hid_p, gpre_p, ki, si, ko, so)
    for store in stores[4:8]:
        store.start()

    for yr, kr, part in ((woy, wiy, mine), (won, win, other)):
        o_s[:, part] = mm(hid[...], wo[:, part]) + mm(hid_p[...], yr[...])
        k_s[:, part] = mm_t(gpre[...], wi[part, :]) + mm_t(gpre_p[...], kr[...])

    @pl.loop(0, 16)
    def _(step):
      for i in [4 * step + u for u in range(4)]:
        rows = pl.ds(pl.multiple_of(i * 8, 8), 8)
        o, k = o_s[rows, :], k_s[rows, :]
        send[2 * i, :, :] = jnp.where(low, o, pltpu.roll(k, 4, 0)).astype(BF)
        send[2 * i + 1, :, :] = jnp.where(low, pltpu.roll(o, 4, 0), k).astype(BF)

    stores[8].start()
    for store in stores:
        store.wait()


def grad_part(n, x_s, c_s, hid, gpre, keep_i, send_i, keep_o, send_o):
    mine = pl.ds(pl.multiple_of(n * 256, 256), 256)
    other = pl.ds(pl.multiple_of(256 - n * 256, 256), 256)

    @pl.loop(0, 2)
    def _(i):
        cols = pl.ds(pl.multiple_of(i * 512, 512), 512)
        g = gpre[:, cols]
        keep_i[0:256, cols] = t_mm(x_s[:, mine], g) * SHARE
        send_i[0:256, cols] = (t_mm(x_s[:, other], g) * SHARE).astype(BF)
        bias = jnp.sum(g.astype(F32), axis=0, keepdims=True) * SHARE
        keep_i[256:272, cols] = jnp.broadcast_to(bias, (16, 512))
        send_i[256:272, cols] = jnp.broadcast_to(bias, (16, 512)).astype(BF)
        h = hid[:, cols]
        keep_o[cols, :] = t_mm(h, c_s[:, mine]) * SHARE
        send_o[cols, :] = (t_mm(h, c_s[:, other]) * SHARE).astype(BF)


def weight_kernel(pos, x_s, c_s, hid, gpre, keep_i, send_i, keep_o, send_o):
    grad_part(pos[3], x_s, c_s, hid, gpre, keep_i, send_i, keep_o, send_o)


def merge_kernel(keep_i, got_i, keep_o, got_o, away_i, away_o):
    away_i[...] = (keep_i[...] + got_i[...].astype(F32)).astype(BF)
    away_o[...] = (keep_o[...] + got_o[...].astype(F32)).astype(BF)


def end_kernel(pos, keep_i, got_i, far_i, keep_o, got_o, far_o, grad_i, bias, grad_o, row):
    def total(a, b, c, rows):
        return a[rows, :] + b[rows, :].astype(F32) + c[rows, :].astype(F32)

    grad_i[...] = total(keep_i, got_i, far_i, slice(0, 256))
    row[...] = total(keep_i, got_i, far_i, slice(256, 272))[0:8, :]
    bias[...] = row[0:1, pl.ds(pl.multiple_of(pos[3] * 512, 512), 512)]
    grad_o[...] = total(keep_o, got_o, far_o, slice(0, HALF))


def attn_kernel(pos, rs, rs2, qkv_ref, g_ref, x_ref, c_ref, mix_ref, gq, keep, send, query, ss):
    low = low_rows((8, 128))

    @pl.loop(0, 32)
    def _(i):
        tiles = []
        for h in range(2):
            pair = []
            for k in range(2):
                d = 4 * i + 2 * h + k
                v = rs[d, :, 0:128].astype(F32) + rs2[d].astype(F32)
                pair.append(v + pltpu.roll(v, 4, 0))
            tiles.append(jnp.where(low, pair[0], pair[1]))
        ss[pl.ds(pl.multiple_of(i * 16, 16), 16), :] = jnp.concatenate(tiles, axis=0).astype(BF)

    ones = head_ones()
    qkv, g = qkv_ref[...], g_ref[...]
    ku, ks = normalize(qkv[:, W : 2 * W], ones)
    vu, vs = normalize(qkv[:, 2 * W :], ones)
    kn, vn = ku.astype(BF), vu.astype(BF)
    left = lax.broadcasted_iota(jnp.int32, (64, 128), 1) < 64
    total = jnp.sum(rs[:, :, 128:256].astype(F32), axis=0)
    total_hi = total.astype(BF)
    total_lo = (total - total_hi.astype(F32)).astype(BF)
    block = lax.broadcasted_iota(jnp.int32, (8, 128), 0) % 4

    def diag(p):
        z = jnp.zeros_like(p)
        return jnp.concatenate([jnp.where(left, p, z), jnp.where(left, z, p)], axis=0)

    gk, gv = [], []
    rows = jnp.zeros((8, 128), F32)
    for j in range(4):
        s = slice(128 * j, 128 * j + 128)
        sm = diag(ss[64 * j : 64 * j + 64, :].astype(F32)).astype(BF)
        gs = diag(ss[256 + 64 * j : 320 + 64 * j, :].astype(F32)).astype(BF)
        mix_ref[:, s] = mm(qkv[:, s], sm).astype(BF)
        gq[:, s] = mm_t(g[:, s], sm).astype(BF)
        rows = jnp.where(block == j, mm_t(total_hi, sm) + mm_t(total_lo, sm), rows)
        gk.append(mm_t(vn[:, s], gs))
        gv.append(mm(kn[:, s], gs))
    query[...] = rows

    def back(gr, u, sc):
        return ((gr - head_mean(gr, ones) - u * head_mean(gr * u, ones)) / sc).astype(BF)

    gq[:, W : 2 * W] = back(jnp.concatenate(gk, axis=1), ku, ks)
    gq[:, 2 * W :] = back(jnp.concatenate(gv, axis=1), vu, vs)
    x, c, mixed = x_ref[...], c_ref[...], mix_ref[...]
    for core, dst in ((pos[3], keep), (1 - pos[3], send)):
        sel = pick(core)
        xk, mk = mm(x, sel).astype(BF), mm(mixed, sel).astype(BF)
        for q in range(2):
            dst[:, W * q : W * q + W] = (t_mm(xk, gq[:, W * q + W : W * q + 2 * W]) * (1.0 / TOTAL)).astype(dst.dtype)
        dst[:, 2 * W :] = (t_mm(mk, c) * (1.0 / TOTAL)).astype(dst.dtype)


def base_kernel(x, c, mixed, gq, wq, wo, base_o, base_k):
    base_o[...] = x[...].astype(F32) + mm(mixed[...], wo[...])
    base_k[...] = c[...].astype(F32) + mm_t(gq[...], wq[...])


def join_kernel(ret, keep, near, out, rows):
    out[:, :, 0:W] = ret[...]
    size = 8 * CHIPS
    for t in range(3):
        for j in range(2):
            part = slice(CHIPS * j, CHIPS * j + CHIPS)
            for q in range(4):
                cols = slice(384 * q + 128 * t, 384 * q + 128 * t + 128)
                v = keep[part, cols] + near[part, cols].astype(F32)
                rows[pl.ds(size * t + 4 * j + q, CHIPS, stride=8), :] = v
        v = rows[size * t : size * t + size, :].reshape(CHIPS, 8, 128)
        out[:, :, W + 128 * t : W + 128 * t + 128] = v.astype(BF)


def final_kernel(slots, ret, base_o, base_k, query, lo, gf, att):
    low = low_rows((8, W))

    @pl.loop(0, 16)
    def _(i):
        os, ks = [], []
        for h in range(2):
            a = ret[slots[4 * i + 2 * h], :, 0:W].astype(F32)
            b = ret[slots[4 * i + 2 * h + 1], :, 0:W].astype(F32)
            os.append(jnp.where(low, a, pltpu.roll(b, 4, 0)))
            ks.append(jnp.where(low, pltpu.roll(a, 4, 0), b))
        rows = pl.ds(pl.multiple_of(i * 16, 16), 16)
        lo[rows, :] = (base_o[rows, :] + jnp.concatenate(os, axis=0)).astype(BF)
        gf[rows, :] = (base_k[rows, :] + jnp.concatenate(ks, axis=0)).astype(BF)

    v = jnp.sum(ret[:, :, W:].astype(F32), axis=0)
    q = query[...]
    for j in range(2):
        for b in range(4):
            r = slice(4 * j + b, 4 * j + b + 1)
            att[j : j + 1, 128 * b : 128 * b + 128] = q[r]
            att[j : j + 1, W + 384 * b : W + 384 * b + 384] = v[r]


def layer(x, ids, wq, wo_att, wi, bi, wo, c):
    n = lax.axis_index("narrow")
    w = lax.axis_index("wide")
    pos = jnp.stack([w // 16, w // 4 % 4, w % 4, n]).astype(jnp.int32)
    pair = [(i, i ^ 1) for i in range(CHIPS)]
    swap = [(0, 1), (1, 0)]

    def across(v):
        return lax.ppermute(v, "wide", pair)

    def beside(v):
        return lax.ppermute(v, "narrow", swap)

    def deal(v):
        return lax.all_to_all(v, "wide", split_axis=0, concat_axis=0, tiled=True)

    def run(body, us, outs, args, scratch=(), smem_in=(), smem_out=(), specs=None, mib=24, out_hbm=False):
        return call(
            body, outs, scratch, smem_in=smem_in, n_in=len(args), smem_out=smem_out, cost=cost(us),
            specs=specs, mib=mib, out_hbm=out_hbm,
        )(*args)

    anywhere = pl.BlockSpec(memory_space=pltpu.HBM)

    def half(v, axis):
        shape = (256, HALF) if axis == 0 else (HALF, 256)
        (out,) = run(
            lambda *refs: slice_kernel(axis, *refs), 1, [sds(shape, BF)], (in_hbm(v),),
            [pltpu.SemaphoreType.DMA], specs={0: anywhere},
        )
        return out

    wiy = across(half(wi, 0))
    woy = across(half(wo, 1))
    bp = across(bi)
    win, won = beside(wiy), beside(woy)

    send, slots, qkv, g = run(
        front_kernel, 5,
        [far((CHIPS, 8, 640), BF), sds((NB,), jnp.int32), far((PTS, 3 * W), BF), far((PTS, W), BF)],
        (in_hbm(ids), in_hbm(x), in_hbm(c), in_hbm(wq), in_hbm(wo_att)),
        [
            pltpu.SMEM((NB,), jnp.int32), pltpu.VMEM((W, 128), F32), pltpu.VMEM((W, 3 * W), BF),
            pltpu.VMEM((W, W), BF), pltpu.SemaphoreType.DMA((2,)),
        ],
        (0,), (1,), specs={3: anywhere, 4: anywhere}, mib=48,
    )
    recv = deal(send)
    keep_q, away_q = run(query_kernel, 2, [sds((PTS, W), F32), sds((PTS, W), BF)], (pos, x, g), (), (0,))
    (dealt_q,) = run(
        deal_query_kernel, 1, [sds((CHIPS, 8, 128), BF)], (keep_q, beside(away_q)),
        [pltpu.VMEM((8 * CHIPS, 128), F32)],
    )
    (spread,) = run(
        spread_kernel, 1, [far((CHIPS, 8, 256), BF)], (recv, dealt_q),
        specs={0: pl.BlockSpec((CHIPS, 8, 128), lambda i: (0, 0, 4))},
    )
    rs = deal(spread)
    grads = [((272, HALF), F32), ((272, HALF), BF), ((HALF, 256), F32), ((HALF, 256), BF)]
    ret, x_s, c_s, hid, gpre, keep_i, send_i, keep_o, send_o = run(
        expert_kernel, 12,
        [far((CHIPS, 8, W), BF), far((W, W), BF), far((W, W), BF), far((W, HALF), BF), far((W, HALF), BF)]
        + [far(*v) for v in grads],
        (pos, recv, *map(in_hbm, (wi, wiy, win, wo, woy, won)), bi.reshape(1, HALF), bp.reshape(1, HALF)),
        [pltpu.VMEM((W, W), BF)] * 2 + [pltpu.VMEM((W, HALF), BF)] * 4 + [pltpu.VMEM((W, W), F32)] * 2
        + [pltpu.VMEM((CHIPS, 8, W), BF)] + [pltpu.VMEM(*v) for v in grads]
        + [
            pltpu.VMEM(v, BF)
            for v in ((W, HALF), (256, HALF), (256, HALF), (HALF, W), (HALF, 256), (HALF, 256))
        ]
        + [pltpu.SemaphoreType.DMA((6,)), pltpu.SemaphoreType.DMA((9,))],
        (0,),
        specs={1: pl.BlockSpec((CHIPS, 8, W), lambda i: (0, 0, 0)), **{k: anywhere for k in range(2, 8)}},
        out_hbm=True, mib=48,
    )
    got_i, got_o = beside(send_i), beside(send_o)
    rs2 = beside(rs)
    mixed, gq, keep, away, query = run(
        attn_kernel, 7,
        [sds((PTS, W), BF), sds((PTS, 3 * W), BF), sds((PTS, 3 * W), F32), sds((PTS, 3 * W), BF), sds((8, 128), F32)],
        (pos, rs, rs2, qkv, g, x, c), [pltpu.VMEM((W, 128), BF)], (0,),
        specs={2: pl.BlockSpec((CHIPS, 8, 128), lambda i: (0, 0, 0))},
    )
    near = beside(away)
    base_o, base_k = run(base_kernel, 1, [far((PTS, W), F32), far((PTS, W), F32)], (x, c, mixed, gq, wq, wo_att))
    away_i, away_o = run(
        merge_kernel, 1, [sds((272, HALF), BF), sds((HALF, 256), BF)], (in_hbm(keep_i), got_i, in_hbm(keep_o), got_o)
    )
    far_i, far_o = across(away_i), across(away_o)
    (joined,) = run(join_kernel, 2, [far((CHIPS, 8, 896), BF)], (ret, keep, near), [pltpu.VMEM((24 * CHIPS, 128), F32)])
    back = deal(joined)
    keep_i, send_i, keep_o, send_o = run(
        weight_kernel, 5, [sds(*v) for v in grads], (pos, x_s, c_s, hid, gpre), (), (0,)
    )
    got_i, got_o = beside(send_i), beside(send_o)
    grad_in, grad_b, grad_out = run(
        end_kernel, 3, [sds((256, HALF), F32), sds((1, 512), F32), sds((HALF, 256), F32)],
        (pos, keep_i, got_i, far_i, keep_o, got_o, far_o), [pltpu.VMEM((8, HALF), F32)], (0,),
    )
    layer_out, grad_feats, att = run(
        final_kernel, 3, [sds((PTS, W), BF), sds((PTS, W), BF), sds((2, 4 * W), F32)],
        (slots, back, in_hbm(base_o), in_hbm(base_k), query), (), (0,),
    )
    return (layer_out, grad_feats, att, grad_in, grad_out, grad_b.reshape(512))


def solution(mesh):
    placed = (
        P(("wide", "narrow"), None),
        P(("wide", "narrow")),
        P(),
        P(),
        P(None, "wide"),
        P("wide"),
        P("wide", None),
        P(("wide", "narrow"), None),
    )
    return jax.shard_map(
        layer,
        mesh=mesh,
        in_specs=placed,
        out_specs=(
            P(("wide", "narrow"), None),
            P(("wide", "narrow"), None),
            P(("wide", "narrow"), None),
            P("narrow", "wide"),
            P("wide", "narrow"),
            P(("wide", "narrow")),
        ),
        check_vma=False,
    )
```

```python
import jax
import jax.numpy as jnp
from jax import lax
from jax.experimental import pallas as pl
from jax.experimental.pallas import tpu as pltpu
from jax.sharding import PartitionSpec as P

F32 = jnp.float32
BF = jnp.bfloat16
EPS = 1e-05
GS = 0.7978845608
GC = 0.044715
W = 512
PTS = 256
NB = 64
CHIPS = 128
TOTAL = 65536.0
SHARE = 64.0 / 65536.0
HALF = 1024
VM = pl.BlockSpec(memory_space=pltpu.VMEM)
SM = pl.BlockSpec(memory_space=pltpu.SMEM)


def mm(a, b):
    return jnp.dot(a, b, preferred_element_type=F32)


def mm_t(a, b):
    return lax.dot_general(a, b, (((1,), (1,)), ((), ())), preferred_element_type=F32)


def t_mm(a, b):
    return lax.dot_general(a, b, (((0,), (0,)), ((), ())), preferred_element_type=F32)


def head_ones():
    r = lax.broadcasted_iota(jnp.int32, (W, W), 0) // 64
    c = lax.broadcasted_iota(jnp.int32, (W, W), 1) // 64
    return jnp.where(r == c, 1.0 / 64.0, 0.0).astype(BF)


def head_mean(v, ones):
    hi = v.astype(BF)
    lo = (v - hi.astype(F32)).astype(BF)
    return mm(hi, ones) + mm(lo, ones)


def normalize(raw, ones):
    cen = raw.astype(F32) - mm(raw, ones)
    scale = jnp.sqrt(head_mean(cen * cen, ones) + EPS)
    return cen / scale, scale


def low_rows(shape):
    return lax.broadcasted_iota(jnp.int32, shape, 0) < 4


def call(body, outs, scratch=(), smem_in=(), n_in=0, smem_out=(), cost=None, specs=None, mib=24, out_hbm=False):
    return pl.pallas_call(
        body,
        out_shape=outs,
        grid=(1,) if specs else (),
        in_specs=[(specs or {}).get(i, SM if i in smem_in else VM) for i in range(n_in)],
        out_specs=[
            pl.BlockSpec(memory_space=pltpu.HBM) if out_hbm else SM if i in smem_out else VM for i in range(len(outs))
        ],
        scratch_shapes=list(scratch),
        cost_estimate=cost,
        compiler_params=pltpu.CompilerParams(vmem_limit_bytes=mib * 1024 * 1024),
    )


def cost(us):
    return pl.CostEstimate(flops=int(us * 1e9), bytes_accessed=int(us * 1e6), transcendentals=0)


def sds(shape, dtype):
    return jax.ShapeDtypeStruct(shape, dtype)


def far(shape, dtype):
    return pltpu.HBM(shape, dtype)


def in_hbm(v):
    return pltpu.with_memory_space_constraint(v, pltpu.HBM)


def front_kernel(ids, x_ref, c_ref, wq_hbm, wo_hbm, send, slots, qkv_ref, g_ref, cnt, ss, wq_ref, wo_ref, sems):
    loads = [
        pltpu.make_async_copy(wq_hbm, wq_ref, sems.at[0]),
        pltpu.make_async_copy(wo_hbm, wo_ref, sems.at[1]),
    ]
    for load in loads:
        load.start()

    for i in range(NB):
        cnt[i] = 0

    @pl.loop(0, NB // 8)
    def _(step):
      for b in [8 * step + u for u in range(8)]:
        r = ids[b]
        k = cnt[r]
        cnt[r] = k + 1
        slots[b] = 2 * r + k

    send[:, :, 0:W] = jnp.zeros((CHIPS, 8, W), BF)
    low = low_rows((8, W))

    @pl.loop(0, 4)
    def _(step):
      for i in [4 * step + u for u in range(4)]:
        x = x_ref[pl.ds(pl.multiple_of(i * 16, 16), 16), :].astype(F32)
        c = c_ref[pl.ds(pl.multiple_of(i * 16, 16), 16), :].astype(F32)
        for h in range(2):
            xa, ca = x[8 * h : 8 * h + 8], c[8 * h : 8 * h + 8]
            xr, cr = pltpu.roll(xa, 4, 0), pltpu.roll(ca, 4, 0)
            send[slots[4 * i + 2 * h], :, 0:W] = jnp.where(low, xa, cr).astype(BF)
            send[slots[4 * i + 2 * h + 1], :, 0:W] = jnp.where(low, xr, ca).astype(BF)

    for load in loads:
        load.wait()
    ones = head_ones()
    qkv = mm(x_ref[...], wq_ref[...]).astype(BF)
    qkv_ref[...] = qkv
    g = mm_t(c_ref[...], wo_ref[...]).astype(BF)
    g_ref[...] = g
    kn = normalize(qkv[:, W : 2 * W], ones)[0].astype(BF)
    vn = normalize(qkv[:, 2 * W :], ones)[0].astype(BF)
    left = lax.broadcasted_iota(jnp.int32, (64, 128), 1) < 64
    for j in range(4):
        s = slice(128 * j, 128 * j + 128)
        a = t_mm(kn[:, s], vn[:, s])
        ss[64 * j : 64 * j + 64, :] = jnp.where(left, a[:64], a[64:])
        a = t_mm(qkv[:, s], g[:, s])
        ss[256 + 64 * j : 320 + 64 * j, :] = jnp.where(left, a[:64], a[64:])
    low2 = low_rows((8, 128))

    @pl.loop(0, 16)
    def _(step):
      for i in [4 * step + u for u in range(4)]:
        v = ss[pl.ds(pl.multiple_of(i * 8, 8), 8), :]
        hi = v.astype(BF).astype(F32)
        lo = v - hi
        send[2 * i, :, W:] = jnp.where(low2, hi, pltpu.roll(lo, 4, 0)).astype(BF)
        send[2 * i + 1, :, W:] = jnp.where(low2, pltpu.roll(hi, 4, 0), lo).astype(BF)


def query_kernel(pos, x_ref, g_ref, keep, send):
    x, g = x_ref[...], g_ref[...]
    for core, dst in ((pos[3], keep), (1 - pos[3], send)):
        xk = mm(x, pick(core)).astype(BF)
        dst[...] = (t_mm(xk, g) * (1.0 / TOTAL)).astype(dst.dtype)


def pick(core):
    r = lax.broadcasted_iota(jnp.int32, (W, PTS), 0)
    k = lax.broadcasted_iota(jnp.int32, (W, PTS), 1)
    return jnp.where(r == 4 * (k % CHIPS) + 2 * core + k // CHIPS, 1.0, 0.0).astype(BF)


def deal_query_kernel(keep, near, out, rows):
    tot = keep[...] + near[...].astype(F32)
    for j in range(2):
        for q in range(4):
            rows[pl.ds(4 * j + q, CHIPS, stride=8), :] = tot[CHIPS * j : CHIPS * j + CHIPS, 128 * q : 128 * q + 128]
    out[...] = rows[...].reshape(CHIPS, 8, 128).astype(BF)


def spread_kernel(recv, query, out):
    v = jnp.sum(recv[...].astype(F32), axis=0)
    v = (v + pltpu.roll(v, 4, 0)) * (1.0 / TOTAL)
    hi = v.astype(BF).astype(F32)
    v = jnp.where(low_rows((8, 128)), hi, v - hi).astype(BF)
    out[:, :, 0:128] = jnp.broadcast_to(v[None], (CHIPS, 8, 128))
    out[:, :, 128:256] = query[...]


def slice_kernel(axis, src, out, sem):
    part = pl.ds(pl.multiple_of(lax.axis_index("narrow") * 256, 256), 256)
    load = pltpu.make_async_copy(src.at[part, :] if axis == 0 else src.at[:, part], out, sem)
    load.start()
    load.wait()


def act(pre, gh, cols, hid, gpre):
    sq = pre * pre
    t = jnp.tanh(GS * (pre + GC * pre * sq))
    up = 0.5 * (1.0 + t)
    hid[:, cols] = (pre * up).astype(BF)
    slope = up + 0.5 * pre * (1.0 - t * t) * GS * (1.0 + 3.0 * GC * sq)
    gpre[:, cols] = (gh * slope).astype(BF)


def expert_kernel(
    pos, recv, wi_h, wiy_h, win_h, wo_h, woy_h, won_h, b_ref, bp_ref,
    send_h, x_h, c_h, hid_h, gpre_h, ki_h, si_h, ko_h, so_h,
    x_s, c_s, hid, gpre, hid_p, gpre_p, o_s, k_s, send, ki, si, ko, so, wi, wiy, win, wo, woy, won, in_sems, out_sems,
):
    n = pos[3]
    mine = pl.ds(pl.multiple_of(n * 256, 256), 256)
    other = pl.ds(pl.multiple_of(256 - n * 256, 256), 256)
    low = low_rows((8, W))
    loads = [
        pltpu.make_async_copy(a, b, in_sems.at[k])
        for k, (a, b) in enumerate(
            ((wi_h, wi), (wo_h, wo), (wiy_h, wiy), (woy_h, woy), (win_h, win), (won_h, won))
        )
    ]
    stores = [
        pltpu.make_async_copy(a, b, out_sems.at[k])
        for k, (a, b) in enumerate(
            (
                (x_s, x_h), (c_s, c_h), (hid, hid_h), (gpre, gpre_h),
                (ki, ki_h), (si, si_h), (ko, ko_h), (so, so_h), (send, send_h),
            )
        )
    ]
    for load in loads:
        load.start()

    @pl.loop(0, 8)
    def _(step):
      for i in [4 * step + u for u in range(4)]:
        xs, cs = [], []
        for h in range(2):
            a = recv[4 * i + 2 * h].astype(F32)
            b = recv[4 * i + 2 * h + 1].astype(F32)
            xs.append(jnp.where(low, a, pltpu.roll(b, 4, 0)))
            cs.append(jnp.where(low, pltpu.roll(a, 4, 0), b))
        rows = pl.ds(pl.multiple_of(i * 16, 16), 16)
        x_s[rows, :] = jnp.concatenate(xs, axis=0).astype(BF)
        c_s[rows, :] = jnp.concatenate(cs, axis=0).astype(BF)

    stores[0].start()
    stores[1].start()
    loads[0].wait()
    loads[1].wait()

    for i in range(4):
        cols = slice(i * 256, i * 256 + 256)
        pre = mm(x_s[...], wi[:, cols]) + b_ref[:, cols]
        gh = mm_t(c_s[...], wo[cols, :])
        act(pre, gh, cols, hid, gpre)

    stores[2].start()
    stores[3].start()
    for load in loads[2:]:
        load.wait()

    for i in range(4):
        cols = slice(i * 256, i * 256 + 256)
        pre = mm(x_s[:, mine], wiy[:, cols]) + mm(x_s[:, other], win[:, cols]) + bp_ref[:, cols]
        gh = mm_t(c_s[:, mine], woy[cols, :]) + mm_t(c_s[:, other], won[cols, :])
        act(pre, gh, cols, hid_p, gpre_p)

    grad_part(n, x_s, c_s, hid_p, gpre_p, ki, si, ko, so)
    for store in stores[4:8]:
        store.start()

    for yr, kr, part in ((woy, wiy, mine), (won, win, other)):
        o_s[:, part] = mm(hid[...], wo[:, part]) + mm(hid_p[...], yr[...])
        k_s[:, part] = mm_t(gpre[...], wi[part, :]) + mm_t(gpre_p[...], kr[...])

    @pl.loop(0, 16)
    def _(step):
      for i in [4 * step + u for u in range(4)]:
        rows = pl.ds(pl.multiple_of(i * 8, 8), 8)
        o, k = o_s[rows, :], k_s[rows, :]
        send[2 * i, :, :] = jnp.where(low, o, pltpu.roll(k, 4, 0)).astype(BF)
        send[2 * i + 1, :, :] = jnp.where(low, pltpu.roll(o, 4, 0), k).astype(BF)

    stores[8].start()
    for store in stores:
        store.wait()


def grad_part(n, x_s, c_s, hid, gpre, keep_i, send_i, keep_o, send_o):
    mine = pl.ds(pl.multiple_of(n * 256, 256), 256)
    other = pl.ds(pl.multiple_of(256 - n * 256, 256), 256)

    @pl.loop(0, 2)
    def _(i):
        cols = pl.ds(pl.multiple_of(i * 512, 512), 512)
        g = gpre[:, cols]
        keep_i[0:256, cols] = t_mm(x_s[:, mine], g) * SHARE
        send_i[0:256, cols] = (t_mm(x_s[:, other], g) * SHARE).astype(BF)
        bias = jnp.sum(g.astype(F32), axis=0, keepdims=True) * SHARE
        keep_i[256:272, cols] = jnp.broadcast_to(bias, (16, 512))
        send_i[256:272, cols] = jnp.broadcast_to(bias, (16, 512)).astype(BF)
        h = hid[:, cols]
        keep_o[cols, :] = t_mm(h, c_s[:, mine]) * SHARE
        send_o[cols, :] = (t_mm(h, c_s[:, other]) * SHARE).astype(BF)


def weight_kernel(pos, x_s, c_s, hid, gpre, keep_i, send_i, keep_o, send_o):
    grad_part(pos[3], x_s, c_s, hid, gpre, keep_i, send_i, keep_o, send_o)


def merge_kernel(keep, got, away):
    away[...] = (keep[...] + got[...].astype(F32)).astype(BF)


def end_kernel(pos, keep_i, got_i, far_i, keep_o, got_o, far_o, grad_i, bias, grad_o, row):
    def total(a, b, c, rows):
        return a[rows, :] + b[rows, :].astype(F32) + c[rows, :].astype(F32)

    grad_i[...] = total(keep_i, got_i, far_i, slice(0, 256))
    row[...] = total(keep_i, got_i, far_i, slice(256, 272))[0:8, :]
    bias[...] = row[0:1, pl.ds(pl.multiple_of(pos[3] * 512, 512), 512)]
    grad_o[...] = total(keep_o, got_o, far_o, slice(0, HALF))


def attn_kernel(pos, rs, rs2, qkv_ref, g_ref, x_ref, c_ref, mix_ref, gq, keep, send, query, ss):
    low = low_rows((8, 128))

    @pl.loop(0, 32)
    def _(i):
        tiles = []
        for h in range(2):
            pair = []
            for k in range(2):
                d = 4 * i + 2 * h + k
                v = rs[d, :, 0:128].astype(F32) + rs2[d].astype(F32)
                pair.append(v + pltpu.roll(v, 4, 0))
            tiles.append(jnp.where(low, pair[0], pair[1]))
        ss[pl.ds(pl.multiple_of(i * 16, 16), 16), :] = jnp.concatenate(tiles, axis=0).astype(BF)

    ones = head_ones()
    qkv, g = qkv_ref[...], g_ref[...]
    ku, ks = normalize(qkv[:, W : 2 * W], ones)
    vu, vs = normalize(qkv[:, 2 * W :], ones)
    kn, vn = ku.astype(BF), vu.astype(BF)
    left = lax.broadcasted_iota(jnp.int32, (64, 128), 1) < 64
    total = jnp.sum(rs[:, :, 128:256].astype(F32), axis=0)
    total_hi = total.astype(BF)
    total_lo = (total - total_hi.astype(F32)).astype(BF)
    block = lax.broadcasted_iota(jnp.int32, (8, 128), 0) % 4

    def diag(p):
        z = jnp.zeros_like(p)
        return jnp.concatenate([jnp.where(left, p, z), jnp.where(left, z, p)], axis=0)

    gk, gv = [], []
    rows = jnp.zeros((8, 128), F32)
    for j in range(4):
        s = slice(128 * j, 128 * j + 128)
        sm = diag(ss[64 * j : 64 * j + 64, :].astype(F32)).astype(BF)
        gs = diag(ss[256 + 64 * j : 320 + 64 * j, :].astype(F32)).astype(BF)
        mix_ref[:, s] = mm(qkv[:, s], sm).astype(BF)
        gq[:, s] = mm_t(g[:, s], sm).astype(BF)
        rows = jnp.where(block == j, mm_t(total_hi, sm) + mm_t(total_lo, sm), rows)
        gk.append(mm_t(vn[:, s], gs))
        gv.append(mm(kn[:, s], gs))
    query[...] = rows

    def back(gr, u, sc):
        return ((gr - head_mean(gr, ones) - u * head_mean(gr * u, ones)) / sc).astype(BF)

    gq[:, W : 2 * W] = back(jnp.concatenate(gk, axis=1), ku, ks)
    gq[:, 2 * W :] = back(jnp.concatenate(gv, axis=1), vu, vs)
    x, c, mixed = x_ref[...], c_ref[...], mix_ref[...]
    for core, dst in ((pos[3], keep), (1 - pos[3], send)):
        sel = pick(core)
        xk, mk = mm(x, sel).astype(BF), mm(mixed, sel).astype(BF)
        for q in range(2):
            dst[:, W * q : W * q + W] = (t_mm(xk, gq[:, W * q + W : W * q + 2 * W]) * (1.0 / TOTAL)).astype(dst.dtype)
        dst[:, 2 * W :] = (t_mm(mk, c) * (1.0 / TOTAL)).astype(dst.dtype)


def base_kernel(x, c, mixed, gq, wq, wo, base_o, base_k):
    base_o[...] = x[...].astype(F32) + mm(mixed[...], wo[...])
    base_k[...] = c[...].astype(F32) + mm_t(gq[...], wq[...])


def join_kernel(ret, keep, near, out, rows):
    out[:, :, 0:W] = ret[...]
    size = 8 * CHIPS
    for t in range(3):
        for j in range(2):
            part = slice(CHIPS * j, CHIPS * j + CHIPS)
            for q in range(4):
                cols = slice(384 * q + 128 * t, 384 * q + 128 * t + 128)
                v = keep[part, cols] + near[part, cols].astype(F32)
                rows[pl.ds(size * t + 4 * j + q, CHIPS, stride=8), :] = v
        v = rows[size * t : size * t + size, :].reshape(CHIPS, 8, 128)
        out[:, :, W + 128 * t : W + 128 * t + 128] = v.astype(BF)


def final_kernel(slots, ret, base_o, base_k, query, lo, gf, att):
    low = low_rows((8, W))

    @pl.loop(0, 16)
    def _(i):
        os, ks = [], []
        for h in range(2):
            a = ret[slots[4 * i + 2 * h], :, 0:W].astype(F32)
            b = ret[slots[4 * i + 2 * h + 1], :, 0:W].astype(F32)
            os.append(jnp.where(low, a, pltpu.roll(b, 4, 0)))
            ks.append(jnp.where(low, pltpu.roll(a, 4, 0), b))
        rows = pl.ds(pl.multiple_of(i * 16, 16), 16)
        lo[rows, :] = (base_o[rows, :] + jnp.concatenate(os, axis=0)).astype(BF)
        gf[rows, :] = (base_k[rows, :] + jnp.concatenate(ks, axis=0)).astype(BF)

    v = jnp.sum(ret[:, :, W:].astype(F32), axis=0)
    q = query[...]
    for j in range(2):
        for b in range(4):
            r = slice(4 * j + b, 4 * j + b + 1)
            att[j : j + 1, 128 * b : 128 * b + 128] = q[r]
            att[j : j + 1, W + 384 * b : W + 384 * b + 384] = v[r]


def layer(x, ids, wq, wo_att, wi, bi, wo, c):
    n = lax.axis_index("narrow")
    w = lax.axis_index("wide")
    pos = jnp.stack([w // 16, w // 4 % 4, w % 4, n]).astype(jnp.int32)
    pair = [(i, i ^ 1) for i in range(CHIPS)]
    swap = [(0, 1), (1, 0)]

    def across(v):
        return lax.ppermute(v, "wide", pair)

    def beside(v):
        return lax.ppermute(v, "narrow", swap)

    def deal(v):
        return lax.all_to_all(v, "wide", split_axis=0, concat_axis=0, tiled=True)

    def run(body, us, outs, args, scratch=(), smem_in=(), smem_out=(), specs=None, mib=24, out_hbm=False):
        return call(
            body, outs, scratch, smem_in=smem_in, n_in=len(args), smem_out=smem_out, cost=cost(us),
            specs=specs, mib=mib, out_hbm=out_hbm,
        )(*args)

    anywhere = pl.BlockSpec(memory_space=pltpu.HBM)

    def half(v, axis):
        shape = (256, HALF) if axis == 0 else (HALF, 256)
        (out,) = run(
            lambda *refs: slice_kernel(axis, *refs), 1, [sds(shape, BF)], (in_hbm(v),),
            [pltpu.SemaphoreType.DMA], specs={0: anywhere},
        )
        return out

    wiy = across(half(wi, 0))
    woy = across(half(wo, 1))
    bp = across(bi)
    win, won = beside(wiy), beside(woy)

    send, slots, qkv, g = run(
        front_kernel, 5,
        [far((CHIPS, 8, 640), BF), sds((NB,), jnp.int32), far((PTS, 3 * W), BF), far((PTS, W), BF)],
        (in_hbm(ids), in_hbm(x), in_hbm(c), in_hbm(wq), in_hbm(wo_att)),
        [
            pltpu.SMEM((NB,), jnp.int32), pltpu.VMEM((W, 128), F32), pltpu.VMEM((W, 3 * W), BF),
            pltpu.VMEM((W, W), BF), pltpu.SemaphoreType.DMA((2,)),
        ],
        (0,), (1,), specs={3: anywhere, 4: anywhere}, mib=48,
    )
    recv = deal(send)
    keep_q, away_q = run(query_kernel, 2, [sds((PTS, W), F32), sds((PTS, W), BF)], (pos, x, g), (), (0,))
    (dealt_q,) = run(
        deal_query_kernel, 1, [sds((CHIPS, 8, 128), BF)], (keep_q, beside(away_q)),
        [pltpu.VMEM((8 * CHIPS, 128), F32)],
    )
    (spread,) = run(
        spread_kernel, 1, [far((CHIPS, 8, 256), BF)], (recv, dealt_q),
        specs={0: pl.BlockSpec((CHIPS, 8, 128), lambda i: (0, 0, 4))},
    )
    rs = deal(spread)
    grads = [((272, HALF), F32), ((272, HALF), BF), ((HALF, 256), F32), ((HALF, 256), BF)]
    ret, x_s, c_s, hid, gpre, keep_i, send_i, keep_o, send_o = run(
        expert_kernel, 12,
        [far((CHIPS, 8, W), BF), far((W, W), BF), far((W, W), BF), far((W, HALF), BF), far((W, HALF), BF)]
        + [far(*v) for v in grads],
        (pos, recv, *map(in_hbm, (wi, wiy, win, wo, woy, won)), bi.reshape(1, HALF), bp.reshape(1, HALF)),
        [pltpu.VMEM((W, W), BF)] * 2 + [pltpu.VMEM((W, HALF), BF)] * 4 + [pltpu.VMEM((W, W), F32)] * 2
        + [pltpu.VMEM((CHIPS, 8, W), BF)] + [pltpu.VMEM(*v) for v in grads]
        + [
            pltpu.VMEM(v, BF)
            for v in ((W, HALF), (256, HALF), (256, HALF), (HALF, W), (HALF, 256), (HALF, 256))
        ]
        + [pltpu.SemaphoreType.DMA((6,)), pltpu.SemaphoreType.DMA((9,))],
        (0,),
        specs={1: pl.BlockSpec((CHIPS, 8, W), lambda i: (0, 0, 0)), **{k: anywhere for k in range(2, 8)}},
        out_hbm=True, mib=48,
    )
    got_i, got_o = beside(send_i), beside(send_o)
    rs2 = beside(rs)
    mixed, gq, keep, away, query = run(
        attn_kernel, 7,
        [sds((PTS, W), BF), sds((PTS, 3 * W), BF), sds((PTS, 3 * W), F32), sds((PTS, 3 * W), BF), sds((8, 128), F32)],
        (pos, rs, rs2, qkv, g, x, c), [pltpu.VMEM((W, 128), BF)], (0,),
        specs={2: pl.BlockSpec((CHIPS, 8, 128), lambda i: (0, 0, 0))},
    )
    near = beside(away)
    base_o, base_k = run(base_kernel, 1, [far((PTS, W), F32), far((PTS, W), F32)], (x, c, mixed, gq, wq, wo_att))
    (away_i,) = run(merge_kernel, 1, [sds((272, HALF), BF)], (in_hbm(keep_i), got_i))
    (away_o,) = run(merge_kernel, 1, [sds((HALF, 256), BF)], (in_hbm(keep_o), got_o))
    far_i, far_o = across(away_i), across(away_o)
    (joined,) = run(join_kernel, 2, [far((CHIPS, 8, 896), BF)], (ret, keep, near), [pltpu.VMEM((24 * CHIPS, 128), F32)])
    back = deal(joined)
    keep_i, send_i, keep_o, send_o = run(
        weight_kernel, 5, [sds(*v) for v in grads], (pos, x_s, c_s, hid, gpre), (), (0,)
    )
    got_i, got_o = beside(send_i), beside(send_o)
    grad_in, grad_b, grad_out = run(
        end_kernel, 3, [sds((256, HALF), F32), sds((1, 512), F32), sds((HALF, 256), F32)],
        (pos, keep_i, got_i, far_i, keep_o, got_o, far_o), [pltpu.VMEM((8, HALF), F32)], (0,),
    )
    layer_out, grad_feats, att = run(
        final_kernel, 3, [sds((PTS, W), BF), sds((PTS, W), BF), sds((2, 4 * W), F32)],
        (slots, back, in_hbm(base_o), in_hbm(base_k), query), (), (0,),
    )
    return (layer_out, grad_feats, att, grad_in, grad_out, grad_b.reshape(512))


def solution(mesh):
    placed = (
        P(("wide", "narrow"), None),
        P(("wide", "narrow")),
        P(),
        P(),
        P(None, "wide"),
        P("wide"),
        P("wide", None),
        P(("wide", "narrow"), None),
    )
    return jax.shard_map(
        layer,
        mesh=mesh,
        in_specs=placed,
        out_specs=(
            P(("wide", "narrow"), None),
            P(("wide", "narrow"), None),
            P(("wide", "narrow"), None),
            P("narrow", "wide"),
            P("wide", "narrow"),
            P(("wide", "narrow")),
        ),
        check_vma=False,
    )
```

```python
import jax
import jax.numpy as jnp
from jax import lax
from jax.experimental import pallas as pl
from jax.experimental.pallas import tpu as pltpu
from jax.sharding import PartitionSpec as P

F32 = jnp.float32
BF = jnp.bfloat16
EPS = 1e-05
GS = 0.7978845608
GC = 0.044715
W = 512
PTS = 256
NB = 64
CHIPS = 128
TOTAL = 65536.0
SHARE = 64.0 / 65536.0
HALF = 1024
VM = pl.BlockSpec(memory_space=pltpu.VMEM)
SM = pl.BlockSpec(memory_space=pltpu.SMEM)


def mm(a, b):
    return jnp.dot(a, b, preferred_element_type=F32)


def mm_t(a, b):
    return lax.dot_general(a, b, (((1,), (1,)), ((), ())), preferred_element_type=F32)


def t_mm(a, b):
    return lax.dot_general(a, b, (((0,), (0,)), ((), ())), preferred_element_type=F32)


def head_ones():
    r = lax.broadcasted_iota(jnp.int32, (W, W), 0) // 64
    c = lax.broadcasted_iota(jnp.int32, (W, W), 1) // 64
    return jnp.where(r == c, 1.0 / 64.0, 0.0).astype(BF)


def head_mean(v, ones):
    hi = v.astype(BF)
    lo = (v - hi.astype(F32)).astype(BF)
    return mm(hi, ones) + mm(lo, ones)


def normalize(raw, ones):
    cen = raw.astype(F32) - mm(raw, ones)
    scale = jnp.sqrt(head_mean(cen * cen, ones) + EPS)
    return cen / scale, scale


def low_rows(shape):
    return lax.broadcasted_iota(jnp.int32, shape, 0) < 4


def call(body, outs, scratch=(), smem_in=(), n_in=0, smem_out=(), cost=None, specs=None, mib=24, out_hbm=False):
    return pl.pallas_call(
        body,
        out_shape=outs,
        grid=(1,) if specs else (),
        in_specs=[(specs or {}).get(i, SM if i in smem_in else VM) for i in range(n_in)],
        out_specs=[
            pl.BlockSpec(memory_space=pltpu.HBM) if out_hbm else SM if i in smem_out else VM for i in range(len(outs))
        ],
        scratch_shapes=list(scratch),
        cost_estimate=cost,
        compiler_params=pltpu.CompilerParams(vmem_limit_bytes=mib * 1024 * 1024),
    )


def cost(us):
    return pl.CostEstimate(flops=int(us * 1e9), bytes_accessed=int(us * 1e6), transcendentals=0)


def sds(shape, dtype):
    return jax.ShapeDtypeStruct(shape, dtype)


def far(shape, dtype):
    return pltpu.HBM(shape, dtype)


def in_hbm(v):
    return pltpu.with_memory_space_constraint(v, pltpu.HBM)


def front_kernel(ids, x_ref, c_ref, wq_hbm, wo_hbm, send, slots, qkv_ref, g_ref, cnt, ss, wq_ref, wo_ref, sems):
    loads = [
        pltpu.make_async_copy(wq_hbm, wq_ref, sems.at[0]),
        pltpu.make_async_copy(wo_hbm, wo_ref, sems.at[1]),
    ]
    for load in loads:
        load.start()

    for i in range(NB):
        cnt[i] = 0

    @pl.loop(0, NB // 8)
    def _(step):
      for b in [8 * step + u for u in range(8)]:
        r = ids[b]
        k = cnt[r]
        cnt[r] = k + 1
        slots[b] = 2 * r + k

    send[:, :, 0 : 2 * W] = jnp.zeros((CHIPS, 4, 2 * W), BF)

    @pl.loop(0, 4)
    def _(step):
        for i in [4 * step + u for u in range(4)]:
            x = x_ref[pl.ds(pl.multiple_of(i * 16, 16), 16), :].astype(F32)
            c = c_ref[pl.ds(pl.multiple_of(i * 16, 16), 16), :].astype(F32)
            for h in range(4):
                send[slots[4 * i + h], :, 0:W] = x[4 * h : 4 * h + 4].astype(BF)
                send[slots[4 * i + h], :, W : 2 * W] = c[4 * h : 4 * h + 4].astype(BF)

    for load in loads:
        load.wait()
    ones = head_ones()
    qkv = mm(x_ref[...], wq_ref[...]).astype(BF)
    qkv_ref[...] = qkv
    g = mm_t(c_ref[...], wo_ref[...]).astype(BF)
    g_ref[...] = g
    kn = normalize(qkv[:, W : 2 * W], ones)[0].astype(BF)
    vn = normalize(qkv[:, 2 * W :], ones)[0].astype(BF)
    left = lax.broadcasted_iota(jnp.int32, (64, 128), 1) < 64
    for j in range(4):
        s = slice(128 * j, 128 * j + 128)
        a = t_mm(kn[:, s], vn[:, s])
        ss[64 * j : 64 * j + 64, :] = jnp.where(left, a[:64], a[64:])
        a = t_mm(qkv[:, s], g[:, s])
        ss[256 + 64 * j : 320 + 64 * j, :] = jnp.where(left, a[:64], a[64:])

    @pl.loop(0, 16)
    def _(step):
        for i in [4 * step + u for u in range(4)]:
            v = ss[pl.ds(pl.multiple_of(i * 8, 8), 8), :]
            send[2 * i, :, 2 * W :] = v[0:4].astype(BF)
            send[2 * i + 1, :, 2 * W :] = v[4:8].astype(BF)


def query_kernel(pos, x_ref, g_ref, keep, send):
    x, g = x_ref[...], g_ref[...]
    for core, dst in ((pos[3], keep), (1 - pos[3], send)):
        xk = mm(x, pick(core)).astype(BF)
        dst[...] = (t_mm(xk, g) * (1.0 / TOTAL)).astype(dst.dtype)


def pick(core):
    r = lax.broadcasted_iota(jnp.int32, (W, PTS), 0)
    k = lax.broadcasted_iota(jnp.int32, (W, PTS), 1)
    return jnp.where(r == 4 * (k % CHIPS) + 2 * core + k // CHIPS, 1.0, 0.0).astype(BF)


def deal_query_kernel(keep, near, out, rows):
    tot = keep[...] + near[...].astype(F32)
    for j in range(2):
        for q in range(4):
            rows[pl.ds(4 * j + q, CHIPS, stride=8), :] = tot[CHIPS * j : CHIPS * j + CHIPS, 128 * q : 128 * q + 128]
    out[...] = rows[...].reshape(CHIPS, 8, 128).astype(BF)


def spread_kernel(recv, query, out):
    v = jnp.sum(recv[...].astype(F32), axis=0) * (1.0 / TOTAL)
    v = jnp.concatenate([v, v], axis=0)
    hi = v.astype(BF).astype(F32)
    v = jnp.where(low_rows((8, 128)), hi, v - hi).astype(BF)
    out[:, :, 0:128] = jnp.broadcast_to(v[None], (CHIPS, 8, 128))
    out[:, :, 128:256] = query[...]


def slice_kernel(axis, src, out, sem):
    part = pl.ds(pl.multiple_of(lax.axis_index("narrow") * 256, 256), 256)
    load = pltpu.make_async_copy(src.at[part, :] if axis == 0 else src.at[:, part], out, sem)
    load.start()
    load.wait()


def act(pre, gh, cols, hid, gpre):
    sq = pre * pre
    t = jnp.tanh(GS * (pre + GC * pre * sq))
    up = 0.5 * (1.0 + t)
    hid[:, cols] = (pre * up).astype(BF)
    slope = up + 0.5 * pre * (1.0 - t * t) * GS * (1.0 + 3.0 * GC * sq)
    gpre[:, cols] = (gh * slope).astype(BF)


def expert_kernel(
    pos, recv, wi_h, wiy_h, win_h, wo_h, woy_h, won_h, b_ref, bp_ref,
    send_h, x_h, c_h, hid_h, gpre_h, ki_h, si_h, ko_h, so_h,
    x_s, c_s, hid, gpre, hid_p, gpre_p, o_s, k_s, send, ki, si, ko, so, wi, wiy, win, wo, woy, won, in_sems, out_sems,
):
    n = pos[3]
    mine = pl.ds(pl.multiple_of(n * 256, 256), 256)
    other = pl.ds(pl.multiple_of(256 - n * 256, 256), 256)
    low = low_rows((8, W))
    loads = [
        pltpu.make_async_copy(a, b, in_sems.at[k])
        for k, (a, b) in enumerate(
            ((wi_h, wi), (wo_h, wo), (wiy_h, wiy), (woy_h, woy), (win_h, win), (won_h, won))
        )
    ]
    stores = [
        pltpu.make_async_copy(a, b, out_sems.at[k])
        for k, (a, b) in enumerate(
            (
                (x_s, x_h), (c_s, c_h), (hid, hid_h), (gpre, gpre_h),
                (ki, ki_h), (si, si_h), (ko, ko_h), (so, so_h), (send, send_h),
            )
        )
    ]
    for load in loads:
        load.start()

    @pl.loop(0, 8)
    def _(step):
        for i in [4 * step + u for u in range(4)]:
            rows = pl.ds(pl.multiple_of(i * 16, 16), 16)
            xs = [recv[4 * i + h, :, 0:W].astype(F32) for h in range(4)]
            cs = [recv[4 * i + h, :, W : 2 * W].astype(F32) for h in range(4)]
            x_s[rows, :] = jnp.concatenate(xs, axis=0).astype(BF)
            c_s[rows, :] = jnp.concatenate(cs, axis=0).astype(BF)

    stores[0].start()
    stores[1].start()
    loads[0].wait()
    loads[1].wait()

    for i in range(4):
        cols = slice(i * 256, i * 256 + 256)
        pre = mm(x_s[...], wi[:, cols]) + b_ref[:, cols]
        gh = mm_t(c_s[...], wo[cols, :])
        act(pre, gh, cols, hid, gpre)

    stores[2].start()
    stores[3].start()
    for load in loads[2:]:
        load.wait()

    for i in range(4):
        cols = slice(i * 256, i * 256 + 256)
        pre = mm(x_s[:, mine], wiy[:, cols]) + mm(x_s[:, other], win[:, cols]) + bp_ref[:, cols]
        gh = mm_t(c_s[:, mine], woy[cols, :]) + mm_t(c_s[:, other], won[cols, :])
        act(pre, gh, cols, hid_p, gpre_p)

    grad_part(n, x_s, c_s, hid_p, gpre_p, ki, si, ko, so)
    for store in stores[4:8]:
        store.start()

    for yr, kr, part in ((woy, wiy, mine), (won, win, other)):
        o_s[:, part] = mm(hid[...], wo[:, part]) + mm(hid_p[...], yr[...])
        k_s[:, part] = mm_t(gpre[...], wi[part, :]) + mm_t(gpre_p[...], kr[...])

    @pl.loop(0, 16)
    def _(step):
      for i in [4 * step + u for u in range(4)]:
        rows = pl.ds(pl.multiple_of(i * 8, 8), 8)
        o, k = o_s[rows, :], k_s[rows, :]
        send[2 * i, :, :] = jnp.where(low, o, pltpu.roll(k, 4, 0)).astype(BF)
        send[2 * i + 1, :, :] = jnp.where(low, pltpu.roll(o, 4, 0), k).astype(BF)

    stores[8].start()
    for store in stores:
        store.wait()


def grad_part(n, x_s, c_s, hid, gpre, keep_i, send_i, keep_o, send_o):
    mine = pl.ds(pl.multiple_of(n * 256, 256), 256)
    other = pl.ds(pl.multiple_of(256 - n * 256, 256), 256)

    @pl.loop(0, 2)
    def _(i):
        cols = pl.ds(pl.multiple_of(i * 512, 512), 512)
        g = gpre[:, cols]
        keep_i[0:256, cols] = t_mm(x_s[:, mine], g) * SHARE
        send_i[0:256, cols] = (t_mm(x_s[:, other], g) * SHARE).astype(BF)
        bias = jnp.sum(g.astype(F32), axis=0, keepdims=True) * SHARE
        keep_i[256:272, cols] = jnp.broadcast_to(bias, (16, 512))
        send_i[256:272, cols] = jnp.broadcast_to(bias, (16, 512)).astype(BF)
        h = hid[:, cols]
        keep_o[cols, :] = t_mm(h, c_s[:, mine]) * SHARE
        send_o[cols, :] = (t_mm(h, c_s[:, other]) * SHARE).astype(BF)


def weight_kernel(pos, x_s, c_s, hid, gpre, keep_i, send_i, keep_o, send_o):
    grad_part(pos[3], x_s, c_s, hid, gpre, keep_i, send_i, keep_o, send_o)


def merge_kernel(keep, got, away):
    away[...] = (keep[...] + got[...].astype(F32)).astype(BF)


def end_kernel(pos, keep_i, got_i, far_i, keep_o, got_o, far_o, grad_i, bias, grad_o, row):
    def total(a, b, c, rows):
        return a[rows, :] + b[rows, :].astype(F32) + c[rows, :].astype(F32)

    grad_i[...] = total(keep_i, got_i, far_i, slice(0, 256))
    row[...] = total(keep_i, got_i, far_i, slice(256, 272))[0:8, :]
    bias[...] = row[0:1, pl.ds(pl.multiple_of(pos[3] * 512, 512), 512)]
    grad_o[...] = total(keep_o, got_o, far_o, slice(0, HALF))


def attn_kernel(pos, rs, rs2, qkv_ref, g_ref, x_ref, c_ref, mix_ref, gq, keep, send, query, ss):
    low = low_rows((8, 128))

    @pl.loop(0, 32)
    def _(i):
        tiles = []
        for h in range(2):
            pair = []
            for k in range(2):
                d = 4 * i + 2 * h + k
                v = rs[d, :, 0:128].astype(F32) + rs2[d].astype(F32)
                pair.append(v + pltpu.roll(v, 4, 0))
            tiles.append(jnp.where(low, pair[0], pair[1]))
        ss[pl.ds(pl.multiple_of(i * 16, 16), 16), :] = jnp.concatenate(tiles, axis=0).astype(BF)

    ones = head_ones()
    qkv, g = qkv_ref[...], g_ref[...]
    ku, ks = normalize(qkv[:, W : 2 * W], ones)
    vu, vs = normalize(qkv[:, 2 * W :], ones)
    kn, vn = ku.astype(BF), vu.astype(BF)
    left = lax.broadcasted_iota(jnp.int32, (64, 128), 1) < 64
    total = jnp.sum(rs[:, :, 128:256].astype(F32), axis=0)
    total_hi = total.astype(BF)
    total_lo = (total - total_hi.astype(F32)).astype(BF)
    block = lax.broadcasted_iota(jnp.int32, (8, 128), 0) % 4

    def diag(p):
        z = jnp.zeros_like(p)
        return jnp.concatenate([jnp.where(left, p, z), jnp.where(left, z, p)], axis=0)

    gk, gv = [], []
    rows = jnp.zeros((8, 128), F32)
    for j in range(4):
        s = slice(128 * j, 128 * j + 128)
        sm = diag(ss[64 * j : 64 * j + 64, :].astype(F32)).astype(BF)
        gs = diag(ss[256 + 64 * j : 320 + 64 * j, :].astype(F32)).astype(BF)
        mix_ref[:, s] = mm(qkv[:, s], sm).astype(BF)
        gq[:, s] = mm_t(g[:, s], sm).astype(BF)
        rows = jnp.where(block == j, mm_t(total_hi, sm) + mm_t(total_lo, sm), rows)
        gk.append(mm_t(vn[:, s], gs))
        gv.append(mm(kn[:, s], gs))
    query[...] = rows

    def back(gr, u, sc):
        return ((gr - head_mean(gr, ones) - u * head_mean(gr * u, ones)) / sc).astype(BF)

    gq[:, W : 2 * W] = back(jnp.concatenate(gk, axis=1), ku, ks)
    gq[:, 2 * W :] = back(jnp.concatenate(gv, axis=1), vu, vs)
    x, c, mixed = x_ref[...], c_ref[...], mix_ref[...]
    for core, dst in ((pos[3], keep), (1 - pos[3], send)):
        sel = pick(core)
        xk, mk = mm(x, sel).astype(BF), mm(mixed, sel).astype(BF)
        for q in range(2):
            dst[:, W * q : W * q + W] = (t_mm(xk, gq[:, W * q + W : W * q + 2 * W]) * (1.0 / TOTAL)).astype(dst.dtype)
        dst[:, 2 * W :] = (t_mm(mk, c) * (1.0 / TOTAL)).astype(dst.dtype)


def base_kernel(x, c, mixed, gq, wq, wo, base_o, base_k):
    base_o[...] = x[...].astype(F32) + mm(mixed[...], wo[...])
    base_k[...] = c[...].astype(F32) + mm_t(gq[...], wq[...])


def join_kernel(ret, keep, near, out, rows):
    out[:, :, 0:W] = ret[...]
    size = 8 * CHIPS
    for t in range(3):
        for j in range(2):
            part = slice(CHIPS * j, CHIPS * j + CHIPS)
            for q in range(4):
                cols = slice(384 * q + 128 * t, 384 * q + 128 * t + 128)
                v = keep[part, cols] + near[part, cols].astype(F32)
                rows[pl.ds(size * t + 4 * j + q, CHIPS, stride=8), :] = v
        v = rows[size * t : size * t + size, :].reshape(CHIPS, 8, 128)
        out[:, :, W + 128 * t : W + 128 * t + 128] = v.astype(BF)


def final_kernel(slots, ret, base_o, base_k, query, lo, gf, att):
    low = low_rows((8, W))

    @pl.loop(0, 16)
    def _(i):
        os, ks = [], []
        for h in range(2):
            a = ret[slots[4 * i + 2 * h], :, 0:W].astype(F32)
            b = ret[slots[4 * i + 2 * h + 1], :, 0:W].astype(F32)
            os.append(jnp.where(low, a, pltpu.roll(b, 4, 0)))
            ks.append(jnp.where(low, pltpu.roll(a, 4, 0), b))
        rows = pl.ds(pl.multiple_of(i * 16, 16), 16)
        lo[rows, :] = (base_o[rows, :] + jnp.concatenate(os, axis=0)).astype(BF)
        gf[rows, :] = (base_k[rows, :] + jnp.concatenate(ks, axis=0)).astype(BF)

    v = jnp.sum(ret[:, :, W:].astype(F32), axis=0)
    q = query[...]
    for j in range(2):
        for b in range(4):
            r = slice(4 * j + b, 4 * j + b + 1)
            att[j : j + 1, 128 * b : 128 * b + 128] = q[r]
            att[j : j + 1, W + 384 * b : W + 384 * b + 384] = v[r]


def layer(x, ids, wq, wo_att, wi, bi, wo, c):
    n = lax.axis_index("narrow")
    w = lax.axis_index("wide")
    pos = jnp.stack([w // 16, w // 4 % 4, w % 4, n]).astype(jnp.int32)
    pair = [(i, i ^ 1) for i in range(CHIPS)]
    swap = [(0, 1), (1, 0)]

    def across(v):
        return lax.ppermute(v, "wide", pair)

    def beside(v):
        return lax.ppermute(v, "narrow", swap)

    def deal(v):
        return lax.all_to_all(v, "wide", split_axis=0, concat_axis=0, tiled=True)

    def run(body, us, outs, args, scratch=(), smem_in=(), smem_out=(), specs=None, mib=24, out_hbm=False):
        return call(
            body, outs, scratch, smem_in=smem_in, n_in=len(args), smem_out=smem_out, cost=cost(us),
            specs=specs, mib=mib, out_hbm=out_hbm,
        )(*args)

    anywhere = pl.BlockSpec(memory_space=pltpu.HBM)

    def half(v, axis):
        shape = (256, HALF) if axis == 0 else (HALF, 256)
        (out,) = run(
            lambda *refs: slice_kernel(axis, *refs), 1, [sds(shape, BF)], (in_hbm(v),),
            [pltpu.SemaphoreType.DMA], specs={0: anywhere},
        )
        return out

    wiy = across(half(wi, 0))
    woy = across(half(wo, 1))
    bp = across(bi)
    win, won = beside(wiy), beside(woy)

    send, slots, qkv, g = run(
        front_kernel, 5,
        [far((CHIPS, 4, 1152), BF), sds((NB,), jnp.int32), far((PTS, 3 * W), BF), far((PTS, W), BF)],
        (in_hbm(ids), in_hbm(x), in_hbm(c), in_hbm(wq), in_hbm(wo_att)),
        [
            pltpu.SMEM((NB,), jnp.int32), pltpu.VMEM((W, 128), F32), pltpu.VMEM((W, 3 * W), BF),
            pltpu.VMEM((W, W), BF), pltpu.SemaphoreType.DMA((2,)),
        ],
        (0,), (1,), specs={3: anywhere, 4: anywhere}, mib=48,
    )
    recv = deal(send)
    keep_q, away_q = run(query_kernel, 2, [sds((PTS, W), F32), sds((PTS, W), BF)], (pos, x, g), (), (0,))
    (dealt_q,) = run(
        deal_query_kernel, 1, [sds((CHIPS, 8, 128), BF)], (keep_q, beside(away_q)),
        [pltpu.VMEM((8 * CHIPS, 128), F32)],
    )
    (spread,) = run(
        spread_kernel, 1, [far((CHIPS, 8, 256), BF)], (recv, dealt_q),
        specs={0: pl.BlockSpec((CHIPS, 4, 128), lambda i: (0, 0, 8))},
    )
    rs = deal(spread)
    grads = [((272, HALF), F32), ((272, HALF), BF), ((HALF, 256), F32), ((HALF, 256), BF)]
    ret, x_s, c_s, hid, gpre, keep_i, send_i, keep_o, send_o = run(
        expert_kernel, 12,
        [far((CHIPS, 8, W), BF), far((W, W), BF), far((W, W), BF), far((W, HALF), BF), far((W, HALF), BF)]
        + [far(*v) for v in grads],
        (pos, recv, *map(in_hbm, (wi, wiy, win, wo, woy, won)), bi.reshape(1, HALF), bp.reshape(1, HALF)),
        [pltpu.VMEM((W, W), BF)] * 2 + [pltpu.VMEM((W, HALF), BF)] * 4 + [pltpu.VMEM((W, W), F32)] * 2
        + [pltpu.VMEM((CHIPS, 8, W), BF)] + [pltpu.VMEM(*v) for v in grads]
        + [
            pltpu.VMEM(v, BF)
            for v in ((W, HALF), (256, HALF), (256, HALF), (HALF, W), (HALF, 256), (HALF, 256))
        ]
        + [pltpu.SemaphoreType.DMA((6,)), pltpu.SemaphoreType.DMA((9,))],
        (0,),
        specs={1: pl.BlockSpec((CHIPS, 4, 2 * W), lambda i: (0, 0, 0)), **{k: anywhere for k in range(2, 8)}},
        out_hbm=True, mib=48,
    )
    got_i, got_o = beside(send_i), beside(send_o)
    rs2 = beside(rs)
    mixed, gq, keep, away, query = run(
        attn_kernel, 7,
        [sds((PTS, W), BF), sds((PTS, 3 * W), BF), sds((PTS, 3 * W), F32), sds((PTS, 3 * W), BF), sds((8, 128), F32)],
        (pos, rs, rs2, qkv, g, x, c), [pltpu.VMEM((W, 128), BF)], (0,),
        specs={2: pl.BlockSpec((CHIPS, 8, 128), lambda i: (0, 0, 0))},
    )
    near = beside(away)
    base_o, base_k = run(base_kernel, 1, [far((PTS, W), F32), far((PTS, W), F32)], (x, c, mixed, gq, wq, wo_att))
    (away_i,) = run(merge_kernel, 1, [sds((272, HALF), BF)], (in_hbm(keep_i), got_i))
    (away_o,) = run(merge_kernel, 1, [sds((HALF, 256), BF)], (in_hbm(keep_o), got_o))
    far_i, far_o = across(away_i), across(away_o)
    (joined,) = run(join_kernel, 2, [far((CHIPS, 8, 896), BF)], (ret, keep, near), [pltpu.VMEM((24 * CHIPS, 128), F32)])
    back = deal(joined)
    keep_i, send_i, keep_o, send_o = run(
        weight_kernel, 5, [sds(*v) for v in grads], (pos, x_s, c_s, hid, gpre), (), (0,)
    )
    got_i, got_o = beside(send_i), beside(send_o)
    grad_in, grad_b, grad_out = run(
        end_kernel, 3, [sds((256, HALF), F32), sds((1, 512), F32), sds((HALF, 256), F32)],
        (pos, keep_i, got_i, far_i, keep_o, got_o, far_o), [pltpu.VMEM((8, HALF), F32)], (0,),
    )
    layer_out, grad_feats, att = run(
        final_kernel, 3, [sds((PTS, W), BF), sds((PTS, W), BF), sds((2, 4 * W), F32)],
        (slots, back, in_hbm(base_o), in_hbm(base_k), query), (), (0,),
    )
    return (layer_out, grad_feats, att, grad_in, grad_out, grad_b.reshape(512))


def solution(mesh):
    placed = (
        P(("wide", "narrow"), None),
        P(("wide", "narrow")),
        P(),
        P(),
        P(None, "wide"),
        P("wide"),
        P("wide", None),
        P(("wide", "narrow"), None),
    )
    return jax.shard_map(
        layer,
        mesh=mesh,
        in_specs=placed,
        out_specs=(
            P(("wide", "narrow"), None),
            P(("wide", "narrow"), None),
            P(("wide", "narrow"), None),
            P("narrow", "wide"),
            P("wide", "narrow"),
            P(("wide", "narrow")),
        ),
        check_vma=False,
    )
```
